32 devices in a mesh: dp: 8 (over y, x, core), tensor: 4 (over z).
Axes of the slice: x: 2, y: 2, z: 4, core: 2. Of those that a mesh axis runs over, the one named last changes fastest.
Arguments:
- images: bfloat16 [64, 257, 1664], P(('dp', 'tensor')), may hold values from -6 to 6
- first_gain: float32 [1664], replicated, may hold values from 0.5 to 1.5
- first_shift: float32 [1664], replicated, may hold values from -4 to 4
- qkv_weight: bfloat16 [3, 1664, 1664], P(None, None, 'tensor'), as said below
- qv_bias: float32 [2, 1664], P(None, 'tensor'), may hold values from -6 to 6
- out_weight: bfloat16 [1664, 1664], P('tensor'), may hold values from -0.625 to 0.625
- out_bias: float32 [1664], replicated, may hold values from -4 to 4
- second_gain: float32 [1664], replicated, may hold values from 0.5 to 1.5
- second_shift: float32 [1664], replicated, may hold values from -4 to 4
- up_weight: bfloat16 [1664, 8192], P(None, 'tensor'), may hold values from -0.15625 to 0.15625
- up_bias: float32 [8192], P('tensor'), may hold values from -6 to 6
- down_weight: bfloat16 [8192, 1664], P('tensor'), may hold values from -0.0625 to 0.0625
- down_bias: float32 [1664], replicated, may hold values from -4 to 4
- cotangent: bfloat16 [64, 257, 1664], P(('dp', 'tensor')), may hold values from -6 to 6
Outputs:
- result: bfloat16 [64, 257, 1664], P(('dp', 'tensor'))
- grad_images: bfloat16 [64, 257, 1664], P(('dp', 'tensor'))
- grad_first_gain: float32 [1664], replicated
- grad_first_shift: float32 [1664], replicated
- grad_qkv_weight: float32 [3, 1664, 1664], P(None, None, 'tensor')
- grad_qv_bias: float32 [2, 1664], P(None, 'tensor')
- grad_out_weight: float32 [1664, 1664], P('tensor')
- grad_out_bias: float32 [1664], replicated
- grad_second_gain: float32 [1664], replicated
- grad_second_shift: float32 [1664], replicated
- grad_up_weight: float32 [1664, 8192], P(None, 'tensor')
- grad_up_bias: float32 [8192], P('tensor')
- grad_down_weight: float32 [8192, 1664], P('tensor')
- grad_down_bias: float32 [1664], replicated
The draws below stay inside these ranges and needn't reach their ends.
Inputs may be any that keep to these rules, and one draw needn't show every extreme that they name: `qkv_weight`: the three parts are query, keys and values, in this order.
All inputs are finite; a program needn't handle non-finite values.
Results may differ from the reference program's by a relative error of at most 0.02.
Values may be sent and summed in bfloat16 or wider, within the bound.
A program may use at most 256 MiB of HBM per device.

```python
import math
import jax
import jax.numpy as jnp
from jax import lax

D = 1664
HEADS = 16
HD = 104
FF = 8192
SEQ = 257
IMAGES = 64


def draw_qkv_weight(key, part):
    first = jax.random.fold_in(key, 0)
    base = jax.random.normal(first, (3, D, D), jnp.float32) * D ** (-0.5)
    return base.astype(jnp.bfloat16)


def steps_of(key, extent, pieces, low, top_value):
    def one(axis_at, shards_of):
        heights = jax.random.uniform(jax.random.fold_in(jax.random.fold_in(key, 6), axis_at), (shards_of,), jnp.float32, low / len(pieces), top_value / len(pieces))
        return jnp.repeat(jnp.exp(heights), extent[axis_at] // shards_of).reshape((-1,) + (1,) * (len(extent) - axis_at - 1))

    loudness = one(*pieces[0])
    for cut in pieces[1:]:
        loudness = loudness * one(*cut)
    return loudness


def scatter_about(stream_key, extent, scale, reach, cuts=(), dtype=jnp.bfloat16):
    drawn = jax.random.normal(stream_key, extent, jnp.float32) * scale
    if len(cuts) > 0:
        drawn = steps_of(stream_key, extent, cuts, -0.22, 0.18) * drawn
    return jnp.clip(drawn, min=-reach, max=reach).astype(dtype)


def setup_inputs(seed: int = 0) -> dict:
    key_list = jax.random.split(jax.random.key(seed), 15)
    return {
        "images": scatter_about(key_list[0], (IMAGES, SEQ, D), 1.0, 6.0, ((0, 32),)),
        "first_gain": jnp.clip(1.0 + 0.1 * jax.random.normal(key_list[1], (D,), jnp.float32), 0.5, 1.5),
        "first_shift": scatter_about(key_list[2], (D,), 0.3, 4.0, (), jnp.float32),
        "qkv_weight": draw_qkv_weight(jax.random.fold_in(key_list[14], 71), 0),
        "qv_bias": scatter_about(key_list[4], (2, D), 0.5, 6.0, ((1, 4),), jnp.float32),
        "out_weight": scatter_about(key_list[5], (D, D), (D // 16) ** -0.5, 0.625, ((0, 4),)),
        "out_bias": scatter_about(key_list[6], (D,), 0.3, 4.0, (), jnp.float32),
        "second_gain": jnp.clip(1.0 + 0.1 * jax.random.normal(key_list[7], (D,), jnp.float32), 0.5, 1.5),
        "second_shift": scatter_about(key_list[8], (D,), 0.3, 4.0, (), jnp.float32),
        "up_weight": scatter_about(key_list[9], (D, FF), D ** -0.5, 0.15625, ((1, 4),)),
        "up_bias": scatter_about(key_list[10], (FF,), 0.5, 6.0, ((0, 4),), jnp.float32),
        "down_weight": scatter_about(key_list[11], (FF, D), FF ** -0.5, 0.0625, ((0, 4),)),
        "down_bias": scatter_about(key_list[12], (D,), 0.3, 4.0, (), jnp.float32),
        "cotangent": scatter_about(key_list[13], (IMAGES, SEQ, D), 1.0, 6.0, ((0, 32),)),
    }


@jax.custom_vjp
def low(v):
    return lax.optimization_barrier(v.astype(jnp.bfloat16)).astype(jnp.float32)

@jax.custom_vjp
def low_back(v):
    return v

def low_keep(v):
    return (low(v), None)

def low_pass(kept, grad):
    return (grad,)

def back_keep(v):
    return (v, None)

def back_low(kept, grad):
    return (low(grad),)
low.defvjp(low_keep, low_pass)
low_back.defvjp(back_keep, back_low)
epsilon = 1e-06

def product(form, left, right):
    return jnp.einsum(form, left, right, precision=lax.Precision.HIGHEST)

def layer_norm(rows, gain, shift):
    centre = lax.optimization_barrier(jnp.mean(rows, axis=-1, keepdims=True))
    centred = rows - centre
    spread = lax.optimization_barrier(jnp.mean(centred * centred, axis=-1, keepdims=True))
    return centred * lax.rsqrt(spread + epsilon) * gain + shift

def attend(query, keys, values):
    scores = low_back(product('shd,thd->hst', query, keys) * query.shape[-1] ** (-0.5))
    weights = low(jax.nn.softmax(scores, axis=-1))
    return product('hst,thd->shd', weights, values)

def forward(images, first_gain, first_shift, qkv_weight, qv_bias, out_weight, out_bias, second_gain, second_shift, up_weight, up_bias, down_weight, down_bias):
    count = images.shape[0]
    normed_first = low(layer_norm(images, first_gain, first_shift))
    query = low(low_back(product('isd,de->ise', normed_first, qkv_weight[0]) + qv_bias[0]))
    keys = low(low_back(product('isd,de->ise', normed_first, qkv_weight[1])))
    values = low(low_back(product('isd,de->ise', normed_first, qkv_weight[2]) + qv_bias[1]))
    shaped = (count, SEQ, HEADS, HD)
    checked = jax.checkpoint(attend)
    mixed = lax.map(lambda triple: checked(triple[0], triple[1], triple[2]), (query.reshape(shaped), keys.reshape(shaped), values.reshape(shaped)))
    heads_out = low(low_back(mixed.reshape(count, SEQ, D)))
    branch = low_back(product('isc,cd->isd', heads_out, out_weight) + out_bias)
    middle = images + branch
    normed_second = low(layer_norm(middle, second_gain, second_shift))
    hidden = low_back(product('isd,df->isf', normed_second, up_weight) + up_bias)
    active = low(jax.nn.gelu(hidden, approximate=False))
    return middle + product('isf,fd->isd', active, down_weight) + down_bias

def reference(images, first_gain, first_shift, qkv_weight, qv_bias, out_weight, out_bias, second_gain, second_shift, up_weight, up_bias, down_weight, down_bias, cotangent):
    params = tuple((p.astype(jnp.float32) for p in (first_gain, first_shift, qkv_weight, qv_bias, out_weight, out_bias, second_gain, second_shift, up_weight, up_bias, down_weight, down_bias)))
    group = math.gcd(IMAGES, 16)
    blocks = IMAGES // group
    inputs = images.astype(jnp.float32).reshape(blocks, group, SEQ, D)
    seeds = cotangent.astype(jnp.float32).reshape(blocks, group, SEQ, D)

    def step(totals, item):
        block_in, block_seed = item
        output, pull = jax.vjp(forward, block_in, *params)
        grads = pull(block_seed)
        totals = tuple((total + grad for total, grad in zip(totals, grads[1:])))
        return (totals, (output.astype(jnp.bfloat16), grads[0].astype(jnp.bfloat16)))
    zeros = tuple((jnp.zeros_like(p) for p in params))
    totals, (outputs, grad_in) = lax.scan(step, zeros, (inputs, seeds))
    return (outputs.reshape(IMAGES, SEQ, D), grad_in.reshape(IMAGES, SEQ, D), totals[0], totals[1], totals[2], totals[3], totals[4], totals[5], totals[6], totals[7], totals[8], totals[9], totals[10], totals[11])
```

```python
import jax
import jax.numpy as jnp
import numpy as np
from jax import lax
from jax.sharding import PartitionSpec as P

HD = 104

epsilon = 1e-06
inv_root_two = 0.7071067811865476
inv_root_tau = 0.3989422804014327
BF = jnp.bfloat16
F32 = jnp.float32


def normalize(rows):
    centre = jnp.mean(rows, axis=-1, keepdims=True)
    centred = rows - centre
    spread = jnp.mean(centred * centred, axis=-1, keepdims=True)
    inverse = lax.rsqrt(spread + epsilon)
    return (centred * inverse, inverse)


def norm_back(grad, unit, inverse, gain):
    scaled = grad * gain
    first = jnp.mean(scaled, axis=-1, keepdims=True)
    second = jnp.mean(scaled * unit, axis=-1, keepdims=True)
    return inverse * (scaled - first - unit * second)


def attend_block(query, keys, values):
    factor = query.shape[-1] ** (-0.5)
    scores = jnp.einsum("bshd,bthd->bhst", query, keys, preferred_element_type=F32) * factor
    top = jnp.max(scores, axis=-1, keepdims=True)
    raised = jnp.exp(scores - top)
    total = jnp.sum(raised, axis=-1, keepdims=True)
    weights = (raised / total).astype(BF)
    mixed = jnp.einsum("bhst,bthd->bshd", weights, values, preferred_element_type=F32)
    return (mixed, (top + jnp.log(total))[..., 0])


def attend_back(query, keys, values, grad_out, log_total):
    factor = query.shape[-1] ** (-0.5)
    scores = jnp.einsum("bshd,bthd->bhst", query, keys, preferred_element_type=F32) * factor
    probs = jnp.exp(scores - log_total[..., None])
    grad_values = jnp.einsum(
        "bhst,bshd->bthd", probs.astype(BF), grad_out, preferred_element_type=F32
    )
    grad_probs = jnp.einsum("bshd,bthd->bhst", grad_out, values, preferred_element_type=F32)
    inner = jnp.sum(probs * grad_probs, axis=-1, keepdims=True)
    grad_scores = (probs * (grad_probs - inner)).astype(BF)
    grad_query = (
        jnp.einsum("bhst,bthd->bshd", grad_scores, keys, preferred_element_type=F32) * factor
    )
    grad_keys = (
        jnp.einsum("bhst,bshd->bthd", grad_scores, query, preferred_element_type=F32) * factor
    )
    return (grad_query.astype(BF), grad_keys.astype(BF), grad_values.astype(BF))


class Layout:
    def __init__(self, dp, tensor):
        self.dp, self.tensor = dp, tensor
        self.n_p, self.n_hi = dp // 2, tensor // 2
        self.bits = [1 << b for b in range(self.n_p.bit_length() - 1)]

    def move(self, x, p=0, c=0, hi=0, lo=0):
        dp_mask, tensor_mask = 2 * p + c, 2 * hi + lo
        pairs = [
            (d * self.tensor + t, (d ^ dp_mask) * self.tensor + (t ^ tensor_mask))
            for d in range(self.dp)
            for t in range(self.tensor)
        ]
        return lax.ppermute(x, ("dp", "tensor"), pairs)

    def spread(self, block, order):
        have = {0: block}
        for bit in order:
            masks = sorted(have)
            got = self.move(jnp.stack([have[m] for m in masks]), p=bit)
            for i, m in enumerate(masks):
                have[m ^ bit] = got[i]
        return [have[m] for m in range(self.n_p)]

    def collect(self, blocks, order):
        have = dict(enumerate(blocks))
        for bit in order:
            keep = [m for m in sorted(have) if not m & bit]
            got = self.move(jnp.stack([have[m | bit] for m in keep]), p=bit)
            have = {
                m: (have[m].astype(F32) + got[i].astype(F32)).astype(BF)
                for i, m in enumerate(keep)
            }
        return have[0]


def on_device(
    lay,
    images,
    first_gain,
    first_shift,
    qkv_weight,
    qv_bias,
    out_weight,
    out_bias,
    second_gain,
    second_shift,
    up_weight,
    up_bias,
    down_weight,
    down_bias,
    cotangent,
):
    n_p, n_hi = lay.n_p, lay.n_hi
    seq_len = images.shape[1]
    width = images.shape[2]
    columns = qkv_weight.shape[2]
    units = up_weight.shape[1]
    hc, hu = columns // 2, units // 2
    dp = lax.axis_index("dp")
    p, c = dp // 2, dp % 2
    d_block, u_block = width // n_p, hu // n_p
    up_order, down_order = lay.bits, lay.bits[::-1]

    def half(x, axis):
        n = x.shape[axis] // 2
        return lax.dynamic_slice_in_dim(x, c * n, n, axis)

    def relative(x, axis):
        n = x.shape[axis] // n_p
        return [lax.dynamic_slice_in_dim(x, (p ^ m) * n, n, axis) for m in range(n_p)]

    def absolute(blocks, axis):
        stacked = jnp.stack(blocks)
        return jnp.concatenate(
            [lax.dynamic_index_in_dim(stacked, p ^ a, 0, keepdims=False) for a in range(n_p)], axis
        )

    def fetch(x, axis, order):
        mine = relative(x, axis)
        return [mine] + [
            lay.spread(lay.move(mine[0], hi=k), order) for k in range(1, n_hi)
        ]

    qkv_half = half(qkv_weight, 2)
    out_half = half(out_weight, 0)
    qkv_parts = fetch(qkv_half, 1, up_order)
    out_parts = fetch(out_half, 1, down_order)
    qkv_work = jnp.concatenate(
        [qkv_half] + [absolute(b, 1) for b in qkv_parts[1:]], 2
    )
    out_work = jnp.concatenate([out_half] + [absolute(b, 1) for b in out_parts[1:]], 0)
    up_parts = fetch(half(up_weight, 1), 1, up_order)
    down_parts = fetch(half(down_weight, 0), 0, down_order)
    up_work = jnp.concatenate([b for part in up_parts for b in part], 1)
    down_work = jnp.concatenate([b for part in down_parts for b in part], 0)
    qv_half, upb_half = half(qv_bias, 1), half(up_bias, 0)
    bias_all = [jnp.concatenate([qv_half.reshape(-1), upb_half])]
    bias_all += [lay.move(bias_all[0], hi=k) for k in range(1, n_hi)]
    qv_work = jnp.concatenate([b[: 2 * hc].reshape(2, hc) for b in bias_all], 1)
    upb_work = jnp.concatenate([s for b in bias_all for s in relative(b[2 * hc :], 0)])

    def gather(x):
        x_c = lay.move(x, c=1)
        x_z = lay.move(x, lo=1)
        x_zc = lay.move(x_z, c=1)
        return jnp.concatenate([x, x_c, x_z, x_zc])

    def scatter(partial):
        n = partial.shape[0] // 4
        own, other, far, far_other = [partial[i * n : (i + 1) * n] for i in range(4)]
        got_far = lay.move(far_other, c=1)
        far_sum = (far.astype(F32) + got_far.astype(F32)).astype(BF)
        got_z = lay.move(far_sum, lo=1)
        got = lay.move(other, c=1)
        return own.astype(F32) + got.astype(F32) + got_z.astype(F32)

    inputs = images.astype(F32)
    unit_first, inverse_first = normalize(inputs)
    normed_first = gather((unit_first * first_gain + first_shift).astype(BF))
    seed_rows = gather(cotangent)
    count = normed_first.shape[0]
    work_columns = qkv_work.shape[2]
    heads_here = work_columns // HD
    projected = jnp.einsum("isd,nde->nise", normed_first, qkv_work, preferred_element_type=F32)
    query = (projected[0] + qv_work[0]).astype(BF)
    keys = projected[1].astype(BF)
    values = (projected[2] + qv_work[1]).astype(BF)
    split = (count // 2, 2, seq_len, heads_here, HD)
    query_blocks = query.reshape(split)
    key_blocks = keys.reshape(split)
    value_blocks = values.reshape(split)
    mixed, log_total = lax.map(
        lambda triple: attend_block(*triple), (query_blocks, key_blocks, value_blocks)
    )
    heads_out = mixed.reshape(count, seq_len, work_columns).astype(BF)
    attention = scatter(
        jnp.einsum("isc,cd->isd", heads_out, out_work, preferred_element_type=F32).astype(BF)
    )
    middle = inputs + (attention + out_bias)
    unit_second, inverse_second = normalize(middle)
    normed_second = gather((unit_second * second_gain + second_shift).astype(BF))
    hidden = (
        jnp.einsum("isd,df->isf", normed_second, up_work, preferred_element_type=F32) + upb_work
    )
    active = jax.nn.gelu(hidden, approximate=False).astype(BF)
    result = (
        middle
        + scatter(
            jnp.einsum("isf,fd->isd", active, down_work, preferred_element_type=F32).astype(BF)
        )
        + down_bias
    ).astype(BF)
    grad_down_work = jnp.einsum("isf,isd->fd", active, seed_rows, preferred_element_type=F32)
    grad_down_bias = jnp.sum(cotangent, axis=(0, 1), dtype=F32)
    grad_active = jnp.einsum("isd,fd->isf", seed_rows, down_work, preferred_element_type=F32)
    normal_cdf = 0.5 * (1.0 + lax.erf(hidden * inv_root_two))
    density = jnp.exp(-0.5 * hidden * hidden) * inv_root_tau
    grad_hidden = (grad_active * (normal_cdf + hidden * density)).astype(BF)
    grad_up_work = jnp.einsum("isd,isf->df", normed_second, grad_hidden, preferred_element_type=F32)
    grad_up_bias = jnp.sum(grad_hidden, axis=(0, 1), dtype=F32)
    grad_normed_second = scatter(
        jnp.einsum("isf,df->isd", grad_hidden, up_work, preferred_element_type=F32).astype(BF)
    )
    grad_second_gain = jnp.sum(grad_normed_second * unit_second, axis=(0, 1))
    grad_second_shift = jnp.sum(grad_normed_second, axis=(0, 1))
    grad_middle = cotangent.astype(F32) + norm_back(
        grad_normed_second, unit_second, inverse_second, second_gain
    )
    grad_branch = grad_middle.astype(BF)
    grad_out_bias = jnp.sum(grad_branch, axis=(0, 1), dtype=F32)
    branch_rows = gather(grad_branch)
    grad_out_work = jnp.einsum("isc,isd->cd", heads_out, branch_rows, preferred_element_type=F32)
    grad_heads = jnp.einsum(
        "isd,cd->isc", branch_rows, out_work, preferred_element_type=F32
    ).astype(BF)
    grad_query, grad_keys, grad_values = lax.map(
        lambda parts: attend_back(*parts),
        (query_blocks, key_blocks, value_blocks, grad_heads.reshape(split), log_total),
    )
    grad_projected = jnp.stack(
        [g.reshape(count, seq_len, work_columns) for g in (grad_query, grad_keys, grad_values)]
    )
    grad_qkv_work = jnp.einsum(
        "isd,nisc->ndc", normed_first, grad_projected, preferred_element_type=F32
    )
    grad_qv_work = jnp.stack(
        [jnp.sum(grad_projected[i], axis=(0, 1), dtype=F32) for i in (0, 2)]
    )
    grad_normed_first = scatter(
        jnp.einsum("nisc,ndc->isd", grad_projected, qkv_work, preferred_element_type=F32).astype(BF)
    )
    grad_first_gain = jnp.sum(grad_normed_first * unit_first, axis=(0, 1))
    grad_first_shift = jnp.sum(grad_normed_first, axis=(0, 1))
    grad_images = (
        grad_middle + norm_back(grad_normed_first, unit_first, inverse_first, first_gain)
    ).astype(BF)

    def settle(parts, order):
        sums = lay.collect(
            [jnp.stack([part[m] for part in parts]) for m in range(n_p)], order
        )
        total = sums[0].astype(F32)
        for k in range(1, n_hi):
            total = total + lay.move(sums[k], hi=k).astype(F32)
        return lay.spread(total.astype(BF), order[::-1])

    def whole(blocks, axis):
        mine = absolute(blocks, axis)
        other = lay.move(mine, c=1)
        first = jnp.where(c == 0, mine, other)
        second = jnp.where(c == 0, other, mine)
        return first.astype(F32), second.astype(F32)

    def block_list(x, start, size, axis):
        return [
            lax.slice_in_dim(x, start + m * size, start + (m + 1) * size, axis=axis)
            for m in range(n_p)
        ]

    grad_down_low, grad_up_low = grad_down_work.astype(BF), grad_up_work.astype(BF)
    down_settled = settle(
        [block_list(grad_down_low, k * hu, u_block, 0) for k in range(n_hi)], down_order
    )
    up_settled = settle(
        [block_list(grad_up_low, k * hu, u_block, 1) for k in range(n_hi)], up_order
    )
    grad_out_low, grad_qkv_low = grad_out_work.astype(BF), grad_qkv_work.astype(BF)
    out_settled = settle(
        [relative(grad_out_low[k * hc : (k + 1) * hc], 1) for k in range(n_hi)], down_order
    )
    qkv_settled = settle(
        [relative(grad_qkv_low[:, :, k * hc : (k + 1) * hc], 1) for k in range(n_hi)], up_order
    )
    grad_down_weight = jnp.concatenate(whole(down_settled, 0), 0)
    grad_up_weight = jnp.concatenate(whole(up_settled, 1), 1)
    grad_out_weight = jnp.concatenate(whole(out_settled, 1), 0)
    grad_qkv_weight = jnp.concatenate(whole(qkv_settled, 1), 2)

    tensor_at = lax.axis_index("tensor")
    all_units, all_columns = units * lay.tensor, columns * lay.tensor
    wide_up = jnp.zeros((all_units,), F32)
    wide_qv = jnp.zeros((2, all_columns), F32)
    for k in range(n_hi):
        shard = tensor_at ^ (2 * k)
        blocks = [
            grad_up_bias[k * hu + m * u_block : k * hu + (m + 1) * u_block] for m in range(n_p)
        ]
        wide_up = lax.dynamic_update_slice(
            wide_up, absolute(blocks, 0), (shard * units + c * hu,)
        )
        wide_qv = lax.dynamic_update_slice(
            wide_qv, grad_qv_work[:, k * hc : (k + 1) * hc], (0, shard * columns + c * hc)
        )

    def total_of(vector):
        for bit in lay.bits:
            vector = vector + lay.move(vector, p=bit)
        vector = vector + lay.move(vector, c=1)
        for k in [1 << b for b in range(lay.tensor.bit_length() - 1)]:
            vector = vector + lay.move(vector, lo=k & 1, hi=k >> 1)
        return vector

    early = total_of(
        jnp.concatenate([grad_down_bias, wide_up, grad_second_gain, grad_second_shift, grad_out_bias])
    )
    late = total_of(jnp.concatenate([wide_qv.reshape(-1), grad_first_gain, grad_first_shift]))
    grad_down_bias, early = early[:width], early[width:]
    grad_up_bias = lax.dynamic_slice(early, (tensor_at * units,), (units,))
    early = early[all_units:].reshape(3, width)
    grad_qv_bias = lax.dynamic_slice(
        late[: 2 * all_columns].reshape(2, all_columns), (0, tensor_at * columns), (2, columns)
    )
    late = late[2 * all_columns :].reshape(2, width)
    return (
        result,
        grad_images,
        late[0],
        late[1],
        grad_qkv_weight,
        grad_qv_bias,
        grad_out_weight,
        early[2],
        early[0],
        early[1],
        grad_up_weight,
        grad_up_bias,
        grad_down_weight,
        grad_down_bias,
    )


def solution(mesh):
    lay = Layout(mesh.shape["dp"], mesh.shape["tensor"])

    def run(*args):
        return on_device(lay, *args)

    return jax.shard_map(
        run,
        mesh=mesh,
        in_specs=(
            P(("dp", "tensor"), None, None),
            P(),
            P(),
            P(None, None, "tensor"),
            P(None, "tensor"),
            P("tensor", None),
            P(),
            P(),
            P(),
            P(None, "tensor"),
            P("tensor"),
            P("tensor", None),
            P(),
            P(("dp", "tensor"), None, None),
        ),
        out_specs=(
            P(("dp", "tensor"), None, None),
            P(("dp", "tensor"), None, None),
            P(),
            P(),
            P(None, None, "tensor"),
            P(None, "tensor"),
            P("tensor", None),
            P(),
            P(),
            P(),
            P(None, "tensor"),
            P("tensor"),
            P("tensor", None),
            P(),
        ),
        check_vma=False,
    )
```

```python
import functools

import jax
import jax.numpy as jnp
from jax import lax
from jax.experimental import pallas as pl
from jax.experimental.pallas import tpu as pltpu
from jax.sharding import PartitionSpec as P

HD = 104
PAD = 16
BF = jnp.bfloat16
F32 = jnp.float32


def dot(a, b, ca, cb):
    return lax.dot_general(a, b, (((ca,), (cb,)), ((), ())), preferred_element_type=F32)


def whole_spec(shape):
    return pl.BlockSpec(shape, lambda *_: (0,) * len(shape), pipeline_mode=pl.Buffered(1))


def head_mask(heads):
    lane = lax.broadcasted_iota(jnp.int32, (8, heads * HD), 1)
    row = lax.broadcasted_iota(jnp.int32, (8, heads * HD), 0)
    return (lane >= row * HD) & (lane < row * HD + HD)


def attend_fwd_kernel(n_i, main, heads, n_add, n_ref, w_ref, b_ref, wo_ref, *refs):
    adds = refs[:n_add]
    qkv_ref, ho_ref, lse_ref, lset_ref, out_ref = refs[n_add:]
    hc = heads * HD
    tail = pl.ds(n_i * main, PAD)
    qkv_ref[...] = (dot(n_ref[...], w_ref[...], 1, 0) + b_ref[...]).astype(BF)
    ho_ref[tail, :] = jnp.zeros((PAD, hc), BF)
    factor = HD ** -0.5
    tail_row = lax.broadcasted_iota(jnp.int32, (PAD, 1), 0)
    per_head = head_mask(heads)

    def image(i, carry):
        rows = pl.ds(pl.multiple_of(i * main, main), main)
        here = tail_row == i
        bar = jnp.where(here, 0.0, -1e30)
        bar_all = jnp.concatenate([jnp.zeros((main, 1), F32), bar], 0)

        def both(cols):
            return jnp.concatenate([qkv_ref[rows, cols], qkv_ref[tail, cols]], 0)

        q_t = jnp.sum(jnp.where(here, qkv_ref[tail, 0:hc].astype(F32), 0.0), 0, keepdims=True)
        q_b = jnp.where(per_head, q_t, 0.0).astype(BF)
        s = dot(both(slice(hc, 2 * hc)), q_b, 1, 1) * factor + bar_all
        top = jnp.max(s, 0, keepdims=True)
        e = jnp.exp(s - top)
        total = jnp.sum(e, 0, keepdims=True)
        o = dot((e * (1.0 / total)).astype(BF), both(slice(2 * hc, 3 * hc)), 0, 0)
        o = jnp.sum(jnp.where(per_head, o, 0.0), 0, keepdims=True).astype(BF)
        ho_ref[tail, :] = jnp.where(here, o, ho_ref[tail, :])
        lset_ref[pl.ds(i, 1), 0:8] = top + jnp.log(total)
        for h in range(heads):
            cols = [slice(t * hc + h * HD, t * hc + (h + 1) * HD) for t in range(3)]
            q = qkv_ref[rows, cols[0]]
            s = dot(qkv_ref[rows, cols[1]], q, 1, 1) * factor
            s_t = dot(qkv_ref[tail, cols[1]], q, 1, 1) * factor + bar
            top = jnp.maximum(jnp.max(s, 0, keepdims=True), jnp.max(s_t, 0, keepdims=True))
            e, e_t = jnp.exp(s - top), jnp.exp(s_t - top)
            total = jnp.sum(e, 0, keepdims=True) + jnp.sum(e_t, 0, keepdims=True)
            inv = 1.0 / total
            o = dot((e * inv).astype(BF), qkv_ref[rows, cols[2]], 0, 0)
            o = o + dot((e_t * inv).astype(BF), qkv_ref[tail, cols[2]], 0, 0)
            ho_ref[rows, h * HD : (h + 1) * HD] = o.astype(BF)
            lse_ref[h : h + 1, rows] = top + jnp.log(total)
        return carry

    lax.fori_loop(0, n_i, image, 0)
    total = dot(ho_ref[...], wo_ref[0:hc, :], 1, 0)
    for ref in adds:
        total = total + ref[...].astype(F32)
    out_ref[...] = total.astype(BF)


def attend_fwd(n_i, n, w, b, wo, adds=()):
    rows, width = n.shape
    hc = w.shape[1] // 3
    main = (rows - PAD) // n_i
    shapes = (
        ((rows, 3 * hc), BF),
        ((rows, hc), BF),
        ((8, n_i * main), F32),
        ((8, 128), F32),
        ((rows, width), BF),
    )
    flops = 2 * rows * width * 4 * hc + 4 * n_i * main * main * hc
    return call(
        functools.partial(attend_fwd_kernel, n_i, main, hc // HD, len(adds)),
        [n, w, b, wo, *adds],
        shapes,
        flops=flops,
        name="attend_fwd",
    )


def attend_bwd_kernel(n_i, main, heads, n_half, n_add, g_ref, *refs):
    halves = [refs[5 * k : 5 * k + 5] for k in range(n_half)]
    adds = refs[5 * n_half : 5 * n_half + n_add]
    refs = refs[5 * n_half + n_add :]
    total = None
    for k, half in enumerate(halves):
        attend_bwd_half(n_i, main, heads, g_ref, *half, refs[2 * k], refs[2 * k + 1], *refs[-2:])
        part = dot(refs[2 * k][...], half[3][...], 1, 1)
        total = part if total is None else total + part
    for ref in adds:
        total = total + ref[...].astype(F32)
    refs[2 * n_half][...] = total.astype(BF)


def attend_bwd_half(
    n_i, main, heads, g_ref, qkv_ref, lse_ref, lset_ref, w_ref, wo_ref, d_ref, gb_ref, gh_ref, kv_ref
):
    hc = heads * HD
    tail = pl.ds(n_i * main, PAD)
    gh_ref[...] = dot(g_ref[...], wo_ref[0:hc, :], 1, 1).astype(BF)
    d_ref[tail, :] = jnp.zeros((PAD, 3 * hc), BF)
    factor = HD ** -0.5
    tail_row = lax.broadcasted_iota(jnp.int32, (PAD, 1), 0)
    per_head = head_mask(heads)

    def image(i, carry):
        rows = pl.ds(pl.multiple_of(i * main, main), main)
        here = tail_row == i
        bar = jnp.where(here, 0.0, -1e30)
        bar_all = jnp.concatenate([jnp.zeros((main, 1), F32), bar], 0)

        def both(cols):
            return jnp.concatenate([qkv_ref[rows, cols], qkv_ref[tail, cols]], 0)

        def last(ref, cols):
            row = jnp.sum(jnp.where(here, ref[tail, cols].astype(F32), 0.0), 0, keepdims=True)
            return jnp.where(per_head, row, 0.0).astype(BF)

        q_b, go_b = last(qkv_ref, slice(0, hc)), last(gh_ref, slice(0, hc))
        k_all, v_all = both(slice(hc, 2 * hc)), both(slice(2 * hc, 3 * hc))
        p = jnp.exp(dot(k_all, q_b, 1, 1) * factor + bar_all - lset_ref[pl.ds(i, 1), 0:8])
        dp = dot(v_all, go_b, 1, 1)
        ds = (p * (dp - jnp.sum(p * dp, 0, keepdims=True))).astype(BF)
        dq = dot(ds, k_all, 0, 0) * factor
        dq = jnp.sum(jnp.where(per_head, dq, 0.0), 0, keepdims=True).astype(BF)
        d_ref[tail, 0:hc] = jnp.where(here, dq, d_ref[tail, 0:hc])
        kv_ref[:, 0:hc] = dot(ds, q_b, 1, 0)
        kv_ref[:, hc : 2 * hc] = dot(p.astype(BF), go_b, 1, 0)
        for h in range(heads):
            head = slice(h * HD, (h + 1) * HD)
            cols = [slice(t * hc + h * HD, t * hc + (h + 1) * HD) for t in range(3)]
            q, go = qkv_ref[rows, cols[0]], gh_ref[rows, head]
            k, k_t = qkv_ref[rows, cols[1]], qkv_ref[tail, cols[1]]
            v, v_t = qkv_ref[rows, cols[2]], qkv_ref[tail, cols[2]]
            lse = lse_ref[h : h + 1, rows]
            p = jnp.exp(dot(k, q, 1, 1) * factor - lse)
            p_t = jnp.exp(dot(k_t, q, 1, 1) * factor + bar - lse)
            dp, dp_t = dot(v, go, 1, 1), dot(v_t, go, 1, 1)
            inner = jnp.sum(p * dp, 0, keepdims=True) + jnp.sum(p_t * dp_t, 0, keepdims=True)
            ds = (p * (dp - inner)).astype(BF)
            ds_t = (p_t * (dp_t - inner)).astype(BF)
            d_ref[rows, cols[0]] = ((dot(ds, k, 0, 0) + dot(ds_t, k_t, 0, 0)) * factor).astype(BF)
            dk = ((dot(ds, q, 1, 0) + kv_ref[0:main, head]) * factor).astype(BF)
            dk_t = ((dot(ds_t, q, 1, 0) + kv_ref[main:, head]) * factor).astype(BF)
            head_v = slice(hc + h * HD, hc + (h + 1) * HD)
            dv = (dot(p.astype(BF), go, 1, 0) + kv_ref[0:main, head_v]).astype(BF)
            dv_t = (dot(p_t.astype(BF), go, 1, 0) + kv_ref[main:, head_v]).astype(BF)
            d_ref[rows, cols[1]] = dk
            d_ref[rows, cols[2]] = dv
            d_ref[tail, cols[1]] = jnp.where(here, dk_t, d_ref[tail, cols[1]])
            d_ref[tail, cols[2]] = jnp.where(here, dv_t, d_ref[tail, cols[2]])
        return carry

    lax.fori_loop(0, n_i, image, 0)
    gb_ref[...] = jnp.sum(d_ref[...].astype(F32), 0, keepdims=True)


def attend_bwd(n_i, g, halves, adds=()):
    rows, width = g.shape
    hc = halves[0][3].shape[1] // 3
    main = (rows - PAD) // n_i
    shapes = [((rows, 3 * hc), BF), ((1, 3 * hc), F32)] * len(halves) + [((rows, width), BF)]
    flops = (2 * rows * width * 4 * hc + 10 * n_i * main * main * hc) * len(halves)
    out = call(
        functools.partial(attend_bwd_kernel, n_i, main, hc // HD, len(halves), len(adds)),
        [g] + [x for half in halves for x in half] + list(adds),
        shapes,
        scratch=[pltpu.VMEM((rows, hc), BF), pltpu.VMEM((main + PAD, 2 * hc), F32)],
        flops=flops,
        name="attend_bwd",
    )
    return out[0:-1:2], out[1:-1:2], out[-1]


epsilon = 1e-06
inv_root_two = 0.7071067811865476
inv_root_tau = 0.3989422804014327
def step_of(rows):
    return next(s for s in (48, 64, 32, 16) if rows % s == 0)


def call(kernel, ins, outs, scratch=(), flops=0, name=None, in_specs=None, **grid):
    moved = sum(x.size * x.dtype.itemsize for x in ins)
    moved += sum(int(jnp.dtype(d).itemsize) * functools.reduce(lambda a, b: a * b, s) for s, d in outs)
    vmem = pl.BlockSpec(memory_space=pltpu.VMEM)
    return pl.pallas_call(
        kernel,
        in_specs=in_specs or [vmem] * len(ins),
        out_specs=grid.pop("out_specs", [vmem] * len(outs)),
        out_shape=[jax.ShapeDtypeStruct(*s) for s in outs],
        scratch_shapes=list(scratch),
        compiler_params=pltpu.CompilerParams(vmem_limit_bytes=60 * 2**20),
        cost_estimate=pl.CostEstimate(flops=int(flops), bytes_accessed=int(moved), transcendentals=0),
        name=name,
        **grid,
    )(*ins)


def mean_parts(rows):
    centred = rows - jnp.mean(rows, axis=1, keepdims=True)
    spread = jnp.mean(centred * centred, axis=1, keepdims=True)
    inverse = lax.rsqrt(spread + epsilon)
    return centred * inverse, inverse


def fold(x):
    total = x[0:8]
    for at in range(8, x.shape[0], 8):
        total = total + x[at : at + 8]
    return total


def pack_kernel(n_i, main, norm, img_ref, gain_ref, shift_ref, x_ref, other_ref):
    width = x_ref.shape[1]

    def emit(at, x, count):
        x_ref[pl.ds(at, count), :] = x
        if norm:
            unit, _ = mean_parts(x.astype(F32))
            other_ref[pl.ds(at, count), :] = (unit * gain_ref[...] + shift_ref[...]).astype(BF)

    size = step_of(main)
    if not norm:
        other_ref[...] = jnp.zeros(other_ref.shape, F32)
    tail_row = lax.broadcasted_iota(jnp.int32, (PAD, 1), 0)
    tails = jnp.zeros((PAD, width), F32)
    for i in range(n_i):

        def step(r, carry, i=i):
            at = pl.multiple_of(r * size, size)
            x = img_ref[i, pl.ds(at, size), :]
            emit(pl.multiple_of(i * main + r * size, size), x, size)
            if not norm:
                other_ref[...] += fold(x.astype(F32))
            return carry

        lax.fori_loop(0, main // size, step, 0)
        tails = jnp.where(tail_row == i, img_ref[i, main : main + 1, :].astype(F32), tails)
    emit(n_i * main, tails.astype(BF), PAD)
    if not norm:
        other_ref[...] += fold(tails)


def pack(img, gain, shift, norm):
    n_i, seq, width = img.shape
    rows = n_i * (seq - 1) + PAD
    other = ((rows, width), BF) if norm else ((8, width), F32)
    return call(
        functools.partial(pack_kernel, n_i, seq - 1, norm),
        [img, gain, shift],
        [((rows, width), BF), other],
        name="pack",
    )


def loop_rows(rows, step):
    size = step_of(rows)

    def one(r, carry):
        step(pl.ds(pl.multiple_of(r * size, size), size))
        return carry

    lax.fori_loop(0, rows // size, one, 0)


def norm_kernel(x_ref, a_ref, b_ref, c_ref, bias_ref, gain_ref, shift_ref, mid_ref, n_ref):
    def step(at):
        moved = a_ref[at, :].astype(F32) + b_ref[at, :].astype(F32) + c_ref[at, :].astype(F32)
        middle = x_ref[at, :].astype(F32) + (moved + bias_ref[...])
        mid_ref[at, :] = middle
        unit, _ = mean_parts(middle)
        n_ref[at, :] = (unit * gain_ref[...] + shift_ref[...]).astype(BF)

    loop_rows(x_ref.shape[0], step)


def norm_second(x, parts, bias, gain, shift):
    return call(
        norm_kernel,
        [x, *parts, bias, gain, shift],
        [(x.shape, F32), (x.shape, BF)],
        name="norm_second",
    )


def norm_back_kernel(res_f32, x_ref, a_ref, b_ref, c_ref, add_ref, gain_ref, *outs):
    out_ref, low_ref, gain_out, shift_out, bias_out = outs
    for ref in (gain_out, shift_out, bias_out):
        ref[...] = jnp.zeros(ref.shape, F32)

    def step(at):
        grad = a_ref[at, :].astype(F32) + b_ref[at, :].astype(F32) + c_ref[at, :].astype(F32)
        unit, inverse = mean_parts(x_ref[at, :].astype(F32))
        scaled = grad * gain_ref[...]
        first = jnp.mean(scaled, axis=1, keepdims=True)
        second = jnp.mean(scaled * unit, axis=1, keepdims=True)
        total = add_ref[at, :].astype(F32) + inverse * (scaled - first - unit * second)
        low = total.astype(BF)
        low_ref[at, :] = low
        if res_f32:
            out_ref[at, :] = total
            bias_out[...] += fold(low.astype(F32))
        gain_out[...] += fold(grad * unit)
        shift_out[...] += fold(grad)

    loop_rows(x_ref.shape[0], step)


def norm_back(x, parts, add, gain, keep):
    rows, width = x.shape
    full = (x.shape, F32) if keep else ((8, width), F32)
    return call(
        functools.partial(norm_back_kernel, keep),
        [x, *parts, add, gain],
        [full, (x.shape, BF)] + [((8, width), F32)] * 3,
        name="norm_back",
    )


def unpack_kernel(n_i, main, sum_parts, *refs):
    size = step_of(main)
    if sum_parts:
        mid_ref, a_ref, b_ref, c_ref, bias_ref, out_ref = refs
    else:
        mid_ref, out_ref = refs

    def value(at):
        x = mid_ref[at, :]
        if sum_parts:
            moved = a_ref[at, :].astype(F32) + b_ref[at, :].astype(F32) + c_ref[at, :].astype(F32)
            x = (x.astype(F32) + moved + bias_ref[...]).astype(BF)
        return x

    for i in range(n_i):

        def step(r, carry, i=i):
            at = pl.multiple_of(i * main + r * size, size)
            out_ref[i, pl.ds(pl.multiple_of(r * size, size), size), :] = value(pl.ds(at, size))
            return carry

        lax.fori_loop(0, main // size, step, 0)
    tails = value(pl.ds(n_i * main, PAD)).astype(F32)
    for i in range(n_i):
        out_ref[i, main : main + 1, :] = tails[i : i + 1].astype(BF)


def unpack(n_i, seq, first, parts=(), bias=None):
    width = first.shape[1]
    ins = [first, *parts] + ([bias] if parts else [])
    return call(
        functools.partial(unpack_kernel, n_i, seq - 1, bool(parts)),
        ins,
        [((n_i, seq, width), BF)],
        name="unpack",
    )[0]


def mlp_kernel(n0, n1, c0, c1, up_ref, upb_ref, down_ref, act_ref, gh_ref, g0, g1, gub_ref, acc):
    j, last = pl.program_id(0), pl.num_programs(0) - 1
    size = n0.shape[0]
    for i, (n_ref, c_ref) in enumerate(((n0, c0), (n1, c1))):
        rows = slice(i * size, (i + 1) * size)
        h = dot(n_ref[...], up_ref[...], 1, 0) + upb_ref[...]
        da = dot(c_ref[...], down_ref[...], 1, 1)
        cdf = 0.5 * (1.0 + lax.erf(h * inv_root_two))
        act_ref[rows, :] = (h * cdf).astype(BF)
        gh = (da * (cdf + h * (jnp.exp(-0.5 * h * h) * inv_root_tau))).astype(BF)
        gh_ref[rows, :] = gh
        total = jnp.sum(gh.astype(F32), axis=0, keepdims=True)
        gub_ref[...] = total if i == 0 else gub_ref[...] + total
        part = dot(gh, up_ref[...], 1, 1)

        @pl.when(j == 0)
        def _():
            acc[rows, :] = part

        @pl.when(j > 0)
        def _():
            acc[rows, :] += part

    @pl.when(j == last)
    def _():
        g0[...] = acc[0:size, :].astype(BF)
        g1[...] = acc[size : 2 * size, :].astype(BF)


def mlp(n, c, up, upb, down, tile=512):
    rows, width = n[0].shape
    units = up.shape[1]
    here = whole_spec((rows, width))
    return call(
        mlp_kernel,
        [*n, *c, up, upb, down],
        [((2 * rows, units), BF)] * 2 + [((rows, width), BF)] * 2 + [((1, units), F32)],
        scratch=[pltpu.VMEM((2 * rows, width), F32)],
        flops=12 * rows * width * units,
        in_specs=[here] * 4
        + [
            pl.BlockSpec((width, tile), lambda j: (0, j)),
            pl.BlockSpec((1, tile), lambda j: (0, j)),
            pl.BlockSpec((tile, width), lambda j: (j, 0)),
        ],
        out_specs=[pl.BlockSpec((2 * rows, tile), lambda j: (0, j))] * 2
        + [here] * 2
        + [pl.BlockSpec((1, tile), lambda j: (0, j))],
        grid=(units // tile,),
        name="mlp",
    )


def wgrad_kernel(n_left, n_right, index_ref, *refs):
    left, right = refs[:n_left], refs[n_left : n_left + n_right]
    out_ref, held, sems = refs[n_left + n_right :]
    size = right[0].shape[0]
    copies = [
        pltpu.make_async_copy(r, held.at[pl.ds(i * size, size)], sems.at[i])
        for i, r in enumerate(right)
    ]

    @pl.when(pl.program_id(0) == 0)
    def _():
        for copy in copies:
            copy.start()
        for copy in copies:
            copy.wait()

    total, at = None, 0
    for ref in left:
        rows = ref.shape[0]
        part = dot(ref[...], held[at : at + rows, :], 0, 0)
        total = part if total is None else total + part
        at += rows
    out_ref[...] = total.astype(BF)


def wgrad(left, right, index, tile):
    width = right[0].shape[1]
    total = sum(r.shape[0] for r in right)
    blocks = index.shape[0]
    in_specs = [pl.BlockSpec((x.shape[0], tile), lambda j, at: (0, at[j])) for x in left]
    in_specs += [pl.BlockSpec(memory_space=pl.ANY)] * len(right)
    moved = 2 * (total * (width + blocks * tile) + blocks * tile * width)
    return pl.pallas_call(
        functools.partial(wgrad_kernel, len(left), len(right)),
        grid_spec=pltpu.PrefetchScalarGridSpec(
            num_scalar_prefetch=1,
            grid=(blocks,),
            in_specs=in_specs,
            out_specs=pl.BlockSpec((tile, width), lambda j, at: (j, 0)),
            scratch_shapes=[
                pltpu.VMEM((total, width), BF),
                pltpu.SemaphoreType.DMA((len(right),)),
            ],
        ),
        out_shape=jax.ShapeDtypeStruct((blocks * tile, width), BF),
        compiler_params=pltpu.CompilerParams(vmem_limit_bytes=60 * 2**20),
        cost_estimate=pl.CostEstimate(
            flops=2 * total * blocks * tile * width, bytes_accessed=moved, transcendentals=0
        ),
        name="wgrad",
    )(index, *left, *right)


def place_kernel(count, transposed, at_ref, *refs):
    blocks, out_ref = refs[:count], refs[count]
    size = blocks[0].shape[0]
    target = refs[count + 1] if transposed else out_ref
    for i, ref in enumerate(blocks):
        rows = pl.ds(pl.multiple_of(at_ref[i] * size, size), size)
        target[rows, :] = ref[...].astype(target.dtype)
    if transposed:
        for at in range(0, target.shape[0], 256):
            out_ref[:, at : at + 256] = target[at : at + 256, :].astype(F32).T


def place(blocks, at, transposed):
    size, width = blocks[0].shape
    rows = size * len(blocks)
    shape = (width, rows) if transposed else (rows, width)
    vmem = pl.BlockSpec(memory_space=pltpu.VMEM)
    return call(
        functools.partial(place_kernel, len(blocks), transposed),
        [at, *blocks],
        [(shape, F32)],
        scratch=[pltpu.VMEM((rows, width), BF)] if transposed else [],
        in_specs=[pl.BlockSpec(memory_space=pltpu.SMEM)] + [vmem] * len(blocks),
        name="place",
    )[0]


class Order:
    def __init__(self):
        self.last = None

    def gate(self, x):
        return x if self.last is None else lax.optimization_barrier((x, self.last))[0]

    def __call__(self, kernel, x, *rest):
        out = kernel(self.gate(x), *rest)
        self.last = jax.tree.leaves(out)[-1]
        return out

    def meet(self, *arrays):
        self.last = lax.optimization_barrier((self.last, *arrays))[0]


class Layout:
    def __init__(self, dp, tensor):
        self.dp, self.tensor = dp, tensor
        self.n_p, self.n_hi = dp // 2, tensor // 2
        self.bits = [1 << b for b in range(self.n_p.bit_length() - 1)]

    def move(self, x, p=0, c=0, hi=0, lo=0):
        dp_mask, tensor_mask = 2 * p + c, 2 * hi + lo
        pairs = [
            (d * self.tensor + t, (d ^ dp_mask) * self.tensor + (t ^ tensor_mask))
            for d in range(self.dp)
            for t in range(self.tensor)
        ]
        return lax.ppermute(x, ("dp", "tensor"), pairs)

    def place_of(self, p, order):
        n = len(order)
        place = 0
        for i, bit in enumerate(order):
            place = place + (p // bit) % 2 * (1 << (n - 1 - i))
        return place

    def spread(self, block, order):
        have = {0: block}
        for bit in order:
            have.update({m ^ bit: self.move(x, p=bit) for m, x in list(have.items())})
        return have

    def spread_direct(self, block):
        return {m: self.move(block, p=m) if m else block for m in range(self.n_p)}


def on_device(
    lay,
    images,
    first_gain,
    first_shift,
    qkv_weight,
    qv_bias,
    out_weight,
    out_bias,
    second_gain,
    second_shift,
    up_weight,
    up_bias,
    down_weight,
    down_bias,
    cotangent,
):
    n_p, n_hi = lay.n_p, lay.n_hi
    n_i, seq, width = images.shape
    columns = qkv_weight.shape[2]
    units = up_weight.shape[1]
    hc, hu = columns // 2, units // 2
    dp = lax.axis_index("dp")
    p, c = dp // 2, dp % 2
    up_order, down_order = lay.bits, lay.bits[::-1]
    order = Order()
    first_gain, first_shift, out_bias, second_gain, second_shift, down_bias = [
        v.reshape(1, width)
        for v in (first_gain, first_shift, out_bias, second_gain, second_shift, down_bias)
    ]

    def half(x, axis):
        n = x.shape[axis] // 2
        return lax.dynamic_slice_in_dim(x, c * n, n, axis)

    def block(x, axis, at):
        n = x.shape[axis] // n_p
        return lax.dynamic_slice_in_dim(x, at * n, n, axis)

    def put(buf, x, axis, at):
        return lax.dynamic_update_slice_in_dim(buf, x, at, axis)

    qkv_half = half(qkv_weight, 2)
    qkv_mine = jnp.concatenate([qkv_half[i] for i in range(3)], 1)
    pad_rows = -hc % (16 * n_p)
    out_mine = jnp.pad(half(out_weight, 0), ((0, pad_rows), (0, 0)))
    qkv_cut, out_cut = block(qkv_mine, 0, p), block(out_mine, 0, p)
    qkv_hi = [lay.move(qkv_cut, hi=k) for k in range(1, n_hi)]
    out_hi = [lay.move(out_cut, hi=k) for k in range(1, n_hi)]
    qv_half, upb_half = half(qv_bias, 1), half(up_bias, 0)
    bias_all = [jnp.concatenate([qv_half.reshape(-1), upb_half])]
    bias_all += [lay.move(bias_all[0], hi=k) for k in range(1, n_hi)]
    upb_work = jnp.concatenate([b[2 * hc :] for b in bias_all]).reshape(1, -1)
    qkv_bias = [
        jnp.concatenate([b[:hc], jnp.zeros((hc,), F32), b[hc : 2 * hc]]).reshape(1, -1)
        for b in bias_all
    ]

    x_unit, first_own = order(pack, images, first_gain, first_shift, True)
    first_c, first_z = lay.move(first_own, c=1), lay.move(first_own, lo=1)
    seed_unit, grad_down_bias = order(pack, cotangent, first_gain, first_shift, False)
    seed_c = lay.move(seed_unit, c=1)

    qkv_work, out_work = [qkv_mine], [out_mine]
    forward = [[None] * 4 for _ in range(n_hi)]

    def attention(k, u, n, adds=()):
        adds = list(adds) + ([forward[k - 1][u][4]] if k else [])
        forward[k][u] = order(
            lambda x: attend_fwd(n_i, x, qkv_work[k], qkv_bias[k], out_work[k], adds), n
        )
        return forward[k][u][4]

    def spread_work(got_all, axis):
        return [
            [(k * n_p + (p ^ m), x) for m, x in lay.spread_direct(got).items()]
            for k, got in enumerate(got_all, 1)
        ]

    attention(0, 0, first_own)
    up_hi = [lay.move(block(half(order.gate(up_weight), 1), 1, p), hi=k) for k in range(1, n_hi)]
    attention(0, 1, first_c)
    first_zc = lay.move(order.gate(first_z), c=1)
    seed_z = lay.move(lax.optimization_barrier((seed_unit, first_zc))[0], lo=1)
    qkv_got = spread_work([order.gate(x) for x in qkv_hi], 0)
    out_got = spread_work([order.gate(x) for x in out_hi], 0)
    attention(0, 2, first_z)
    down_hi = [
        lay.move(block(half(order.gate(down_weight), 0), 0, p), hi=k) for k in range(1, n_hi)
    ]
    attention(0, 3, first_zc)
    up_got = spread_work([order.gate(x) for x in up_hi], 1)
    for k in range(1, n_hi):
        for got, work, like in ((qkv_got, qkv_work, qkv_mine), (out_got, out_work, out_mine)):
            full = jnp.zeros_like(like)
            for at, x in got[k - 1]:
                full = put(full, x, 0, (at - k * n_p) * x.shape[0])
            work.append(full)
    normed = (first_own, first_c, first_z, first_zc)
    for k in range(1, n_hi - 1):
        for u in range(4):
            attention(k, u, normed[u])
    k = n_hi - 1
    moved_3 = lay.move(attention(k, 3, first_zc), c=1)
    seed_zc = lay.move(order.gate(seed_z), c=1)
    moved_1 = lay.move(attention(k, 1, first_c), c=1)
    down_got = spread_work([order.gate(x) for x in down_hi], 0)
    moved_2 = lay.move(attention(k, 2, first_z, [moved_3]), lo=1)
    attention_parts = (attention(k, 0, first_own), moved_1, moved_2)
    seed = [seed_unit, seed_c, seed_z, seed_zc]
    normed_first = list(normed)

    def fill_up(x):
        work = put(jnp.zeros((width, n_hi * hu), BF), half(x, 1), 1, 0)
        for at, part in (pair for got in up_got for pair in got):
            work = put(work, part, 1, at * part.shape[1])
        return work

    def fill_down(x):
        work = put(jnp.zeros((n_hi * hu, width), BF), half(x, 0), 0, 0)
        for at, part in (pair for got in down_got for pair in got):
            work = put(work, part, 0, at * part.shape[0])
        return work

    up_work = order(fill_up, up_weight)
    down_work = order(fill_down, down_weight)
    middle, second_own = order(
        lambda x: norm_second(x, attention_parts, out_bias, second_gain, second_shift), x_unit
    )
    second_c, second_z = lay.move(second_own, c=1), lay.move(second_own, lo=1)

    near = order(lambda n: mlp([n, second_c], seed[:2], up_work, upb_work, down_work), second_own)
    second_zc = lay.move(order.gate(second_z), c=1)
    other_c = lay.move(near[3], c=1)
    low_near = order(lambda x: dot(x, down_work, 1, 0).astype(BF), near[0])
    far = order(lambda n: mlp([n, second_zc], seed[2:], up_work, upb_work, down_work), second_z)
    normed_second = [second_own, second_c, second_z, second_zc]

    def index(order_of, other):
        top = lay.place_of(p, order_of) // (n_p // 2)
        return jnp.stack([2 * k + (top ^ other) for k in range(n_hi)]).astype(jnp.int32)

    def mlp_grad(which, right, order_of, other):
        return order(
            lambda x: wgrad([x, far[which]], right, index(order_of, other), hu // 2), near[which]
        )

    far_c = lay.move(far[3], c=1)
    down_send = mlp_grad(0, seed, down_order, 1)
    down_recv = lay.move(down_send, p=down_order[0])

    def join(*parts):
        total = parts[0].astype(F32)
        for x in parts[1:]:
            total = total + x.astype(F32)
        return total.astype(BF)

    far_sum = order(lambda x: join(x, far_c), far[2])
    grad_second = (near[2], other_c, lay.move(far_sum, lo=1))
    up_send = mlp_grad(1, normed_second, up_order, 1)
    up_recv = lay.move(up_send, p=up_order[0])
    down_keep = mlp_grad(0, seed, down_order, 0)
    rows = x_unit.shape[0]
    grad_middle, grad_branch, grad_second_gain, grad_second_shift, grad_out_bias = order(
        lambda x: norm_back(x, grad_second, seed_unit, second_gain, True), middle
    )
    branch_c, branch_z = lay.move(grad_branch, c=1), lay.move(grad_branch, lo=1)
    low_far = order(lambda x: dot(x, down_work, 1, 0).astype(BF), far[0])
    low_far_c = lay.move(low_far[rows:], c=1)
    low_near_c = lay.move(low_near[rows:], c=1)
    up_keep = mlp_grad(1, normed_second, up_order, 0)

    def halve(keep, recv, order_of, stage, parts):
        bit = order_of[stage]
        side = (p // bit) % 2
        shape = (parts, 2, keep.shape[0] // (2 * parts), width)

        def pick(x, s):
            x = lax.dynamic_index_in_dim(x.reshape(shape), s, 1, keepdims=False)
            return x.reshape(-1, width)

        send = order(lambda x: join(pick(x, 1 - side), pick(recv, 1 - side)), keep)
        keep = join(pick(keep, side), pick(recv, side))
        return keep, lay.move(send, p=bit)

    def settle_hi(keep, recv):
        size = keep.shape[0] // n_hi
        total = order(lambda x: join(x, recv), keep)
        got = [lay.move(total[k * size : (k + 1) * size], hi=k) for k in range(1, n_hi)]
        return total[:size], got

    def whole_grad(mine, order_of):
        have = lay.spread(mine, order_of[::-1])
        at, out = [], []
        for core in (0, 1):
            for mask, x in have.items():
                at.append((c ^ core) * n_p + lay.place_of(p ^ mask, order_of))
                out.append(lay.move(x, c=1) if core else x)
        return out, jnp.stack(at).astype(jnp.int32)

    backward = [[None] * 4 for _ in range(n_hi)]
    branch = [grad_branch, branch_c, branch_z, None]

    def attention_back(k, u, adds=()):
        adds = list(adds) + ([backward[k + 1][u][2]] if k < n_hi - 1 else [])
        f = forward[k][u]
        backward[k][u] = order(
            lambda g: attend_bwd(n_i, g, [(f[0], f[2], f[3], qkv_work[k], out_work[k])], adds),
            branch[u],
        )
        return backward[k][u][2]

    whole_index = jnp.zeros((1,), jnp.int32)

    def attention_grad(k):
        qkv = order(
            lambda x: wgrad([x] + [b[0][0] for b in backward[k][1:]], normed_first, whole_index, 3 * hc),
            backward[k][0][0][0],
        )
        heads = [f[1] for f in forward[k]]
        out = order(lambda x: wgrad([x] + heads[1:], branch, whole_index, hc), heads[0])
        return jnp.concatenate([qkv, out])

    def attention_send(k, order_of):
        grad = attention_grad(k)
        if order_of != orders[0]:
            blocks = jnp.split(grad, n_p)
            owner = {lay.place_of(q, order_of): lay.place_of(q, orders[0]) for q in range(n_p)}
            grad = jnp.concatenate([blocks[owner[i]] for i in range(n_p)])
        top = lay.place_of(p, order_of) // (n_p // 2)
        size = grad.shape[0] // 2
        send = lax.dynamic_slice_in_dim(grad, (1 - top) * size, size, 0)
        keep = lax.dynamic_slice_in_dim(grad, top * size, size, 0)
        return keep, lay.move(send, p=order_of[0])

    down_pair, up_pair = (down_keep, down_recv), (up_keep, up_recv)
    attn_pairs = [None] * n_hi
    orders = [up_order] + [down_order] * (n_hi - 1)
    n_stage = len(lay.bits)
    k = n_hi - 1
    down_pair = halve(*down_pair, down_order, 1, n_hi)
    attention_back(k, 0)
    branch[3] = lay.move(order.gate(branch_z), c=1)
    attention_back(k, 1)
    up_pair = halve(*up_pair, up_order, 1, n_hi)
    low_far_sum = order(lambda x: join(x, low_far_c), low_far[:rows])
    low_far_z = lay.move(low_far_sum, lo=1)
    attention_back(k, 2)
    attention_back(k, 3)
    for stage in range(2, n_stage):
        down_pair = halve(*down_pair, down_order, stage, n_hi)
        up_pair = halve(*up_pair, up_order, stage, n_hi)
    down_mine, down_hi_got = settle_hi(*down_pair)
    attn_pairs[k] = attention_send(k, orders[k])
    for k in range(n_hi - 2, 0, -1):
        for u in range(4):
            attention_back(k, u)
        attn_pairs[k] = attention_send(k, orders[k])
    moved_3 = lay.move(attention_back(0, 3), c=1)
    up_mine, up_hi_got = settle_hi(*up_pair)
    moved_1 = lay.move(attention_back(0, 1), c=1)
    for k in range(1, n_hi):
        for stage in range(1, n_stage):
            attn_pairs[k] = halve(*attn_pairs[k], orders[k], stage, 1)
    moved_2 = lay.move(attention_back(0, 2, [moved_3]), lo=1)
    down_mine = order(lambda x: join(x, *down_hi_got), down_mine)
    down_all = whole_grad(down_mine, down_order)
    grad_first = (attention_back(0, 0), moved_1, moved_2)
    attn_hi = []
    for k in range(1, n_hi):
        total = order(lambda x, k=k: join(x, attn_pairs[k][1]), attn_pairs[k][0])
        attn_hi.append(lay.move(total, hi=k))
    attn_pairs[0] = attention_send(0, orders[0])
    up_mine = order(lambda x: join(x, *up_hi_got), up_mine)
    up_all = whole_grad(up_mine, up_order)
    result_parts = (low_near[:rows], low_near_c, low_far_z)
    result = order(lambda x: unpack(n_i, seq, x, result_parts, down_bias), middle)
    for stage in range(1, n_stage):
        attn_pairs[0] = halve(*attn_pairs[0], orders[0], stage, 1)
    _, grad_images, grad_first_gain, grad_first_shift, _ = order(
        lambda x: norm_back(x, grad_first, grad_middle, first_gain, False), x_unit
    )
    attn_mine = order(lambda x: join(x, attn_pairs[0][1], *attn_hi), attn_pairs[0][0])
    attn_all = whole_grad(attn_mine, orders[0])
    grad_images = order(lambda x: unpack(n_i, seq, x), grad_images)
    grad_down_weight = order(
        lambda x: place([x] + down_all[0][1:], down_all[1], False), down_all[0][0]
    )
    grad_up_weight = order(lambda x: place([x] + up_all[0][1:], up_all[1], True), up_all[0][0])

    tensor_at = lax.axis_index("tensor")
    all_units, all_columns = units * lay.tensor, columns * lay.tensor
    grad_up_bias = (near[4] + far[4])[0]
    wide_up = jnp.zeros((all_units,), F32)
    wide_qv = jnp.zeros((2, all_columns), F32)
    for k in range(n_hi):
        shard = tensor_at ^ (2 * k)
        wide_up = put(wide_up, grad_up_bias[k * hu : (k + 1) * hu], 0, shard * units + c * hu)
        bias = sum(b[1][0] for b in backward[k])[0]
        bias = jnp.stack([bias[:hc], bias[2 * hc :]])
        wide_qv = put(wide_qv, bias, 1, shard * columns + c * hc)
    sums = (
        grad_first_gain,
        grad_first_shift,
        grad_out_bias,
        grad_second_gain,
        grad_second_shift,
        grad_down_bias,
    )
    vector = jnp.concatenate(
        [jnp.sum(x, axis=0) for x in sums] + [wide_up, wide_qv.reshape(-1)]
    )
    for bit in lay.bits:
        vector = vector + lay.move(vector, p=bit)
    vector = vector + lay.move(vector, c=1)
    for k in [1 << b for b in range(lay.tensor.bit_length() - 1)]:
        vector = vector + lay.move(vector, lo=k & 1, hi=k >> 1)
    norms = vector[: 6 * width].reshape(6, width)
    vector = vector[6 * width :]
    grad_up_bias = lax.dynamic_slice_in_dim(vector, tensor_at * units, units, 0)
    grad_qv_bias = lax.dynamic_slice_in_dim(
        vector[all_units:].reshape(2, all_columns), tensor_at * columns, columns, 1
    )

    buf = jnp.zeros((8 * hc, width), BF)
    for i, x in enumerate(attn_all[0]):
        buf = put(buf, x, 0, attn_all[1][i] * x.shape[0])
    buf = buf.reshape(2, 4, hc, width)
    grad_out_weight = buf[:, 3].reshape(columns, width).astype(F32)
    grad_qkv_weight = jnp.stack([buf[:, i].reshape(columns, width).T for i in range(3)]).astype(F32)
    return (
        result,
        grad_images,
        norms[0],
        norms[1],
        grad_qkv_weight,
        grad_qv_bias,
        grad_out_weight,
        norms[2],
        norms[3],
        norms[4],
        grad_up_weight,
        grad_up_bias,
        grad_down_weight,
        norms[5],
    )


def solution(mesh):
    lay = Layout(mesh.shape["dp"], mesh.shape["tensor"])
    rows = P(("dp", "tensor"), None, None)
    qkv, qv = P(None, None, "tensor"), P(None, "tensor")
    line, up, down, rep = P("tensor"), P(None, "tensor"), P("tensor", None), P()
    return jax.shard_map(
        functools.partial(on_device, lay),
        mesh=mesh,
        in_specs=(rows, rep, rep, qkv, qv, down, rep, rep, rep, up, line, down, rep, rows),
        out_specs=(rows, rows, rep, rep, qkv, qv, down, rep, rep, rep, up, line, down, rep),
        check_vma=False,
    )
```

```python
import functools

import jax
import jax.numpy as jnp
from jax import lax
from jax.experimental import pallas as pl
from jax.experimental.pallas import tpu as pltpu
from jax.sharding import PartitionSpec as P

HD = 104
PAD = 16
BF = jnp.bfloat16
F32 = jnp.float32


def dot(a, b, ca, cb):
    return lax.dot_general(a, b, (((ca,), (cb,)), ((), ())), preferred_element_type=F32)


def whole_spec(shape):
    return pl.BlockSpec(shape, lambda *_: (0,) * len(shape), pipeline_mode=pl.Buffered(1))


def head_mask(heads):
    lane = lax.broadcasted_iota(jnp.int32, (8, heads * HD), 1)
    row = lax.broadcasted_iota(jnp.int32, (8, heads * HD), 0)
    return (lane >= row * HD) & (lane < row * HD + HD)


def attend_fwd_kernel(n_i, main, heads, n_add, n_ref, w_ref, b_ref, *refs):
    adds = refs[:n_add]
    qkv_ref, ho_ref, lse_ref, lset_ref, out_ref = refs[n_add:]
    hc = heads * HD
    tail = pl.ds(n_i * main, PAD)
    qkv_ref[...] = (dot(n_ref[...], w_ref[0 : 3 * hc, :], 1, 1) + b_ref[...]).astype(BF)
    ho_ref[tail, :] = jnp.zeros((PAD, hc), BF)
    factor = HD ** -0.5
    tail_row = lax.broadcasted_iota(jnp.int32, (PAD, 1), 0)
    per_head = head_mask(heads)

    def image(i, carry):
        rows = pl.ds(pl.multiple_of(i * main, main), main)
        here = tail_row == i
        bar = jnp.where(here, 0.0, -1e30)
        bar_all = jnp.concatenate([jnp.zeros((main, 1), F32), bar], 0)

        def both(cols):
            return jnp.concatenate([qkv_ref[rows, cols], qkv_ref[tail, cols]], 0)

        q_t = jnp.sum(jnp.where(here, qkv_ref[tail, 0:hc].astype(F32), 0.0), 0, keepdims=True)
        q_b = jnp.where(per_head, q_t, 0.0).astype(BF)
        s = dot(both(slice(hc, 2 * hc)), q_b, 1, 1) * factor + bar_all
        top = jnp.max(s, 0, keepdims=True)
        e = jnp.exp(s - top)
        total = jnp.sum(e, 0, keepdims=True)
        o = dot((e * (1.0 / total)).astype(BF), both(slice(2 * hc, 3 * hc)), 0, 0)
        o = jnp.sum(jnp.where(per_head, o, 0.0), 0, keepdims=True).astype(BF)
        ho_ref[tail, :] = jnp.where(here, o, ho_ref[tail, :])
        lset_ref[pl.ds(i, 1), 0:8] = top + jnp.log(total)
        for h in range(heads):
            cols = [slice(t * hc + h * HD, t * hc + (h + 1) * HD) for t in range(3)]
            q = qkv_ref[rows, cols[0]]
            s = dot(qkv_ref[rows, cols[1]], q, 1, 1) * factor
            s_t = dot(qkv_ref[tail, cols[1]], q, 1, 1) * factor + bar
            top = jnp.maximum(jnp.max(s, 0, keepdims=True), jnp.max(s_t, 0, keepdims=True))
            e, e_t = jnp.exp(s - top), jnp.exp(s_t - top)
            total = jnp.sum(e, 0, keepdims=True) + jnp.sum(e_t, 0, keepdims=True)
            inv = 1.0 / total
            o = dot((e * inv).astype(BF), qkv_ref[rows, cols[2]], 0, 0)
            o = o + dot((e_t * inv).astype(BF), qkv_ref[tail, cols[2]], 0, 0)
            ho_ref[rows, h * HD : (h + 1) * HD] = o.astype(BF)
            lse_ref[h : h + 1, rows] = top + jnp.log(total)
        return carry

    lax.fori_loop(0, n_i, image, 0)
    total = dot(ho_ref[...], w_ref[3 * hc :, :], 1, 0)
    for ref in adds:
        total = total + ref[...].astype(F32)
    out_ref[...] = total.astype(BF)


def attend_fwd(n_i, n, w, b, adds=()):
    rows, width = n.shape
    hc = w.shape[0] // 4
    main = (rows - PAD) // n_i
    shapes = (
        ((rows, 3 * hc), BF),
        ((rows, hc), BF),
        ((8, n_i * main), F32),
        ((8, 128), F32),
        ((rows, width), BF),
    )
    flops = 2 * rows * width * 4 * hc + 4 * n_i * main * main * hc
    return call(
        functools.partial(attend_fwd_kernel, n_i, main, hc // HD, len(adds)),
        [n, w, b, *adds],
        shapes,
        flops=flops,
        name="attend_fwd",
    )


def attend_bwd_kernel(n_i, main, heads, n_add, g_ref, qkv_ref, lse_ref, lset_ref, w_ref, *refs):
    adds = refs[:n_add]
    d_ref, gb_ref, gn_ref, gh_ref, kv_ref = refs[n_add:]
    hc = heads * HD
    tail = pl.ds(n_i * main, PAD)
    gh_ref[...] = dot(g_ref[...], w_ref[3 * hc :, :], 1, 1).astype(BF)
    d_ref[tail, :] = jnp.zeros((PAD, 3 * hc), BF)
    factor = HD ** -0.5
    tail_row = lax.broadcasted_iota(jnp.int32, (PAD, 1), 0)
    per_head = head_mask(heads)

    def image(i, carry):
        rows = pl.ds(pl.multiple_of(i * main, main), main)
        here = tail_row == i
        bar = jnp.where(here, 0.0, -1e30)
        bar_all = jnp.concatenate([jnp.zeros((main, 1), F32), bar], 0)

        def both(cols):
            return jnp.concatenate([qkv_ref[rows, cols], qkv_ref[tail, cols]], 0)

        def last(ref, cols):
            row = jnp.sum(jnp.where(here, ref[tail, cols].astype(F32), 0.0), 0, keepdims=True)
            return jnp.where(per_head, row, 0.0).astype(BF)

        q_b, go_b = last(qkv_ref, slice(0, hc)), last(gh_ref, slice(0, hc))
        k_all, v_all = both(slice(hc, 2 * hc)), both(slice(2 * hc, 3 * hc))
        p = jnp.exp(dot(k_all, q_b, 1, 1) * factor + bar_all - lset_ref[pl.ds(i, 1), 0:8])
        dp = dot(v_all, go_b, 1, 1)
        ds = (p * (dp - jnp.sum(p * dp, 0, keepdims=True))).astype(BF)
        dq = dot(ds, k_all, 0, 0) * factor
        dq = jnp.sum(jnp.where(per_head, dq, 0.0), 0, keepdims=True).astype(BF)
        d_ref[tail, 0:hc] = jnp.where(here, dq, d_ref[tail, 0:hc])
        kv_ref[:, 0:hc] = dot(ds, q_b, 1, 0)
        kv_ref[:, hc : 2 * hc] = dot(p.astype(BF), go_b, 1, 0)
        for h in range(heads):
            head = slice(h * HD, (h + 1) * HD)
            cols = [slice(t * hc + h * HD, t * hc + (h + 1) * HD) for t in range(3)]
            q, go = qkv_ref[rows, cols[0]], gh_ref[rows, head]
            k, k_t = qkv_ref[rows, cols[1]], qkv_ref[tail, cols[1]]
            v, v_t = qkv_ref[rows, cols[2]], qkv_ref[tail, cols[2]]
            lse = lse_ref[h : h + 1, rows]
            p = jnp.exp(dot(k, q, 1, 1) * factor - lse)
            p_t = jnp.exp(dot(k_t, q, 1, 1) * factor + bar - lse)
            dp, dp_t = dot(v, go, 1, 1), dot(v_t, go, 1, 1)
            inner = jnp.sum(p * dp, 0, keepdims=True) + jnp.sum(p_t * dp_t, 0, keepdims=True)
            ds = (p * (dp - inner)).astype(BF)
            ds_t = (p_t * (dp_t - inner)).astype(BF)
            d_ref[rows, cols[0]] = ((dot(ds, k, 0, 0) + dot(ds_t, k_t, 0, 0)) * factor).astype(BF)
            dk = ((dot(ds, q, 1, 0) + kv_ref[0:main, head]) * factor).astype(BF)
            dk_t = ((dot(ds_t, q, 1, 0) + kv_ref[main:, head]) * factor).astype(BF)
            head_v = slice(hc + h * HD, hc + (h + 1) * HD)
            dv = (dot(p.astype(BF), go, 1, 0) + kv_ref[0:main, head_v]).astype(BF)
            dv_t = (dot(p_t.astype(BF), go, 1, 0) + kv_ref[main:, head_v]).astype(BF)
            d_ref[rows, cols[1]] = dk
            d_ref[rows, cols[2]] = dv
            d_ref[tail, cols[1]] = jnp.where(here, dk_t, d_ref[tail, cols[1]])
            d_ref[tail, cols[2]] = jnp.where(here, dv_t, d_ref[tail, cols[2]])
        return carry

    lax.fori_loop(0, n_i, image, 0)
    gb_ref[...] = jnp.sum(d_ref[...].astype(F32), 0, keepdims=True)
    total = dot(d_ref[...], w_ref[0 : 3 * hc, :], 1, 0)
    for ref in adds:
        total = total + ref[...].astype(F32)
    gn_ref[...] = total.astype(BF)


def attend_bwd(n_i, g, half, adds=()):
    rows, width = g.shape
    hc = half[3].shape[0] // 4
    main = (rows - PAD) // n_i
    shapes = [((rows, 3 * hc), BF), ((1, 3 * hc), F32), ((rows, width), BF)]
    return call(
        functools.partial(attend_bwd_kernel, n_i, main, hc // HD, len(adds)),
        [g, *half, *adds],
        shapes,
        scratch=[pltpu.VMEM((rows, hc), BF), pltpu.VMEM((main + PAD, 2 * hc), F32)],
        flops=2 * rows * width * 4 * hc + 10 * n_i * main * main * hc,
        name="attend_bwd",
    )


epsilon = 1e-06
inv_root_two = 0.7071067811865476
inv_root_tau = 0.3989422804014327
HINT = 30
def step_of(rows):
    return next(s for s in (48, 64, 32, 16) if rows % s == 0)


def call(kernel, ins, outs, scratch=(), flops=0, name=None, in_specs=None, **grid):
    moved = sum(x.size * x.dtype.itemsize for x in ins)
    moved += sum(int(jnp.dtype(d).itemsize) * functools.reduce(lambda a, b: a * b, s) for s, d in outs)
    vmem = pl.BlockSpec(memory_space=pltpu.VMEM)
    return pl.pallas_call(
        kernel,
        in_specs=in_specs or [vmem] * len(ins),
        out_specs=grid.pop("out_specs", [vmem] * len(outs)),
        out_shape=[jax.ShapeDtypeStruct(*s) for s in outs],
        scratch_shapes=list(scratch),
        compiler_params=pltpu.CompilerParams(vmem_limit_bytes=60 * 2**20),
        cost_estimate=pl.CostEstimate(
            flops=int(flops) * HINT, bytes_accessed=int(moved) * HINT, transcendentals=0
        ),
        name=name,
        **grid,
    )(*ins)


def mean_parts(rows):
    centred = rows - jnp.mean(rows, axis=1, keepdims=True)
    spread = jnp.mean(centred * centred, axis=1, keepdims=True)
    inverse = lax.rsqrt(spread + epsilon)
    return centred * inverse, inverse


def fold(x):
    total = x[0:8]
    for at in range(8, x.shape[0], 8):
        total = total + x[at : at + 8]
    return total


def pack_kernel(n_i, main, norm, img_ref, gain_ref, shift_ref, x_ref, other_ref):
    width = x_ref.shape[1]

    def emit(at, x, count):
        x_ref[pl.ds(at, count), :] = x
        if norm:
            unit, _ = mean_parts(x.astype(F32))
            other_ref[pl.ds(at, count), :] = (unit * gain_ref[...] + shift_ref[...]).astype(BF)

    size = step_of(main)
    if not norm:
        other_ref[...] = jnp.zeros(other_ref.shape, F32)
    tail_row = lax.broadcasted_iota(jnp.int32, (PAD, 1), 0)
    tails = jnp.zeros((PAD, width), F32)
    for i in range(n_i):

        def step(r, carry, i=i):
            at = pl.multiple_of(r * size, size)
            x = img_ref[i, pl.ds(at, size), :]
            emit(pl.multiple_of(i * main + r * size, size), x, size)
            if not norm:
                other_ref[...] += fold(x.astype(F32))
            return carry

        lax.fori_loop(0, main // size, step, 0)
        tails = jnp.where(tail_row == i, img_ref[i, main : main + 1, :].astype(F32), tails)
    emit(n_i * main, tails.astype(BF), PAD)
    if not norm:
        other_ref[...] += fold(tails)


def pack(img, gain, shift, norm):
    n_i, seq, width = img.shape
    rows = n_i * (seq - 1) + PAD
    other = ((rows, width), BF) if norm else ((8, width), F32)
    return call(
        functools.partial(pack_kernel, n_i, seq - 1, norm),
        [img, gain, shift],
        [((rows, width), BF), other],
        name="pack",
    )


def loop_rows(rows, step):
    size = step_of(rows)

    def one(r, carry):
        step(pl.ds(pl.multiple_of(r * size, size), size))
        return carry

    lax.fori_loop(0, rows // size, one, 0)


def norm_kernel(x_ref, a_ref, b_ref, c_ref, bias_ref, gain_ref, shift_ref, mid_ref, n_ref):
    def step(at):
        moved = a_ref[at, :].astype(F32) + b_ref[at, :].astype(F32) + c_ref[at, :].astype(F32)
        middle = x_ref[at, :].astype(F32) + (moved + bias_ref[...])
        mid_ref[at, :] = middle
        unit, _ = mean_parts(middle)
        n_ref[at, :] = (unit * gain_ref[...] + shift_ref[...]).astype(BF)

    loop_rows(x_ref.shape[0], step)


def norm_second(x, parts, bias, gain, shift):
    return call(
        norm_kernel,
        [x, *parts, bias, gain, shift],
        [(x.shape, F32), (x.shape, BF)],
        name="norm_second",
    )


def norm_back_kernel(res_f32, x_ref, a_ref, b_ref, c_ref, add_ref, gain_ref, *outs):
    out_ref, low_ref, gain_out, shift_out, bias_out = outs
    for ref in (gain_out, shift_out, bias_out):
        ref[...] = jnp.zeros(ref.shape, F32)

    def step(at):
        grad = a_ref[at, :].astype(F32) + b_ref[at, :].astype(F32) + c_ref[at, :].astype(F32)
        unit, inverse = mean_parts(x_ref[at, :].astype(F32))
        scaled = grad * gain_ref[...]
        first = jnp.mean(scaled, axis=1, keepdims=True)
        second = jnp.mean(scaled * unit, axis=1, keepdims=True)
        total = add_ref[at, :].astype(F32) + inverse * (scaled - first - unit * second)
        low = total.astype(BF)
        low_ref[at, :] = low
        if res_f32:
            out_ref[at, :] = total
            bias_out[...] += fold(low.astype(F32))
        gain_out[...] += fold(grad * unit)
        shift_out[...] += fold(grad)

    loop_rows(x_ref.shape[0], step)


def norm_back(x, parts, add, gain, keep):
    rows, width = x.shape
    full = (x.shape, F32) if keep else ((8, width), F32)
    return call(
        functools.partial(norm_back_kernel, keep),
        [x, *parts, add, gain],
        [full, (x.shape, BF)] + [((8, width), F32)] * 3,
        name="norm_back",
    )


def unpack_kernel(n_i, main, sum_parts, *refs):
    size = step_of(main)
    if sum_parts:
        mid_ref, a_ref, b_ref, c_ref, bias_ref, out_ref = refs
    else:
        mid_ref, out_ref = refs

    def value(at):
        x = mid_ref[at, :]
        if sum_parts:
            moved = a_ref[at, :].astype(F32) + b_ref[at, :].astype(F32) + c_ref[at, :].astype(F32)
            x = (x.astype(F32) + moved + bias_ref[...]).astype(BF)
        return x

    for i in range(n_i):

        def step(r, carry, i=i):
            at = pl.multiple_of(i * main + r * size, size)
            out_ref[i, pl.ds(pl.multiple_of(r * size, size), size), :] = value(pl.ds(at, size))
            return carry

        lax.fori_loop(0, main // size, step, 0)
    tails = value(pl.ds(n_i * main, PAD)).astype(F32)
    for i in range(n_i):
        out_ref[i, main : main + 1, :] = tails[i : i + 1].astype(BF)


def unpack(n_i, seq, first, parts=(), bias=None):
    width = first.shape[1]
    ins = [first, *parts] + ([bias] if parts else [])
    return call(
        functools.partial(unpack_kernel, n_i, seq - 1, bool(parts)),
        ins,
        [((n_i, seq, width), BF)],
        name="unpack",
    )[0]


def mlp_kernel(n_add, n0, n1, c0, c1, up_ref, upb_ref, down_ref, *refs):
    act_ref, gh_ref, g0, g1, gub_ref, acc = refs[2 * n_add :]
    j, last = pl.program_id(0), pl.num_programs(0) - 1
    size = n0.shape[0]
    for i, (n_ref, c_ref) in enumerate(((n0, c0), (n1, c1))):
        rows = slice(i * size, (i + 1) * size)
        h = dot(n_ref[...], up_ref[...], 1, 0) + upb_ref[...]
        da = dot(c_ref[...], down_ref[...], 1, 1)
        cdf = 0.5 * (1.0 + lax.erf(h * inv_root_two))
        act_ref[rows, :] = (h * cdf).astype(BF)
        gh = (da * (cdf + h * (jnp.exp(-0.5 * h * h) * inv_root_tau))).astype(BF)
        gh_ref[rows, :] = gh
        total = jnp.sum(gh.astype(F32), axis=0, keepdims=True)
        gub_ref[...] = total if i == 0 else gub_ref[...] + total
        part = dot(gh, up_ref[...], 1, 1)

        @pl.when(j == 0)
        def _():
            acc[rows, :] = part

        @pl.when(j > 0)
        def _():
            acc[rows, :] += part

    @pl.when(j == last)
    def _():
        for i, out in enumerate((g0, g1)):
            total = acc[i * size : (i + 1) * size, :]
            if n_add:
                total = total + refs[i][...].astype(F32)
            out[...] = total.astype(BF)


def mlp(k, n_hi, n, c, up, upb, down, before):
    rows, width = n[0].shape
    units = up.shape[1]
    tile = min(512, units)
    steps = units // tile
    here = whole_spec((rows, width))
    held = [] if before is None else [before[2], before[3], before[0], before[1]]
    wide = pl.BlockSpec((2 * rows, tile), lambda j: (0, k * steps + j))
    return call(
        functools.partial(mlp_kernel, len(held) // 2),
        [*n, *c, up, upb, down, *held],
        [((2 * rows, n_hi * units), BF)] * 2 + [((rows, width), BF)] * 2 + [((1, units), F32)],
        scratch=[pltpu.VMEM((2 * rows, width), F32)],
        flops=12 * rows * width * units,
        in_specs=[here] * 4
        + [
            pl.BlockSpec((width, tile), lambda j: (0, j)),
            pl.BlockSpec((1, tile), lambda j: (0, j)),
            pl.BlockSpec((tile, width), lambda j: (j, 0)),
        ]
        + ([here] * 2 + [pl.BlockSpec(memory_space=pl.ANY)] * 2 if held else []),
        out_specs=[wide] * 2 + [here] * 2 + [pl.BlockSpec((1, tile), lambda j: (0, j))],
        grid=(steps,),
        input_output_aliases={9: 0, 10: 1} if held else {},
        name="mlp",
    )


def row_product_kernel(n_parts, act_ref, *refs):
    parts, outs = refs[:n_parts], refs[n_parts:]
    size, units = outs[0].shape[0], parts[0].shape[0]
    for i, out in enumerate(outs):
        rows = slice(i * size, (i + 1) * size)
        total = None
        for k, ref in enumerate(parts):
            part = dot(act_ref[rows, k * units : (k + 1) * units], ref[...], 1, 0)
            total = part if total is None else total + part
        out[...] = total.astype(BF)


def row_product(act, parts):
    rows, width = act.shape[0] // 2, parts[0].shape[1]
    return call(
        functools.partial(row_product_kernel, len(parts)),
        [act, *parts],
        [((rows, width), BF)] * 2,
        flops=4 * rows * width * act.shape[1],
        name="row_product",
    )


def wgrad_kernel(n_left, n_right, index_ref, *refs):
    left, right = refs[:n_left], refs[n_left : n_left + n_right]
    out_ref, held, sems = refs[n_left + n_right :]
    size = right[0].shape[0]
    copies = [
        pltpu.make_async_copy(r, held.at[pl.ds(i * size, size)], sems.at[i])
        for i, r in enumerate(right)
    ]

    first = pl.program_id(0) == 0

    @pl.when(first)
    def _():
        for copy in copies:
            copy.start()

    total, at = None, 0
    for ref in left:
        rows = ref.shape[0]

        @pl.when(first)
        def _(at=at, rows=rows):
            for copy in copies[at // size : (at + rows) // size]:
                copy.wait()

        part = dot(ref[...], held[at : at + rows, :], 0, 0)
        total = part if total is None else total + part
        at += rows
    out_ref[...] = total.astype(BF)


def wgrad(left, right, index, tile):
    width = right[0].shape[1]
    total = sum(r.shape[0] for r in right)
    blocks = index.shape[0]
    in_specs = [pl.BlockSpec((x.shape[0], tile), lambda j, at: (0, at[j])) for x in left]
    in_specs += [pl.BlockSpec(memory_space=pl.ANY)] * len(right)
    moved = 2 * (total * (width + blocks * tile) + blocks * tile * width)
    return pl.pallas_call(
        functools.partial(wgrad_kernel, len(left), len(right)),
        grid_spec=pltpu.PrefetchScalarGridSpec(
            num_scalar_prefetch=1,
            grid=(blocks,),
            in_specs=in_specs,
            out_specs=pl.BlockSpec((tile, width), lambda j, at: (j, 0)),
            scratch_shapes=[
                pltpu.VMEM((total, width), BF),
                pltpu.SemaphoreType.DMA((len(right),)),
            ],
        ),
        out_shape=jax.ShapeDtypeStruct((blocks * tile, width), BF),
        compiler_params=pltpu.CompilerParams(vmem_limit_bytes=60 * 2**20),
        cost_estimate=pl.CostEstimate(
            flops=2 * total * blocks * tile * width * HINT,
            bytes_accessed=moved * HINT,
            transcendentals=0,
        ),
        name="wgrad",
    )(index, *left, *right)


def place_kernel(count, transposed, at_ref, *refs):
    pieces, out_ref = refs[:count], refs[count]
    total = sum(ref.shape[0] for ref in pieces)
    size = total // at_ref.shape[0]
    target = refs[count + 1] if transposed else out_ref
    i = 0
    for ref in pieces:
        for start in range(0, ref.shape[0], size):
            rows = pl.ds(pl.multiple_of(at_ref[i] * size, size), size)
            target[rows, :] = ref[start : start + size, :].astype(target.dtype)
            i += 1
    if transposed:
        for at in range(0, total, 256):
            out_ref[:, at : at + 256] = target[at : at + 256, :].astype(F32).T


def place(pieces, at, transposed):
    width = pieces[0].shape[1]
    rows = sum(x.shape[0] for x in pieces)
    shape = (width, rows) if transposed else (rows, width)
    vmem = pl.BlockSpec(memory_space=pltpu.VMEM)
    return call(
        functools.partial(place_kernel, len(pieces), transposed),
        [at, *pieces],
        [(shape, F32)],
        scratch=[pltpu.VMEM((rows, width), BF)] if transposed else [],
        in_specs=[pl.BlockSpec(memory_space=pltpu.SMEM)] + [vmem] * len(pieces),
        name="place",
    )[0]


def attend_wgrad_kernel(n, rows_of, *refs):
    d, heads, first, branch = [refs[i * n : (i + 1) * n] for i in range(4)]
    out_ref, held, sems = refs[4 * n :]
    size, hc = d[0].shape[0], heads[0].shape[1]
    sources = list(first) + list(branch)
    copies = [
        pltpu.make_async_copy(r, held.at[pl.ds(i * size, size)], sems.at[i])
        for i, r in enumerate(sources)
    ]
    for copy in copies:
        copy.start()
    for at, left in ((0, d), (n, heads)):
        total = None
        for i, ref in enumerate(left):
            copies[at + i].wait()
            part = dot(ref[...], held[(at + i) * size : (at + i + 1) * size, :], 0, 0)
            total = part if total is None else total + part
        low = total.astype(BF)
        for i in range(low.shape[0] // hc):
            to = rows_of[i if at == 0 else 3] * hc
            out_ref[to : to + hc, :] = low[i * hc : (i + 1) * hc]


def attend_wgrad(d, heads, first, branch, rows_of):
    size, width = first[0].shape
    hc = heads[0].shape[1]
    vmem = pl.BlockSpec(memory_space=pltpu.VMEM)
    n = len(d)
    return call(
        functools.partial(attend_wgrad_kernel, n, tuple(rows_of)),
        [*d, *heads, *first, *branch],
        [((4 * hc, width), BF)],
        scratch=[pltpu.VMEM((2 * n * size, width), BF), pltpu.SemaphoreType.DMA((2 * n,))],
        flops=8 * n * size * hc * width,
        in_specs=[vmem] * (2 * n) + [pl.BlockSpec(memory_space=pl.ANY)] * (2 * n),
        name="attend_wgrad",
    )[0]


def place_heads_kernel(count, at_ref, *refs):
    pieces, qkv_ref, out_ref, buf = refs[:count], *refs[count:]
    hc = out_ref.shape[0] // 2
    size = buf.shape[0] // at_ref.shape[0]
    i = 0
    for ref in pieces:
        for start in range(0, ref.shape[0], size):
            rows = pl.ds(pl.multiple_of(at_ref[i] * size, size), size)
            buf[rows, :] = ref[start : start + size, :]
            i += 1
    for core in (0, 1):
        for mat in range(4):
            x = buf[(core * 4 + mat) * hc : (core * 4 + mat + 1) * hc, :].astype(F32)
            if mat == 3:
                out_ref[core * hc : (core + 1) * hc, :] = x
            else:
                qkv_ref[mat, core * hc : (core + 1) * hc, :] = x


def place_heads(pieces, at):
    rows, width = sum(x.shape[0] for x in pieces), pieces[0].shape[1]
    hc = rows // 8
    size = rows // at.shape[0]
    if size % 16:
        buf, i = jnp.zeros((rows, width), BF), 0
        for x in pieces:
            for start in range(0, x.shape[0], size):
                buf = lax.dynamic_update_slice_in_dim(buf, x[start : start + size], at[i] * size, 0)
                i += 1
        buf = buf.reshape(2, 4, hc, width).astype(F32)
        mats = [buf[:, i].reshape(2 * hc, width) for i in range(4)]
        return jnp.stack(mats[:3]), mats[3]
    vmem = pl.BlockSpec(memory_space=pltpu.VMEM)
    return call(
        functools.partial(place_heads_kernel, len(pieces)),
        [at, *pieces],
        [((3, 2 * hc, width), F32), ((2 * hc, width), F32)],
        scratch=[pltpu.VMEM((rows, width), BF)],
        in_specs=[pl.BlockSpec(memory_space=pltpu.SMEM)] + [vmem] * len(pieces),
        name="place_heads",
    )


class Order:
    def __init__(self):
        self.last, self.also = None, ()

    def gate(self, x):
        if self.last is None:
            return x
        return lax.optimization_barrier((x, self.last, *self.also))[0]

    def __call__(self, kernel, x, *rest):
        out = kernel(self.gate(x), *rest)
        self.last, self.also = jax.tree.leaves(out)[-1], ()
        return out

    def meet(self, *arrays):
        self.also += arrays


class Layout:
    def __init__(self, dp, tensor):
        self.dp, self.tensor = dp, tensor
        self.n_p, self.n_hi = dp // 2, tensor // 2
        self.bits = [1 << b for b in range(self.n_p.bit_length() - 1)]

    def move(self, x, p=0, c=0, hi=0, lo=0):
        dp_mask, tensor_mask = 2 * p + c, 2 * hi + lo
        pairs = [
            (d * self.tensor + t, (d ^ dp_mask) * self.tensor + (t ^ tensor_mask))
            for d in range(self.dp)
            for t in range(self.tensor)
        ]
        return lax.ppermute(x, ("dp", "tensor"), pairs)

    def place_of(self, p, order):
        n = len(order)
        place = 0
        for i, bit in enumerate(order):
            place = place + (p // bit) % 2 * (1 << (n - 1 - i))
        return place

    def spread_masks(self, order):
        masks = [0]
        for bit in order:
            masks += [m ^ bit for m in masks]
        return masks

    def spread_direct(self, block):
        return {m: self.move(block, p=m) if m else block for m in range(self.n_p)}


def on_device(
    lay,
    images,
    first_gain,
    first_shift,
    qkv_weight,
    qv_bias,
    out_weight,
    out_bias,
    second_gain,
    second_shift,
    up_weight,
    up_bias,
    down_weight,
    down_bias,
    cotangent,
):
    n_p, n_hi = lay.n_p, lay.n_hi
    n_i, seq, width = images.shape
    columns = qkv_weight.shape[2]
    units = up_weight.shape[1]
    hc, hu = columns // 2, units // 2
    dp = lax.axis_index("dp")
    p, c = dp // 2, dp % 2
    up_order, down_order = lay.bits, lay.bits[::-1]
    order = Order()
    first_gain, first_shift, out_bias, second_gain, second_shift, down_bias = [
        v.reshape(1, width)
        for v in (first_gain, first_shift, out_bias, second_gain, second_shift, down_bias)
    ]

    def half(x, axis):
        n = x.shape[axis] // 2
        return lax.dynamic_slice_in_dim(x, c * n, n, axis)

    def block(x, axis, at):
        n = x.shape[axis] // n_p
        return lax.dynamic_slice_in_dim(x, at * n, n, axis)

    def put(buf, x, axis, at):
        return lax.dynamic_update_slice_in_dim(buf, x, at, axis)

    x_unit, first_own = order(pack, images, first_gain, first_shift, True)
    first_c, first_z = lay.move(first_own, c=1), lay.move(first_own, lo=1)
    head_rows = jnp.swapaxes(qkv_weight, 1, 2)

    def weights_here(x):
        return jnp.concatenate([half(x[i], 0) for i in range(3)] + [half(out_weight, 0)])

    if n_p == 4:

        def cut_of(x):
            mat = lax.dynamic_index_in_dim(x, jnp.minimum(p, 2), 0, keepdims=False)
            return jnp.where(p == 3, half(out_weight, 0), half(mat, 0))

        work_cut = order(cut_of, head_rows)
    else:
        work_cut = block(weights_here(head_rows), 0, p)
    work_hi = [lay.move(work_cut, hi=k) for k in range(1, n_hi)]
    qv_half, upb_half = half(qv_bias, 1), half(up_bias, 0)
    bias_all = [jnp.concatenate([qv_half.reshape(-1), upb_half])]
    work_mine = order(weights_here, head_rows)
    work = [work_mine]
    forward = [[None] * 4 for _ in range(n_hi)]

    def qkv_bias_of(b):
        return jnp.concatenate([b[:hc], jnp.zeros((hc,), F32), b[hc : 2 * hc]]).reshape(1, -1)

    qkv_bias = [qkv_bias_of(bias_all[0])]

    def attention(k, u, n, adds=()):
        adds = list(adds) + ([forward[k - 1][u][4]] if k else [])
        forward[k][u] = order(lambda x: attend_fwd(n_i, x, work[k], qkv_bias[k], adds), n)
        return forward[k][u][4]

    def stage(held, axis, bit):
        return jnp.concatenate([held, lay.move(held, p=bit)], axis)

    attention(0, 0, first_own)
    bias_hi = [lay.move(order.gate(bias_all[0]), hi=k) for k in range(1, n_hi)]
    attention(0, 1, first_c)
    seed_unit, grad_down_bias = order(pack, cotangent, first_gain, first_shift, False)
    seed_c = lay.move(seed_unit, c=1)
    order.meet(*work_hi)
    work_got = [lay.spread_direct(order.gate(x)) for x in work_hi]
    first_zc = lay.move(order.gate(first_z), c=1)
    attention(0, 2, first_z)
    seed_z = lay.move(seed_unit, lo=1)
    attention(0, 3, first_zc)
    up_cut = order(lambda x: block(half(x, 1), 1, p), up_weight)
    up_hi = [lay.move(up_cut, hi=k) for k in range(1, n_hi)]
    down_cut = order(lambda x: block(half(x, 0), 0, p), down_weight)
    down_hi = [lay.move(down_cut, hi=k) for k in range(1, n_hi)]

    def assemble(got):
        masks = sorted(got)

        def run(x):
            full = jnp.zeros_like(work_mine)
            for mask in masks:
                x = x if mask == 0 else got[mask]
                full = put(full, x, 0, (p ^ mask) * x.shape[0])
            return full

        return order(run, got[0])

    work += [assemble(got) for got in work_got]
    bias_all += [order.gate(x) for x in bias_hi]
    qkv_bias += [qkv_bias_of(b) for b in bias_all[1:]]
    normed = (first_own, first_c, first_z, first_zc)
    for k in range(1, n_hi - 1):
        for u in range(4):
            attention(k, u, normed[u])
    k = n_hi - 1

    def widen(pairs, axis):
        return [order(lambda x, y=y: jnp.concatenate([x, y], axis), x) for x, y in pairs]

    moved_3 = lay.move(attention(k, 3, first_zc), c=1)
    order.meet(seed_c)
    moved_1 = lay.move(attention(k, 1, first_c), c=1)
    moved_2 = lay.move(attention(k, 2, first_z, [moved_3]), lo=1)
    order.meet(moved_1, seed_z, *up_hi)
    seed_zc = lay.move(order.gate(seed_z), c=1)
    up_got = [order.gate(x) for x in up_hi]
    up_got = [(x, lay.move(x, p=up_order[0])) for x in up_got]
    down_got = [order.gate(x) for x in down_hi]
    down_got = [(x, lay.move(x, p=down_order[0])) for x in down_got]
    attention_parts = (attention(k, 0, first_own), moved_1, moved_2)
    normed_first = list(normed)
    up_work = [order(lambda x: half(x, 1), up_weight)]
    down_work = [order(lambda x: half(x, 0), down_weight)]
    for i in range(1, len(lay.bits)):
        up_got = [(x, lay.move(x, p=up_order[i])) for x in widen(up_got, 1)]
        down_got = [(x, lay.move(x, p=down_order[i])) for x in widen(down_got, 0)]
    order.meet(seed_zc)
    seed = [seed_unit, seed_c, seed_z, seed_zc]

    middle, second_own = order(
        lambda x: norm_second(x, attention_parts, out_bias, second_gain, second_shift), x_unit
    )
    second_c, second_z = lay.move(second_own, c=1), lay.move(second_own, lo=1)

    def fill(parts, axis, order_of):
        size = parts[0].shape[axis] * 2 // n_p
        shape = [width, width]
        shape[axis] = hu
        masks = lay.spread_masks(order_of)

        def run(x):
            full, at = jnp.zeros(shape, BF), 0
            for part in (x, *parts[1:]):
                for i in range(part.shape[axis] // size):
                    piece = lax.slice_in_dim(part, i * size, (i + 1) * size, axis=axis)
                    full = put(full, piece, axis, (p ^ masks[at]) * size)
                    at += 1
            return full

        return order(run, parts[0])

    up_half = [upb_half.reshape(1, -1)] + [b[2 * hc :].reshape(1, -1) for b in bias_all[1:]]

    def mlp_half(k, first, second, seeds, before):
        return order(
            lambda x: mlp(k, n_hi, [x, second], seeds, up_work[k], up_half[k], down_work[k], before),
            first,
        )

    near = mlp_half(0, second_own, second_c, seed[:2], None)
    up_work += [fill(parts, 1, up_order) for parts in up_got]
    down_work += [fill(parts, 0, down_order) for parts in down_got]
    near_bias, far_bias = [near[4]], []
    for k in range(1, n_hi):
        near = mlp_half(k, second_own, second_c, seed[:2], near)
        near_bias.append(near[4])
    second_zc = lay.move(order.gate(second_z), c=1)
    other_c = lay.move(near[3], c=1)
    low_near = order(lambda x: row_product(x, down_work), near[0])
    low_near_c = lay.move(low_near[1], c=1)
    far = None
    for k in range(n_hi):
        far = mlp_half(k, second_z, second_zc, seed[2:], far)
        far_bias.append(far[4])
    normed_second = [second_own, second_c, second_z, second_zc]

    def index(order_of, other):
        top = lay.place_of(p, order_of) // (n_p // 2)
        return jnp.stack([2 * k + (top ^ other) for k in range(n_hi)]).astype(jnp.int32)

    def mlp_grad(which, right, order_of, other):
        return order(
            lambda x: wgrad([x, far[which]], right, index(order_of, other), hu // 2), near[which]
        )

    far_c = lay.move(far[3], c=1)
    down_send = mlp_grad(0, seed, down_order, 1)
    down_recv = lay.move(down_send, p=down_order[0])

    def join(*parts):
        total = parts[0].astype(F32)
        for x in parts[1:]:
            total = total + x.astype(F32)
        return total.astype(BF)

    far_sum = order(lambda x: join(x, far_c), far[2])
    grad_second = (near[2], other_c, lay.move(far_sum, lo=1))
    up_send = mlp_grad(1, normed_second, up_order, 1)
    up_recv = lay.move(up_send, p=up_order[0])
    down_keep = mlp_grad(0, seed, down_order, 0)
    grad_middle, grad_branch, grad_second_gain, grad_second_shift, grad_out_bias = order(
        lambda x: norm_back(x, grad_second, seed_unit, second_gain, True), middle
    )
    branch_c, branch_z = lay.move(grad_branch, c=1), lay.move(grad_branch, lo=1)
    low_far = order(lambda x: row_product(x, down_work), far[0])
    low_far_c = lay.move(low_far[1], c=1)
    up_keep = mlp_grad(1, normed_second, up_order, 0)

    def halve(keep, recv, order_of, stage, parts):
        bit = order_of[stage]
        side = (p // bit) % 2
        shape = (parts, 2, keep.shape[0] // (2 * parts), width)

        def pick(x, s):
            x = lax.dynamic_index_in_dim(x.reshape(shape), s, 1, keepdims=False)
            return x.reshape(-1, width)

        send = order(lambda x: join(pick(x, 1 - side), pick(recv, 1 - side)), keep)
        keep = join(pick(keep, side), pick(recv, side))
        return keep, lay.move(send, p=bit)

    def settle_hi(keep, recv):
        size = keep.shape[0] // n_hi
        total = order(lambda x: join(x, recv), keep)
        got = [lay.move(total[k * size : (k + 1) * size], hi=k) for k in range(1, n_hi)]
        return total[:size], got

    class Spread:
        def __init__(self, mine, order_of):
            self.pieces, self.order_of, self.bits = [mine], order_of, order_of[::-1]
            self.got, self.at = lay.move(mine, p=self.bits[0]), 1

        def step(self):
            self.pieces.append(self.got)
            held = order(lambda x: jnp.concatenate([x] + self.pieces[1:]), self.pieces[0])
            if self.at < len(self.bits):
                self.got = lay.move(held, p=self.bits[self.at])
            else:
                self.pieces = [held, lay.move(held, c=1)]
            self.at += 1

        def finish(self):
            while self.at <= len(self.bits):
                self.step()
            masks = lay.spread_masks(self.bits)
            places = [lay.place_of(p ^ mask, self.order_of) for mask in masks]
            at = [c * n_p + x for x in places] + [(1 - c) * n_p + x for x in places]
            return self.pieces, jnp.stack(at).astype(jnp.int32)

    backward = [[None] * 4 for _ in range(n_hi)]
    branch = [grad_branch, branch_c, branch_z, None]

    def attention_back(k, u, adds=()):
        adds = list(adds) + ([backward[k + 1][u][2]] if k < n_hi - 1 else [])
        f = forward[k][u]
        backward[k][u] = order(
            lambda g: attend_bwd(n_i, g, (f[0], f[2], f[3], work[k]), adds),
            branch[u],
        )
        return backward[k][u][2]

    def attention_send(k, order_of):
        owner = [0] * n_p
        for q in range(n_p):
            owner[lay.place_of(q, order_of)] = lay.place_of(q, orders[0])
        grad = order(
            lambda x: attend_wgrad(
                [x] + [b[0] for b in backward[k][1:]],
                [f[1] for f in forward[k]],
                normed_first,
                branch,
                owner if n_p == 4 else range(4),
            ),
            backward[k][0][0],
        )
        if n_p != 4:
            blocks = jnp.split(grad, n_p)
            grad = jnp.concatenate([blocks[i] for i in owner])
        top = lay.place_of(p, order_of) // (n_p // 2)
        size = grad.shape[0] // 2
        send = order(lambda x: lax.dynamic_slice_in_dim(x, (1 - top) * size, size, 0), grad)
        keep = lax.dynamic_slice_in_dim(grad, top * size, size, 0)
        return keep, lay.move(send, p=order_of[0])

    down_pair, up_pair = (down_keep, down_recv), (up_keep, up_recv)
    attn_pairs = [None] * n_hi
    orders = [up_order] + [down_order] * (n_hi - 1)
    n_stage = len(lay.bits)
    k = n_hi - 1
    down_pair = halve(*down_pair, down_order, 1, n_hi)
    attention_back(k, 0)
    branch[3] = lay.move(order.gate(branch_z), c=1)
    attention_back(k, 1)
    up_pair = halve(*up_pair, up_order, 1, n_hi)
    low_far_sum = order(lambda x: join(x, low_far_c), low_far[0])
    low_far_z = lay.move(low_far_sum, lo=1)
    attention_back(k, 2)
    for step in range(2, n_stage):
        down_pair = halve(*down_pair, down_order, step, n_hi)
        up_pair = halve(*up_pair, up_order, step, n_hi)
    down_mine, down_hi_got = settle_hi(*down_pair)
    attention_back(k, 3)
    attn_pairs[k] = attention_send(k, orders[k])
    up_mine, up_hi_got = settle_hi(*up_pair)
    result_parts = (low_near[0], low_near_c, low_far_z)
    result = order(lambda x: unpack(n_i, seq, x, result_parts, down_bias), middle)
    for k in range(n_hi - 2, 0, -1):
        for u in range(4):
            attention_back(k, u)
        attn_pairs[k] = attention_send(k, orders[k])
    moved_3 = lay.move(attention_back(0, 3), c=1)
    down_mine = order(lambda x: join(x, *down_hi_got), down_mine)
    down_all = Spread(down_mine, down_order)
    moved_1 = lay.move(attention_back(0, 1), c=1)
    down_all.step()
    moved_2 = lay.move(attention_back(0, 2, [moved_3]), lo=1)
    for k in range(1, n_hi):
        for step in range(1, n_stage):
            attn_pairs[k] = halve(*attn_pairs[k], orders[k], step, 1)
    up_mine = order(lambda x: join(x, *up_hi_got), up_mine)
    up_all = Spread(up_mine, up_order)
    order.meet(moved_1)
    grad_first = (attention_back(0, 0), moved_1, moved_2)
    up_all.step()
    attn_hi = []
    for k in range(1, n_hi):
        total = order(lambda x, k=k: join(x, attn_pairs[k][1]), attn_pairs[k][0])
        attn_hi.append(lay.move(total, hi=k))
    down_all = down_all.finish()
    grad = order(
        lambda x: attend_wgrad(
            [x] + [b[0] for b in backward[0][1:]],
            [f[1] for f in forward[0]],
            normed_first,
            branch,
            range(4),
        ),
        backward[0][0][0],
    )
    places = [lay.place_of(p ^ mask, orders[0]) for mask in range(n_p)]
    attn_own = block(grad, 0, places[0])
    attn_got = []
    for mask in range(1, n_p):
        out = order(lambda x, mask=mask: block(x, 0, places[mask]), grad)
        attn_got.append(lay.move(out, p=mask))

    def place_all(blocks, at, transposed):
        return order(lambda x: place([x] + blocks[1:], at, transposed), blocks[0])

    grad_down_weight = place_all(*down_all, False)
    _, grad_images, grad_first_gain, grad_first_shift, _ = order(
        lambda x: norm_back(x, grad_first, grad_middle, first_gain, False), x_unit
    )
    attn_mine = order(lambda x: join(x, *attn_got, *attn_hi), attn_own)
    attn_all = lay.spread_direct(attn_mine)

    tensor_at = lax.axis_index("tensor")
    all_units, all_columns = units * lay.tensor, columns * lay.tensor
    grad_up_bias = jnp.concatenate([(a + b)[0] for a, b in zip(near_bias, far_bias)])
    wide_up = jnp.zeros((all_units,), F32)
    wide_qv = jnp.zeros((2, all_columns), F32)
    for k in range(n_hi):
        shard = tensor_at ^ (2 * k)
        wide_up = put(wide_up, grad_up_bias[k * hu : (k + 1) * hu], 0, shard * units + c * hu)
        bias = sum(b[1] for b in backward[k])[0]
        bias = jnp.stack([bias[:hc], bias[2 * hc :]])
        wide_qv = put(wide_qv, bias, 1, shard * columns + c * hc)
    sums = (
        grad_first_gain,
        grad_first_shift,
        grad_out_bias,
        grad_second_gain,
        grad_second_shift,
        grad_down_bias,
    )
    vector = jnp.concatenate(
        [jnp.sum(x, axis=0) for x in sums] + [wide_up, wide_qv.reshape(-1)]
    )
    hops = [dict(c=1)] + [
        dict(lo=(1 << b) & 1, hi=(1 << b) >> 1) for b in range(lay.tensor.bit_length() - 1)
    ]
    hops += [dict(p=bit) for bit in lay.bits]

    def hop(vector):
        got = lay.move(vector, **hops.pop(0))
        return vector, got

    def add(pair):
        return order(lambda x: x + pair[1], pair[0])

    pair = hop(vector)
    grad_images = order(lambda x: unpack(n_i, seq, x), grad_images)
    pair = hop(add(pair))
    for _ in range(lay.tensor.bit_length() - 2):
        pair = hop(add(pair))
    up_all = up_all.finish()
    pair = hop(add(pair))
    grad_up_weight = place_all(*up_all, True)
    masks = sorted(attn_all)
    held = order(
        lambda x: jnp.concatenate([x] + [attn_all[mask] for mask in masks[1:]]), attn_all[0]
    )
    held_c = lay.move(held, c=1)
    at = [lay.place_of(p ^ mask, orders[0]) for mask in masks]
    at = [c * n_p + x for x in at] + [(1 - c) * n_p + x for x in at]
    attn_all = ([held, held_c], jnp.stack(at).astype(jnp.int32))
    while hops:
        pair = hop(add(pair))
    vector = add(pair)
    norms = vector[: 6 * width].reshape(6, width)
    vector = vector[6 * width :]
    grad_up_bias = lax.dynamic_slice_in_dim(vector, tensor_at * units, units, 0)
    grad_qv_bias = lax.dynamic_slice_in_dim(
        vector[all_units:].reshape(2, all_columns), tensor_at * columns, columns, 1
    )

    grad_qkv_weight, grad_out_weight = place_heads(*attn_all)
    grad_qkv_weight = jnp.swapaxes(grad_qkv_weight, 1, 2)
    return (
        result,
        grad_images,
        norms[0],
        norms[1],
        grad_qkv_weight,
        grad_qv_bias,
        grad_out_weight,
        norms[2],
        norms[3],
        norms[4],
        grad_up_weight,
        grad_up_bias,
        grad_down_weight,
        norms[5],
    )


def solution(mesh):
    lay = Layout(mesh.shape["dp"], mesh.shape["tensor"])
    rows = P(("dp", "tensor"), None, None)
    qkv, qv = P(None, None, "tensor"), P(None, "tensor")
    line, up, down, rep = P("tensor"), P(None, "tensor"), P("tensor", None), P()
    return jax.shard_map(
        functools.partial(on_device, lay),
        mesh=mesh,
        in_specs=(rows, rep, rep, qkv, qv, down, rep, rep, rep, up, line, down, rep, rows),
        out_specs=(rows, rows, rep, rep, qkv, qv, down, rep, rep, rep, up, line, down, rep),
        check_vma=False,
    )
```

```python
import functools

import jax
import jax.numpy as jnp
from jax import lax
from jax.experimental import pallas as pl
from jax.experimental.pallas import tpu as pltpu
from jax.sharding import PartitionSpec as P

HD = 104
PAD = 16
BF = jnp.bfloat16
F32 = jnp.float32


def dot(a, b, ca, cb):
    return lax.dot_general(a, b, (((ca,), (cb,)), ((), ())), preferred_element_type=F32)


def whole_spec(shape):
    return pl.BlockSpec(shape, lambda *_: (0,) * len(shape), pipeline_mode=pl.Buffered(1))


def head_mask(heads):
    lane = lax.broadcasted_iota(jnp.int32, (8, heads * HD), 1)
    row = lax.broadcasted_iota(jnp.int32, (8, heads * HD), 0)
    return (lane >= row * HD) & (lane < row * HD + HD)


def attend_fwd_kernel(n_i, main, heads, n_add, n_ref, w_ref, b_ref, *refs):
    adds = refs[:n_add]
    qkv_ref, ho_ref, lse_ref, lset_ref, out_ref = refs[n_add:]
    hc = heads * HD
    tail = pl.ds(n_i * main, PAD)
    qkv_ref[...] = (dot(n_ref[...], w_ref[0 : 3 * hc, :], 1, 1) + b_ref[...]).astype(BF)
    ho_ref[tail, :] = jnp.zeros((PAD, hc), BF)
    factor = HD ** -0.5
    tail_row = lax.broadcasted_iota(jnp.int32, (PAD, 1), 0)
    per_head = head_mask(heads)

    def image(i, carry):
        rows = pl.ds(pl.multiple_of(i * main, main), main)
        here = tail_row == i
        bar = jnp.where(here, 0.0, -1e30)
        bar_all = jnp.concatenate([jnp.zeros((main, 1), F32), bar], 0)

        def both(cols):
            return jnp.concatenate([qkv_ref[rows, cols], qkv_ref[tail, cols]], 0)

        q_t = jnp.sum(jnp.where(here, qkv_ref[tail, 0:hc].astype(F32), 0.0), 0, keepdims=True)
        q_b = jnp.where(per_head, q_t, 0.0).astype(BF)
        s = dot(both(slice(hc, 2 * hc)), q_b, 1, 1) * factor + bar_all
        top = jnp.max(s, 0, keepdims=True)
        e = jnp.exp(s - top)
        total = jnp.sum(e, 0, keepdims=True)
        o = dot((e * (1.0 / total)).astype(BF), both(slice(2 * hc, 3 * hc)), 0, 0)
        o = jnp.sum(jnp.where(per_head, o, 0.0), 0, keepdims=True).astype(BF)
        ho_ref[tail, :] = jnp.where(here, o, ho_ref[tail, :])
        lset_ref[pl.ds(i, 1), 0:8] = top + jnp.log(total)
        for h in range(heads):
            cols = [slice(t * hc + h * HD, t * hc + (h + 1) * HD) for t in range(3)]
            q = qkv_ref[rows, cols[0]]
            s = dot(qkv_ref[rows, cols[1]], q, 1, 1) * factor
            s_t = dot(qkv_ref[tail, cols[1]], q, 1, 1) * factor + bar
            top = jnp.maximum(jnp.max(s, 0, keepdims=True), jnp.max(s_t, 0, keepdims=True))
            e, e_t = jnp.exp(s - top), jnp.exp(s_t - top)
            total = jnp.sum(e, 0, keepdims=True) + jnp.sum(e_t, 0, keepdims=True)
            inv = 1.0 / total
            o = dot((e * inv).astype(BF), qkv_ref[rows, cols[2]], 0, 0)
            o = o + dot((e_t * inv).astype(BF), qkv_ref[tail, cols[2]], 0, 0)
            ho_ref[rows, h * HD : (h + 1) * HD] = o.astype(BF)
            lse_ref[h : h + 1, rows] = top + jnp.log(total)
        return carry

    lax.fori_loop(0, n_i, image, 0)
    total = dot(ho_ref[...], w_ref[3 * hc :, :], 1, 0)
    for ref in adds:
        total = total + ref[...].astype(F32)
    out_ref[...] = total.astype(BF)


def attend_fwd(n_i, n, w, b, adds=()):
    rows, width = n.shape
    hc = w.shape[0] // 4
    main = (rows - PAD) // n_i
    shapes = (
        ((rows, 3 * hc), BF),
        ((rows, hc), BF),
        ((8, n_i * main), F32),
        ((8, 128), F32),
        ((rows, width), BF),
    )
    flops = 2 * rows * width * 4 * hc + 4 * n_i * main * main * hc
    return call(
        functools.partial(attend_fwd_kernel, n_i, main, hc // HD, len(adds)),
        [n, w, b, *adds],
        shapes,
        flops=flops,
        name="attend_fwd",
    )


def attend_bwd_kernel(n_i, main, heads, n_add, g_ref, qkv_ref, lse_ref, lset_ref, w_ref, *refs):
    adds = refs[:n_add]
    d_ref, gb_ref, gn_ref, gh_ref, kv_ref = refs[n_add:]
    hc = heads * HD
    tail = pl.ds(n_i * main, PAD)
    gh_ref[...] = dot(g_ref[...], w_ref[3 * hc :, :], 1, 1).astype(BF)
    d_ref[tail, :] = jnp.zeros((PAD, 3 * hc), BF)
    factor = HD ** -0.5
    tail_row = lax.broadcasted_iota(jnp.int32, (PAD, 1), 0)
    per_head = head_mask(heads)

    def image(i, carry):
        rows = pl.ds(pl.multiple_of(i * main, main), main)
        here = tail_row == i
        bar = jnp.where(here, 0.0, -1e30)
        bar_all = jnp.concatenate([jnp.zeros((main, 1), F32), bar], 0)

        def both(cols):
            return jnp.concatenate([qkv_ref[rows, cols], qkv_ref[tail, cols]], 0)

        def last(ref, cols):
            row = jnp.sum(jnp.where(here, ref[tail, cols].astype(F32), 0.0), 0, keepdims=True)
            return jnp.where(per_head, row, 0.0).astype(BF)

        q_b, go_b = last(qkv_ref, slice(0, hc)), last(gh_ref, slice(0, hc))
        k_all, v_all = both(slice(hc, 2 * hc)), both(slice(2 * hc, 3 * hc))
        p = jnp.exp(dot(k_all, q_b, 1, 1) * factor + bar_all - lset_ref[pl.ds(i, 1), 0:8])
        dp = dot(v_all, go_b, 1, 1)
        ds = (p * (dp - jnp.sum(p * dp, 0, keepdims=True))).astype(BF)
        dq = dot(ds, k_all, 0, 0) * factor
        dq = jnp.sum(jnp.where(per_head, dq, 0.0), 0, keepdims=True).astype(BF)
        d_ref[tail, 0:hc] = jnp.where(here, dq, d_ref[tail, 0:hc])
        kv_ref[:, 0:hc] = dot(ds, q_b, 1, 0)
        kv_ref[:, hc : 2 * hc] = dot(p.astype(BF), go_b, 1, 0)
        for h in range(heads):
            head = slice(h * HD, (h + 1) * HD)
            cols = [slice(t * hc + h * HD, t * hc + (h + 1) * HD) for t in range(3)]
            q, go = qkv_ref[rows, cols[0]], gh_ref[rows, head]
            k, k_t = qkv_ref[rows, cols[1]], qkv_ref[tail, cols[1]]
            v, v_t = qkv_ref[rows, cols[2]], qkv_ref[tail, cols[2]]
            lse = lse_ref[h : h + 1, rows]
            p = jnp.exp(dot(k, q, 1, 1) * factor - lse)
            p_t = jnp.exp(dot(k_t, q, 1, 1) * factor + bar - lse)
            dp, dp_t = dot(v, go, 1, 1), dot(v_t, go, 1, 1)
            inner = jnp.sum(p * dp, 0, keepdims=True) + jnp.sum(p_t * dp_t, 0, keepdims=True)
            ds = (p * (dp - inner)).astype(BF)
            ds_t = (p_t * (dp_t - inner)).astype(BF)
            d_ref[rows, cols[0]] = ((dot(ds, k, 0, 0) + dot(ds_t, k_t, 0, 0)) * factor).astype(BF)
            dk = ((dot(ds, q, 1, 0) + kv_ref[0:main, head]) * factor).astype(BF)
            dk_t = ((dot(ds_t, q, 1, 0) + kv_ref[main:, head]) * factor).astype(BF)
            head_v = slice(hc + h * HD, hc + (h + 1) * HD)
            dv = (dot(p.astype(BF), go, 1, 0) + kv_ref[0:main, head_v]).astype(BF)
            dv_t = (dot(p_t.astype(BF), go, 1, 0) + kv_ref[main:, head_v]).astype(BF)
            d_ref[rows, cols[1]] = dk
            d_ref[rows, cols[2]] = dv
            d_ref[tail, cols[1]] = jnp.where(here, dk_t, d_ref[tail, cols[1]])
            d_ref[tail, cols[2]] = jnp.where(here, dv_t, d_ref[tail, cols[2]])
        return carry

    lax.fori_loop(0, n_i, image, 0)
    gb_ref[...] = jnp.sum(d_ref[...].astype(F32), 0, keepdims=True)
    total = dot(d_ref[...], w_ref[0 : 3 * hc, :], 1, 0)
    for ref in adds:
        total = total + ref[...].astype(F32)
    gn_ref[...] = total.astype(BF)


def attend_bwd(n_i, g, half, adds=()):
    rows, width = g.shape
    hc = half[3].shape[0] // 4
    main = (rows - PAD) // n_i
    shapes = [((rows, 3 * hc), BF), ((1, 3 * hc), F32), ((rows, width), BF)]
    return call(
        functools.partial(attend_bwd_kernel, n_i, main, hc // HD, len(adds)),
        [g, *half, *adds],
        shapes,
        scratch=[pltpu.VMEM((rows, hc), BF), pltpu.VMEM((main + PAD, 2 * hc), F32)],
        flops=2 * rows * width * 4 * hc + 10 * n_i * main * main * hc,
        name="attend_bwd",
    )


epsilon = 1e-06
inv_root_two = 0.7071067811865476
inv_root_tau = 0.3989422804014327
HINT = 30
def step_of(rows):
    return next(s for s in (48, 64, 32, 16) if rows % s == 0)


def call(kernel, ins, outs, scratch=(), flops=0, name=None, in_specs=None, **grid):
    moved = sum(x.size * x.dtype.itemsize for x in ins)
    moved += sum(int(jnp.dtype(d).itemsize) * functools.reduce(lambda a, b: a * b, s) for s, d in outs)
    vmem = pl.BlockSpec(memory_space=pltpu.VMEM)
    return pl.pallas_call(
        kernel,
        in_specs=in_specs or [vmem] * len(ins),
        out_specs=grid.pop("out_specs", [vmem] * len(outs)),
        out_shape=[jax.ShapeDtypeStruct(*s) for s in outs],
        scratch_shapes=list(scratch),
        compiler_params=pltpu.CompilerParams(vmem_limit_bytes=60 * 2**20),
        cost_estimate=pl.CostEstimate(
            flops=int(flops) * HINT, bytes_accessed=int(moved) * HINT, transcendentals=0
        ),
        name=name,
        **grid,
    )(*ins)


def mean_parts(rows):
    centred = rows - jnp.mean(rows, axis=1, keepdims=True)
    spread = jnp.mean(centred * centred, axis=1, keepdims=True)
    inverse = lax.rsqrt(spread + epsilon)
    return centred * inverse, inverse


def fold(x):
    total = x[0:8]
    for at in range(8, x.shape[0], 8):
        total = total + x[at : at + 8]
    return total


def pack_kernel(n_i, main, norm, img_ref, gain_ref, shift_ref, x_ref, other_ref):
    width = x_ref.shape[1]

    def emit(at, x, count):
        x_ref[pl.ds(at, count), :] = x
        if norm:
            unit, _ = mean_parts(x.astype(F32))
            other_ref[pl.ds(at, count), :] = (unit * gain_ref[...] + shift_ref[...]).astype(BF)

    size = step_of(main)
    if not norm:
        other_ref[...] = jnp.zeros(other_ref.shape, F32)
    tail_row = lax.broadcasted_iota(jnp.int32, (PAD, 1), 0)
    tails = jnp.zeros((PAD, width), F32)
    for i in range(n_i):

        def step(r, carry, i=i):
            at = pl.multiple_of(r * size, size)
            x = img_ref[i, pl.ds(at, size), :]
            emit(pl.multiple_of(i * main + r * size, size), x, size)
            if not norm:
                other_ref[...] += fold(x.astype(F32))
            return carry

        lax.fori_loop(0, main // size, step, 0)
        tails = jnp.where(tail_row == i, img_ref[i, main : main + 1, :].astype(F32), tails)
    emit(n_i * main, tails.astype(BF), PAD)
    if not norm:
        other_ref[...] += fold(tails)


def pack(img, gain, shift, norm):
    n_i, seq, width = img.shape
    rows = n_i * (seq - 1) + PAD
    other = ((rows, width), BF) if norm else ((8, width), F32)
    return call(
        functools.partial(pack_kernel, n_i, seq - 1, norm),
        [img, gain, shift],
        [((rows, width), BF), other],
        name="pack",
    )


def loop_rows(rows, step):
    size = step_of(rows)

    def one(r, carry):
        step(pl.ds(pl.multiple_of(r * size, size), size))
        return carry

    lax.fori_loop(0, rows // size, one, 0)


def norm_kernel(x_ref, a_ref, b_ref, c_ref, bias_ref, gain_ref, shift_ref, mid_ref, n_ref):
    def step(at):
        moved = a_ref[at, :].astype(F32) + b_ref[at, :].astype(F32) + c_ref[at, :].astype(F32)
        middle = x_ref[at, :].astype(F32) + (moved + bias_ref[...])
        mid_ref[at, :] = middle
        unit, _ = mean_parts(middle)
        n_ref[at, :] = (unit * gain_ref[...] + shift_ref[...]).astype(BF)

    loop_rows(x_ref.shape[0], step)


def norm_second(x, parts, bias, gain, shift):
    return call(
        norm_kernel,
        [x, *parts, bias, gain, shift],
        [(x.shape, F32), (x.shape, BF)],
        name="norm_second",
    )


def norm_back_kernel(res_f32, x_ref, a_ref, b_ref, c_ref, add_ref, gain_ref, *outs):
    out_ref, low_ref, gain_out, shift_out, bias_out = outs
    for ref in (gain_out, shift_out, bias_out):
        ref[...] = jnp.zeros(ref.shape, F32)

    def step(at):
        grad = a_ref[at, :].astype(F32) + b_ref[at, :].astype(F32) + c_ref[at, :].astype(F32)
        unit, inverse = mean_parts(x_ref[at, :].astype(F32))
        scaled = grad * gain_ref[...]
        first = jnp.mean(scaled, axis=1, keepdims=True)
        second = jnp.mean(scaled * unit, axis=1, keepdims=True)
        total = add_ref[at, :].astype(F32) + inverse * (scaled - first - unit * second)
        low = total.astype(BF)
        low_ref[at, :] = low
        if res_f32:
            out_ref[at, :] = total
            bias_out[...] += fold(low.astype(F32))
        gain_out[...] += fold(grad * unit)
        shift_out[...] += fold(grad)

    loop_rows(x_ref.shape[0], step)


def norm_back(x, parts, add, gain, keep):
    rows, width = x.shape
    full = (x.shape, F32) if keep else ((8, width), F32)
    return call(
        functools.partial(norm_back_kernel, keep),
        [x, *parts, add, gain],
        [full, (x.shape, BF)] + [((8, width), F32)] * 3,
        name="norm_back",
    )


def unpack_kernel(n_i, main, sum_parts, *refs):
    size = step_of(main)
    if sum_parts:
        mid_ref, a_ref, b_ref, c_ref, bias_ref, out_ref = refs
    else:
        mid_ref, out_ref = refs

    def value(at):
        x = mid_ref[at, :]
        if sum_parts:
            moved = a_ref[at, :].astype(F32) + b_ref[at, :].astype(F32) + c_ref[at, :].astype(F32)
            x = (x.astype(F32) + moved + bias_ref[...]).astype(BF)
        return x

    for i in range(n_i):

        def step(r, carry, i=i):
            at = pl.multiple_of(i * main + r * size, size)
            out_ref[i, pl.ds(pl.multiple_of(r * size, size), size), :] = value(pl.ds(at, size))
            return carry

        lax.fori_loop(0, main // size, step, 0)
    tails = value(pl.ds(n_i * main, PAD)).astype(F32)
    for i in range(n_i):
        out_ref[i, main : main + 1, :] = tails[i : i + 1].astype(BF)


def unpack(n_i, seq, first, parts=(), bias=None):
    width = first.shape[1]
    ins = [first, *parts] + ([bias] if parts else [])
    return call(
        functools.partial(unpack_kernel, n_i, seq - 1, bool(parts)),
        ins,
        [((n_i, seq, width), BF)],
        name="unpack",
    )[0]


def mlp_kernel(n_add, n0, n1, c0, c1, up_ref, upb_ref, down_ref, *refs):
    act_ref, gh_ref, g0, g1, gub_ref, acc = refs[2 * n_add :]
    j, last = pl.program_id(0), pl.num_programs(0) - 1
    size = n0.shape[0]
    for i, (n_ref, c_ref) in enumerate(((n0, c0), (n1, c1))):
        rows = slice(i * size, (i + 1) * size)
        h = dot(n_ref[...], up_ref[...], 1, 0) + upb_ref[...]
        da = dot(c_ref[...], down_ref[...], 1, 1)
        cdf = 0.5 * (1.0 + lax.erf(h * inv_root_two))
        act_ref[rows, :] = (h * cdf).astype(BF)
        gh = (da * (cdf + h * (jnp.exp(-0.5 * h * h) * inv_root_tau))).astype(BF)
        gh_ref[rows, :] = gh
        total = jnp.sum(gh.astype(F32), axis=0, keepdims=True)
        gub_ref[...] = total if i == 0 else gub_ref[...] + total
        part = dot(gh, up_ref[...], 1, 1)

        @pl.when(j == 0)
        def _():
            acc[rows, :] = part

        @pl.when(j > 0)
        def _():
            acc[rows, :] += part

    @pl.when(j == last)
    def _():
        for i, out in enumerate((g0, g1)):
            total = acc[i * size : (i + 1) * size, :]
            if n_add:
                total = total + refs[i][...].astype(F32)
            out[...] = total.astype(BF)


def mlp(k, n_hi, n, c, up, upb, down, before):
    rows, width = n[0].shape
    units = up.shape[1]
    tile = min(512, units)
    steps = units // tile
    here = whole_spec((rows, width))
    held = [] if before is None else [before[2], before[3], before[0], before[1]]
    wide = pl.BlockSpec((2 * rows, tile), lambda j: (0, k * steps + j))
    return call(
        functools.partial(mlp_kernel, len(held) // 2),
        [*n, *c, up, upb, down, *held],
        [((2 * rows, n_hi * units), BF)] * 2 + [((rows, width), BF)] * 2 + [((1, units), F32)],
        scratch=[pltpu.VMEM((2 * rows, width), F32)],
        flops=12 * rows * width * units,
        in_specs=[here] * 4
        + [
            pl.BlockSpec((width, tile), lambda j: (0, j)),
            pl.BlockSpec((1, tile), lambda j: (0, j)),
            pl.BlockSpec((tile, width), lambda j: (j, 0)),
        ]
        + ([here] * 2 + [pl.BlockSpec(memory_space=pl.ANY)] * 2 if held else []),
        out_specs=[wide] * 2 + [here] * 2 + [pl.BlockSpec((1, tile), lambda j: (0, j))],
        grid=(steps,),
        input_output_aliases={9: 0, 10: 1} if held else {},
        name="mlp",
    )


def row_product_kernel(n_parts, act_ref, *refs):
    parts, outs = refs[:n_parts], refs[n_parts:]
    size, units = outs[0].shape[0], parts[0].shape[0]
    for i, out in enumerate(outs):
        rows = slice(i * size, (i + 1) * size)
        total = None
        for k, ref in enumerate(parts):
            part = dot(act_ref[rows, k * units : (k + 1) * units], ref[...], 1, 0)
            total = part if total is None else total + part
        out[...] = total.astype(BF)


def row_product(act, parts):
    rows, width = act.shape[0] // 2, parts[0].shape[1]
    return call(
        functools.partial(row_product_kernel, len(parts)),
        [act, *parts],
        [((rows, width), BF)] * 2,
        flops=4 * rows * width * act.shape[1],
        name="row_product",
    )


def wgrad_kernel(n_left, n_right, index_ref, *refs):
    left, right = refs[:n_left], refs[n_left : n_left + n_right]
    out_ref, held, sems = refs[n_left + n_right :]
    size = right[0].shape[0]
    copies = [
        pltpu.make_async_copy(r, held.at[pl.ds(i * size, size)], sems.at[i])
        for i, r in enumerate(right)
    ]

    first = pl.program_id(0) == 0

    @pl.when(first)
    def _():
        for copy in copies:
            copy.start()

    total, at = None, 0
    for ref in left:
        rows = ref.shape[0]

        @pl.when(first)
        def _(at=at, rows=rows):
            for copy in copies[at // size : (at + rows) // size]:
                copy.wait()

        part = dot(ref[...], held[at : at + rows, :], 0, 0)
        total = part if total is None else total + part
        at += rows
    out_ref[...] = total.astype(BF)


def wgrad(left, right, index, tile):
    width = right[0].shape[1]
    total = sum(r.shape[0] for r in right)
    blocks = index.shape[0]
    in_specs = [pl.BlockSpec((x.shape[0], tile), lambda j, at: (0, at[j])) for x in left]
    in_specs += [pl.BlockSpec(memory_space=pl.ANY)] * len(right)
    moved = 2 * (total * (width + blocks * tile) + blocks * tile * width)
    return pl.pallas_call(
        functools.partial(wgrad_kernel, len(left), len(right)),
        grid_spec=pltpu.PrefetchScalarGridSpec(
            num_scalar_prefetch=1,
            grid=(blocks,),
            in_specs=in_specs,
            out_specs=pl.BlockSpec((tile, width), lambda j, at: (j, 0)),
            scratch_shapes=[
                pltpu.VMEM((total, width), BF),
                pltpu.SemaphoreType.DMA((len(right),)),
            ],
        ),
        out_shape=jax.ShapeDtypeStruct((blocks * tile, width), BF),
        compiler_params=pltpu.CompilerParams(vmem_limit_bytes=60 * 2**20),
        cost_estimate=pl.CostEstimate(
            flops=2 * total * blocks * tile * width * HINT,
            bytes_accessed=moved * HINT,
            transcendentals=0,
        ),
        name="wgrad",
    )(index, *left, *right)


def place_kernel(count, transposed, at_ref, *refs):
    pieces, out_ref = refs[:count], refs[count]
    total = sum(ref.shape[0] for ref in pieces)
    size = total // at_ref.shape[0]
    target = refs[count + 1] if transposed else out_ref
    i = 0
    for ref in pieces:
        for start in range(0, ref.shape[0], size):
            rows = pl.ds(pl.multiple_of(at_ref[i] * size, size), size)
            target[rows, :] = ref[start : start + size, :].astype(target.dtype)
            i += 1
    if transposed:
        for at in range(0, total, 256):
            out_ref[:, at : at + 256] = target[at : at + 256, :].astype(F32).T


def place(pieces, at, transposed):
    width = pieces[0].shape[1]
    rows = sum(x.shape[0] for x in pieces)
    shape = (width, rows) if transposed else (rows, width)
    vmem = pl.BlockSpec(memory_space=pltpu.VMEM)
    return call(
        functools.partial(place_kernel, len(pieces), transposed),
        [at, *pieces],
        [(shape, F32)],
        scratch=[pltpu.VMEM((rows, width), BF)] if transposed else [],
        in_specs=[pl.BlockSpec(memory_space=pltpu.SMEM)] + [vmem] * len(pieces),
        name="place",
    )[0]


def attend_wgrad_kernel(n, rows_of, *refs):
    d, heads, first, branch = [refs[i * n : (i + 1) * n] for i in range(4)]
    out_ref, held, sems = refs[4 * n :]
    size, hc = d[0].shape[0], heads[0].shape[1]
    sources = list(first) + list(branch)
    copies = [
        pltpu.make_async_copy(r, held.at[pl.ds(i * size, size)], sems.at[i])
        for i, r in enumerate(sources)
    ]
    for copy in copies:
        copy.start()
    for at, left in ((0, d), (n, heads)):
        total = None
        for i, ref in enumerate(left):
            copies[at + i].wait()
            part = dot(ref[...], held[(at + i) * size : (at + i + 1) * size, :], 0, 0)
            total = part if total is None else total + part
        low = total.astype(BF)
        for i in range(low.shape[0] // hc):
            to = rows_of[i if at == 0 else 3] * hc
            out_ref[to : to + hc, :] = low[i * hc : (i + 1) * hc]


def attend_wgrad(d, heads, first, branch, rows_of):
    size, width = first[0].shape
    hc = heads[0].shape[1]
    vmem = pl.BlockSpec(memory_space=pltpu.VMEM)
    n = len(d)
    return call(
        functools.partial(attend_wgrad_kernel, n, tuple(rows_of)),
        [*d, *heads, *first, *branch],
        [((4 * hc, width), BF)],
        scratch=[pltpu.VMEM((2 * n * size, width), BF), pltpu.SemaphoreType.DMA((2 * n,))],
        flops=8 * n * size * hc * width,
        in_specs=[vmem] * (2 * n) + [pl.BlockSpec(memory_space=pl.ANY)] * (2 * n),
        name="attend_wgrad",
    )[0]


def place_heads_kernel(count, at_ref, *refs):
    pieces, qkv_ref, out_ref, buf = refs[:count], *refs[count:]
    hc = out_ref.shape[0] // 2
    size = buf.shape[0] // at_ref.shape[0]
    i = 0
    for ref in pieces:
        for start in range(0, ref.shape[0], size):
            rows = pl.ds(pl.multiple_of(at_ref[i] * size, size), size)
            buf[rows, :] = ref[start : start + size, :]
            i += 1
    for core in (0, 1):
        for mat in range(4):
            x = buf[(core * 4 + mat) * hc : (core * 4 + mat + 1) * hc, :].astype(F32)
            if mat == 3:
                out_ref[core * hc : (core + 1) * hc, :] = x
            else:
                qkv_ref[mat, core * hc : (core + 1) * hc, :] = x


def place_heads(pieces, at):
    rows, width = sum(x.shape[0] for x in pieces), pieces[0].shape[1]
    hc = rows // 8
    size = rows // at.shape[0]
    if size % 16:
        buf, i = jnp.zeros((rows, width), BF), 0
        for x in pieces:
            for start in range(0, x.shape[0], size):
                buf = lax.dynamic_update_slice_in_dim(buf, x[start : start + size], at[i] * size, 0)
                i += 1
        buf = buf.reshape(2, 4, hc, width).astype(F32)
        mats = [buf[:, i].reshape(2 * hc, width) for i in range(4)]
        return jnp.stack(mats[:3]), mats[3]
    vmem = pl.BlockSpec(memory_space=pltpu.VMEM)
    return call(
        functools.partial(place_heads_kernel, len(pieces)),
        [at, *pieces],
        [((3, 2 * hc, width), F32), ((2 * hc, width), F32)],
        scratch=[pltpu.VMEM((rows, width), BF)],
        in_specs=[pl.BlockSpec(memory_space=pltpu.SMEM)] + [vmem] * len(pieces),
        name="place_heads",
    )


class Order:
    def __init__(self):
        self.last, self.also = None, ()

    def gate(self, x):
        if self.last is None:
            return x
        return lax.optimization_barrier((x, self.last, *self.also))[0]

    def __call__(self, kernel, x, *rest):
        out = kernel(self.gate(x), *rest)
        self.last, self.also = jax.tree.leaves(out)[-1], ()
        return out

    def meet(self, *arrays):
        self.also += arrays


class Layout:
    def __init__(self, dp, tensor):
        self.dp, self.tensor = dp, tensor
        self.n_p, self.n_hi = dp // 2, tensor // 2
        self.bits = [1 << b for b in range(self.n_p.bit_length() - 1)]

    def move(self, x, p=0, c=0, hi=0, lo=0):
        dp_mask, tensor_mask = 2 * p + c, 2 * hi + lo
        pairs = [
            (d * self.tensor + t, (d ^ dp_mask) * self.tensor + (t ^ tensor_mask))
            for d in range(self.dp)
            for t in range(self.tensor)
        ]
        return lax.ppermute(x, ("dp", "tensor"), pairs)

    def place_of(self, p, order):
        n = len(order)
        place = 0
        for i, bit in enumerate(order):
            place = place + (p // bit) % 2 * (1 << (n - 1 - i))
        return place

    def spread_masks(self, order):
        masks = [0]
        for bit in order:
            masks += [m ^ bit for m in masks]
        return masks

    def spread_direct(self, block):
        return {m: self.move(block, p=m) if m else block for m in range(self.n_p)}


def on_device(
    lay,
    images,
    first_gain,
    first_shift,
    qkv_weight,
    qv_bias,
    out_weight,
    out_bias,
    second_gain,
    second_shift,
    up_weight,
    up_bias,
    down_weight,
    down_bias,
    cotangent,
):
    n_p, n_hi = lay.n_p, lay.n_hi
    n_i, seq, width = images.shape
    columns = qkv_weight.shape[2]
    units = up_weight.shape[1]
    hc, hu = columns // 2, units // 2
    dp = lax.axis_index("dp")
    p, c = dp // 2, dp % 2
    up_order, down_order = lay.bits, lay.bits[::-1]
    order = Order()
    first_gain, first_shift, out_bias, second_gain, second_shift, down_bias = [
        v.reshape(1, width)
        for v in (first_gain, first_shift, out_bias, second_gain, second_shift, down_bias)
    ]

    def half(x, axis):
        n = x.shape[axis] // 2
        return lax.dynamic_slice_in_dim(x, c * n, n, axis)

    def block(x, axis, at):
        n = x.shape[axis] // n_p
        return lax.dynamic_slice_in_dim(x, at * n, n, axis)

    def put(buf, x, axis, at):
        return lax.dynamic_update_slice_in_dim(buf, x, at, axis)

    x_unit, first_own = order(pack, images, first_gain, first_shift, True)
    first_c, first_z = lay.move(first_own, c=1), lay.move(first_own, lo=1)
    head_rows = jnp.swapaxes(qkv_weight, 1, 2)

    def weights_here(x):
        return jnp.concatenate([half(x[i], 0) for i in range(3)] + [half(out_weight, 0)])

    if n_p == 4:

        def cut_of(x):
            mat = lax.dynamic_index_in_dim(x, jnp.minimum(p, 2), 0, keepdims=False)
            return jnp.where(p == 3, half(out_weight, 0), half(mat, 0))

        work_cut = order(cut_of, head_rows)
    else:
        work_cut = block(weights_here(head_rows), 0, p)
    work_hi = [lay.move(work_cut, hi=k) for k in range(1, n_hi)]
    qv_half, upb_half = half(qv_bias, 1), half(up_bias, 0)
    bias_all = [jnp.concatenate([qv_half.reshape(-1), upb_half])]
    work_mine = order(weights_here, head_rows)
    work = [work_mine]
    forward = [[None] * 4 for _ in range(n_hi)]

    def qkv_bias_of(b):
        return jnp.concatenate([b[:hc], jnp.zeros((hc,), F32), b[hc : 2 * hc]]).reshape(1, -1)

    qkv_bias = [qkv_bias_of(bias_all[0])]

    def attention(k, u, n, adds=()):
        adds = list(adds) + ([forward[k - 1][u][4]] if k else [])
        forward[k][u] = order(lambda x: attend_fwd(n_i, x, work[k], qkv_bias[k], adds), n)
        return forward[k][u][4]

    def stage(held, axis, bit):
        return jnp.concatenate([held, lay.move(held, p=bit)], axis)

    attention(0, 0, first_own)
    bias_hi = [lay.move(order.gate(bias_all[0]), hi=k) for k in range(1, n_hi)]
    attention(0, 1, first_c)
    seed_unit, grad_down_bias = order(pack, cotangent, first_gain, first_shift, False)
    seed_c = lay.move(seed_unit, c=1)
    order.meet(*work_hi)
    work_got = [lay.spread_direct(order.gate(x)) for x in work_hi]
    first_zc = lay.move(order.gate(first_z), c=1)
    attention(0, 2, first_z)
    seed_z = lay.move(seed_unit, lo=1)
    attention(0, 3, first_zc)
    up_cut = order(lambda x: block(half(x, 1), 1, p), up_weight)
    up_hi = [lay.move(up_cut, hi=k) for k in range(1, n_hi)]
    down_cut = order(lambda x: block(half(x, 0), 0, p), down_weight)
    down_hi = [lay.move(down_cut, hi=k) for k in range(1, n_hi)]

    def assemble(got):
        masks = sorted(got)

        def run(x):
            full = jnp.zeros_like(work_mine)
            for mask in masks:
                x = x if mask == 0 else got[mask]
                full = put(full, x, 0, (p ^ mask) * x.shape[0])
            return full

        return order(run, got[0])

    work += [assemble(got) for got in work_got]
    bias_all += [order.gate(x) for x in bias_hi]
    qkv_bias += [qkv_bias_of(b) for b in bias_all[1:]]
    normed = (first_own, first_c, first_z, first_zc)
    for k in range(1, n_hi - 1):
        for u in range(4):
            attention(k, u, normed[u])
    k = n_hi - 1

    def widen(pairs, axis):
        return [order(lambda x, y=y: jnp.concatenate([x, y], axis), x) for x, y in pairs]

    moved_3 = lay.move(attention(k, 3, first_zc), c=1)
    order.meet(seed_c)
    moved_1 = lay.move(attention(k, 1, first_c), c=1)
    moved_2 = lay.move(attention(k, 2, first_z, [moved_3]), lo=1)
    order.meet(moved_1, seed_z, *up_hi)
    seed_zc = lay.move(order.gate(seed_z), c=1)
    up_got = [order.gate(x) for x in up_hi]
    up_got = [(x, lay.move(x, p=up_order[0])) for x in up_got]
    down_got = [order.gate(x) for x in down_hi]
    down_got = [(x, lay.move(x, p=down_order[0])) for x in down_got]
    attention_parts = (attention(k, 0, first_own), moved_1, moved_2)
    normed_first = list(normed)
    up_work = [order(lambda x: half(x, 1), up_weight)]
    down_work = [order(lambda x: half(x, 0), down_weight)]
    for i in range(1, len(lay.bits)):
        up_got = [(x, lay.move(x, p=up_order[i])) for x in widen(up_got, 1)]
        down_got = [(x, lay.move(x, p=down_order[i])) for x in widen(down_got, 0)]
    order.meet(seed_zc)
    seed = [seed_unit, seed_c, seed_z, seed_zc]

    middle, second_own = order(
        lambda x: norm_second(x, attention_parts, out_bias, second_gain, second_shift), x_unit
    )
    second_c, second_z = lay.move(second_own, c=1), lay.move(second_own, lo=1)

    def fill(parts, axis, order_of):
        size = parts[0].shape[axis] * 2 // n_p
        shape = [width, width]
        shape[axis] = hu
        masks = lay.spread_masks(order_of)

        def run(x):
            full, at = jnp.zeros(shape, BF), 0
            for part in (x, *parts[1:]):
                for i in range(part.shape[axis] // size):
                    piece = lax.slice_in_dim(part, i * size, (i + 1) * size, axis=axis)
                    full = put(full, piece, axis, (p ^ masks[at]) * size)
                    at += 1
            return full

        return order(run, parts[0])

    up_half = [upb_half.reshape(1, -1)] + [b[2 * hc :].reshape(1, -1) for b in bias_all[1:]]

    def mlp_half(k, first, second, seeds, before):
        return order(
            lambda x: mlp(k, n_hi, [x, second], seeds, up_work[k], up_half[k], down_work[k], before),
            first,
        )

    near = mlp_half(0, second_own, second_c, seed[:2], None)
    up_work += [fill(parts, 1, up_order) for parts in up_got]
    down_work += [fill(parts, 0, down_order) for parts in down_got]
    near_bias, far_bias = [near[4]], []
    for k in range(1, n_hi):
        near = mlp_half(k, second_own, second_c, seed[:2], near)
        near_bias.append(near[4])
    second_zc = lay.move(order.gate(second_z), c=1)
    other_c = lay.move(near[3], c=1)
    low_near = order(lambda x: row_product(x, down_work), near[0])
    low_near_c = lay.move(low_near[1], c=1)
    far = None
    for k in range(n_hi):
        if k == n_hi - 1:
            order.meet(other_c, low_near_c)
        far = mlp_half(k, second_z, second_zc, seed[2:], far)
        far_bias.append(far[4])
    normed_second = [second_own, second_c, second_z, second_zc]

    def index(order_of, other):
        top = lay.place_of(p, order_of) // (n_p // 2)
        return jnp.stack([2 * k + (top ^ other) for k in range(n_hi)]).astype(jnp.int32)

    def mlp_grad(which, right, order_of, other):
        return order(
            lambda x: wgrad([x, far[which]], right, index(order_of, other), hu // 2), near[which]
        )

    far_c = lay.move(far[3], c=1)
    down_send = mlp_grad(0, seed, down_order, 1)
    down_recv = lay.move(down_send, p=down_order[0])

    def join(*parts):
        total = parts[0].astype(F32)
        for x in parts[1:]:
            total = total + x.astype(F32)
        return total.astype(BF)

    far_sum = order(lambda x: join(x, far_c), far[2])
    grad_second = (near[2], other_c, lay.move(far_sum, lo=1))
    up_send = mlp_grad(1, normed_second, up_order, 1)
    up_recv = lay.move(up_send, p=up_order[0])
    down_keep = mlp_grad(0, seed, down_order, 0)
    grad_middle, grad_branch, grad_second_gain, grad_second_shift, grad_out_bias = order(
        lambda x: norm_back(x, grad_second, seed_unit, second_gain, True), middle
    )
    branch_c, branch_z = lay.move(grad_branch, c=1), lay.move(grad_branch, lo=1)
    low_far = order(lambda x: row_product(x, down_work), far[0])
    low_far_c = lay.move(low_far[1], c=1)
    up_keep = mlp_grad(1, normed_second, up_order, 0)

    def halve(keep, recv, order_of, stage, parts):
        bit = order_of[stage]
        side = (p // bit) % 2
        shape = (parts, 2, keep.shape[0] // (2 * parts), width)

        def pick(x, s):
            x = lax.dynamic_index_in_dim(x.reshape(shape), s, 1, keepdims=False)
            return x.reshape(-1, width)

        send = order(lambda x: join(pick(x, 1 - side), pick(recv, 1 - side)), keep)
        keep = join(pick(keep, side), pick(recv, side))
        return keep, lay.move(send, p=bit)

    def settle_hi(keep, recv):
        size = keep.shape[0] // n_hi
        total = order(lambda x: join(x, recv), keep)
        got = [lay.move(total[k * size : (k + 1) * size], hi=k) for k in range(1, n_hi)]
        return total[:size], got

    class Spread:
        def __init__(self, mine, order_of):
            self.pieces, self.order_of, self.bits = [mine], order_of, order_of[::-1]
            self.got, self.at = lay.move(mine, p=self.bits[0]), 1

        def step(self):
            self.pieces.append(self.got)
            held = order(lambda x: jnp.concatenate([x] + self.pieces[1:]), self.pieces[0])
            if self.at < len(self.bits):
                self.got = lay.move(held, p=self.bits[self.at])
            else:
                self.pieces = [held, lay.move(held, c=1)]
            self.at += 1

        def finish(self):
            while self.at <= len(self.bits):
                self.step()
            masks = lay.spread_masks(self.bits)
            places = [lay.place_of(p ^ mask, self.order_of) for mask in masks]
            at = [c * n_p + x for x in places] + [(1 - c) * n_p + x for x in places]
            return self.pieces, jnp.stack(at).astype(jnp.int32)

    backward = [[None] * 4 for _ in range(n_hi)]
    branch = [grad_branch, branch_c, branch_z, None]

    def attention_back(k, u, adds=()):
        adds = list(adds) + ([backward[k + 1][u][2]] if k < n_hi - 1 else [])
        f = forward[k][u]
        backward[k][u] = order(
            lambda g: attend_bwd(n_i, g, (f[0], f[2], f[3], work[k]), adds),
            branch[u],
        )
        return backward[k][u][2]

    def attention_send(k, order_of):
        owner = [0] * n_p
        for q in range(n_p):
            owner[lay.place_of(q, order_of)] = lay.place_of(q, orders[0])
        grad = order(
            lambda x: attend_wgrad(
                [x] + [b[0] for b in backward[k][1:]],
                [f[1] for f in forward[k]],
                normed_first,
                branch,
                owner if n_p == 4 else range(4),
            ),
            backward[k][0][0],
        )
        if n_p != 4:
            blocks = jnp.split(grad, n_p)
            grad = jnp.concatenate([blocks[i] for i in owner])
        top = lay.place_of(p, order_of) // (n_p // 2)
        size = grad.shape[0] // 2
        send = order(lambda x: lax.dynamic_slice_in_dim(x, (1 - top) * size, size, 0), grad)
        keep = lax.dynamic_slice_in_dim(grad, top * size, size, 0)
        return keep, lay.move(send, p=order_of[0])

    down_pair, up_pair = (down_keep, down_recv), (up_keep, up_recv)
    attn_pairs = [None] * n_hi
    orders = [up_order] + [down_order] * (n_hi - 1)
    n_stage = len(lay.bits)
    k = n_hi - 1
    down_pair = halve(*down_pair, down_order, 1, n_hi)
    attention_back(k, 0)
    branch[3] = lay.move(order.gate(branch_z), c=1)
    attention_back(k, 1)
    up_pair = halve(*up_pair, up_order, 1, n_hi)
    low_far_sum = order(lambda x: join(x, low_far_c), low_far[0])
    low_far_z = lay.move(low_far_sum, lo=1)
    attention_back(k, 2)
    for step in range(2, n_stage):
        down_pair = halve(*down_pair, down_order, step, n_hi)
        up_pair = halve(*up_pair, up_order, step, n_hi)
    down_mine, down_hi_got = settle_hi(*down_pair)
    attention_back(k, 3)
    attn_pairs[k] = attention_send(k, orders[k])
    up_mine, up_hi_got = settle_hi(*up_pair)
    result_parts = (low_near[0], low_near_c, low_far_z)
    result = order(lambda x: unpack(n_i, seq, x, result_parts, down_bias), middle)
    for k in range(n_hi - 2, 0, -1):
        for u in range(4):
            attention_back(k, u)
        attn_pairs[k] = attention_send(k, orders[k])
    moved_3 = lay.move(attention_back(0, 3), c=1)
    down_mine = order(lambda x: join(x, *down_hi_got), down_mine)
    down_all = Spread(down_mine, down_order)
    moved_1 = lay.move(attention_back(0, 1), c=1)
    down_all.step()
    moved_2 = lay.move(attention_back(0, 2, [moved_3]), lo=1)
    for k in range(1, n_hi):
        for step in range(1, n_stage):
            attn_pairs[k] = halve(*attn_pairs[k], orders[k], step, 1)
    order.meet(moved_1)
    grad_first = (attention_back(0, 0), moved_1, moved_2)
    up_mine = order(lambda x: join(x, *up_hi_got), up_mine)
    up_all = Spread(up_mine, up_order)
    attn_hi = []
    for k in range(1, n_hi):
        total = order(lambda x, k=k: join(x, attn_pairs[k][1]), attn_pairs[k][0])
        attn_hi.append(lay.move(total, hi=k))
    down_all = down_all.finish()
    grad = order(
        lambda x: attend_wgrad(
            [x] + [b[0] for b in backward[0][1:]],
            [f[1] for f in forward[0]],
            normed_first,
            branch,
            range(4),
        ),
        backward[0][0][0],
    )
    places = [lay.place_of(p ^ mask, orders[0]) for mask in range(n_p)]
    attn_own = block(grad, 0, places[0])
    attn_got = []
    for mask in range(1, n_p):
        out = order(lambda x, mask=mask: block(x, 0, places[mask]), grad)
        attn_got.append(lay.move(out, p=mask))
    up_all.step()

    def place_all(blocks, at, transposed):
        return order(lambda x: place([x] + blocks[1:], at, transposed), blocks[0])

    grad_down_weight = place_all(*down_all, False)
    _, grad_images, grad_first_gain, grad_first_shift, _ = order(
        lambda x: norm_back(x, grad_first, grad_middle, first_gain, False), x_unit
    )
    attn_mine = order(lambda x: join(x, *attn_got, *attn_hi), attn_own)
    attn_all = lay.spread_direct(attn_mine)

    tensor_at = lax.axis_index("tensor")
    all_units, all_columns = units * lay.tensor, columns * lay.tensor
    grad_up_bias = jnp.concatenate([(a + b)[0] for a, b in zip(near_bias, far_bias)])
    wide_up = jnp.zeros((all_units,), F32)
    wide_qv = jnp.zeros((2, all_columns), F32)
    for k in range(n_hi):
        shard = tensor_at ^ (2 * k)
        wide_up = put(wide_up, grad_up_bias[k * hu : (k + 1) * hu], 0, shard * units + c * hu)
        bias = sum(b[1] for b in backward[k])[0]
        bias = jnp.stack([bias[:hc], bias[2 * hc :]])
        wide_qv = put(wide_qv, bias, 1, shard * columns + c * hc)
    sums = (
        grad_first_gain,
        grad_first_shift,
        grad_out_bias,
        grad_second_gain,
        grad_second_shift,
        grad_down_bias,
    )
    vector = jnp.concatenate(
        [jnp.sum(x, axis=0) for x in sums] + [wide_up, wide_qv.reshape(-1)]
    )
    hops = [dict(c=1)] + [
        dict(lo=(1 << b) & 1, hi=(1 << b) >> 1) for b in range(lay.tensor.bit_length() - 1)
    ]
    hops += [dict(p=bit) for bit in lay.bits]

    def hop(vector):
        got = lay.move(vector, **hops.pop(0))
        return vector, got

    def add(pair):
        return order(lambda x: x + pair[1], pair[0])

    pair = hop(vector)
    grad_images = order(lambda x: unpack(n_i, seq, x), grad_images)
    pair = hop(add(pair))
    for _ in range(lay.tensor.bit_length() - 2):
        pair = hop(add(pair))
    up_all = up_all.finish()
    pair = hop(add(pair))
    masks = sorted(attn_all)
    held = order(
        lambda x: jnp.concatenate([x] + [attn_all[mask] for mask in masks[1:]]), attn_all[0]
    )
    held_c = lay.move(held, c=1)
    grad_up_weight = place_all(*up_all, True)
    at = [lay.place_of(p ^ mask, orders[0]) for mask in masks]
    at = [c * n_p + x for x in at] + [(1 - c) * n_p + x for x in at]
    attn_all = ([held, held_c], jnp.stack(at).astype(jnp.int32))
    while hops:
        pair = hop(add(pair))
    vector = add(pair)
    norms = vector[: 6 * width].reshape(6, width)
    vector = vector[6 * width :]
    grad_up_bias = lax.dynamic_slice_in_dim(vector, tensor_at * units, units, 0)
    grad_qv_bias = lax.dynamic_slice_in_dim(
        vector[all_units:].reshape(2, all_columns), tensor_at * columns, columns, 1
    )

    grad_qkv_weight, grad_out_weight = place_heads(*attn_all)
    grad_qkv_weight = jnp.swapaxes(grad_qkv_weight, 1, 2)
    return (
        result,
        grad_images,
        norms[0],
        norms[1],
        grad_qkv_weight,
        grad_qv_bias,
        grad_out_weight,
        norms[2],
        norms[3],
        norms[4],
        grad_up_weight,
        grad_up_bias,
        grad_down_weight,
        norms[5],
    )


def solution(mesh):
    lay = Layout(mesh.shape["dp"], mesh.shape["tensor"])
    rows = P(("dp", "tensor"), None, None)
    qkv, qv = P(None, None, "tensor"), P(None, "tensor")
    line, up, down, rep = P("tensor"), P(None, "tensor"), P("tensor", None), P()
    return jax.shard_map(
        functools.partial(on_device, lay),
        mesh=mesh,
        in_specs=(rows, rep, rep, qkv, qv, down, rep, rep, rep, up, line, down, rep, rows),
        out_specs=(rows, rows, rep, rep, qkv, qv, down, rep, rep, rep, up, line, down, rep),
        check_vma=False,
    )
```

```python
import functools

import jax
import jax.numpy as jnp
from jax import lax
from jax.experimental import pallas as pl
from jax.experimental.pallas import tpu as pltpu
from jax.sharding import PartitionSpec as P

HD = 104
PAD = 16
BF = jnp.bfloat16
F32 = jnp.float32


def dot(a, b, ca, cb):
    return lax.dot_general(a, b, (((ca,), (cb,)), ((), ())), preferred_element_type=F32)


def whole_spec(shape):
    return pl.BlockSpec(shape, lambda *_: (0,) * len(shape), pipeline_mode=pl.Buffered(1))


def head_mask(heads):
    lane = lax.broadcasted_iota(jnp.int32, (8, heads * HD), 1)
    row = lax.broadcasted_iota(jnp.int32, (8, heads * HD), 0)
    return (lane >= row * HD) & (lane < row * HD + HD)


def attend_fwd_kernel(n_i, main, heads, n_add, n_ref, w_ref, b_ref, *refs):
    adds = refs[:n_add]
    qkv_ref, ho_ref, lse_ref, lset_ref, out_ref = refs[n_add:]
    hc = heads * HD
    tail = pl.ds(n_i * main, PAD)
    qkv_ref[...] = (dot(n_ref[...], w_ref[0 : 3 * hc, :], 1, 1) + b_ref[...]).astype(BF)
    ho_ref[tail, :] = jnp.zeros((PAD, hc), BF)
    factor = HD ** -0.5
    tail_row = lax.broadcasted_iota(jnp.int32, (PAD, 1), 0)
    per_head = head_mask(heads)

    def image(i, carry):
        rows = pl.ds(pl.multiple_of(i * main, main), main)
        here = tail_row == i
        bar = jnp.where(here, 0.0, -1e30)
        bar_all = jnp.concatenate([jnp.zeros((main, 1), F32), bar], 0)

        def both(cols):
            return jnp.concatenate([qkv_ref[rows, cols], qkv_ref[tail, cols]], 0)

        q_t = jnp.sum(jnp.where(here, qkv_ref[tail, 0:hc].astype(F32), 0.0), 0, keepdims=True)
        q_b = jnp.where(per_head, q_t, 0.0).astype(BF)
        s = dot(both(slice(hc, 2 * hc)), q_b, 1, 1) * factor + bar_all
        top = jnp.max(s, 0, keepdims=True)
        e = jnp.exp(s - top)
        total = jnp.sum(e, 0, keepdims=True)
        o = dot((e * (1.0 / total)).astype(BF), both(slice(2 * hc, 3 * hc)), 0, 0)
        o = jnp.sum(jnp.where(per_head, o, 0.0), 0, keepdims=True).astype(BF)
        ho_ref[tail, :] = jnp.where(here, o, ho_ref[tail, :])
        lset_ref[pl.ds(i, 1), 0:8] = top + jnp.log(total)
        for h in range(heads):
            cols = [slice(t * hc + h * HD, t * hc + (h + 1) * HD) for t in range(3)]
            q = qkv_ref[rows, cols[0]]
            s = dot(qkv_ref[rows, cols[1]], q, 1, 1) * factor
            s_t = dot(qkv_ref[tail, cols[1]], q, 1, 1) * factor + bar
            top = jnp.maximum(jnp.max(s, 0, keepdims=True), jnp.max(s_t, 0, keepdims=True))
            e, e_t = jnp.exp(s - top), jnp.exp(s_t - top)
            total = jnp.sum(e, 0, keepdims=True) + jnp.sum(e_t, 0, keepdims=True)
            inv = 1.0 / total
            o = dot((e * inv).astype(BF), qkv_ref[rows, cols[2]], 0, 0)
            o = o + dot((e_t * inv).astype(BF), qkv_ref[tail, cols[2]], 0, 0)
            ho_ref[rows, h * HD : (h + 1) * HD] = o.astype(BF)
            lse_ref[h : h + 1, rows] = top + jnp.log(total)
        return carry

    lax.fori_loop(0, n_i, image, 0)
    total = dot(ho_ref[...], w_ref[3 * hc :, :], 1, 0)
    for ref in adds:
        total = total + ref[...].astype(F32)
    out_ref[...] = total.astype(BF)


def attend_fwd(n_i, n, w, b, adds=()):
    rows, width = n.shape
    hc = w.shape[0] // 4
    main = (rows - PAD) // n_i
    shapes = (
        ((rows, 3 * hc), BF),
        ((rows, hc), BF),
        ((8, n_i * main), F32),
        ((8, 128), F32),
        ((rows, width), BF),
    )
    flops = 2 * rows * width * 4 * hc + 4 * n_i * main * main * hc
    return call(
        functools.partial(attend_fwd_kernel, n_i, main, hc // HD, len(adds)),
        [n, w, b, *adds],
        shapes,
        flops=flops,
        name="attend_fwd",
    )


def attend_bwd_kernel(n_i, main, heads, n_add, g_ref, qkv_ref, lse_ref, lset_ref, w_ref, *refs):
    adds = refs[:n_add]
    d_ref, gb_ref, gn_ref, gh_ref, kv_ref = refs[n_add:]
    hc = heads * HD
    tail = pl.ds(n_i * main, PAD)
    gh_ref[...] = dot(g_ref[...], w_ref[3 * hc :, :], 1, 1).astype(BF)
    d_ref[tail, :] = jnp.zeros((PAD, 3 * hc), BF)
    factor = HD ** -0.5
    tail_row = lax.broadcasted_iota(jnp.int32, (PAD, 1), 0)
    per_head = head_mask(heads)

    def image(i, carry):
        rows = pl.ds(pl.multiple_of(i * main, main), main)
        here = tail_row == i
        bar = jnp.where(here, 0.0, -1e30)
        bar_all = jnp.concatenate([jnp.zeros((main, 1), F32), bar], 0)

        def both(cols):
            return jnp.concatenate([qkv_ref[rows, cols], qkv_ref[tail, cols]], 0)

        def last(ref, cols):
            row = jnp.sum(jnp.where(here, ref[tail, cols].astype(F32), 0.0), 0, keepdims=True)
            return jnp.where(per_head, row, 0.0).astype(BF)

        q_b, go_b = last(qkv_ref, slice(0, hc)), last(gh_ref, slice(0, hc))
        k_all, v_all = both(slice(hc, 2 * hc)), both(slice(2 * hc, 3 * hc))
        p = jnp.exp(dot(k_all, q_b, 1, 1) * factor + bar_all - lset_ref[pl.ds(i, 1), 0:8])
        dp = dot(v_all, go_b, 1, 1)
        ds = (p * (dp - jnp.sum(p * dp, 0, keepdims=True))).astype(BF)
        dq = dot(ds, k_all, 0, 0) * factor
        dq = jnp.sum(jnp.where(per_head, dq, 0.0), 0, keepdims=True).astype(BF)
        d_ref[tail, 0:hc] = jnp.where(here, dq, d_ref[tail, 0:hc])
        kv_ref[:, 0:hc] = dot(ds, q_b, 1, 0)
        kv_ref[:, hc : 2 * hc] = dot(p.astype(BF), go_b, 1, 0)
        for h in range(heads):
            head = slice(h * HD, (h + 1) * HD)
            cols = [slice(t * hc + h * HD, t * hc + (h + 1) * HD) for t in range(3)]
            q, go = qkv_ref[rows, cols[0]], gh_ref[rows, head]
            k, k_t = qkv_ref[rows, cols[1]], qkv_ref[tail, cols[1]]
            v, v_t = qkv_ref[rows, cols[2]], qkv_ref[tail, cols[2]]
            lse = lse_ref[h : h + 1, rows]
            p = jnp.exp(dot(k, q, 1, 1) * factor - lse)
            p_t = jnp.exp(dot(k_t, q, 1, 1) * factor + bar - lse)
            dp, dp_t = dot(v, go, 1, 1), dot(v_t, go, 1, 1)
            inner = jnp.sum(p * dp, 0, keepdims=True) + jnp.sum(p_t * dp_t, 0, keepdims=True)
            ds = (p * (dp - inner)).astype(BF)
            ds_t = (p_t * (dp_t - inner)).astype(BF)
            d_ref[rows, cols[0]] = ((dot(ds, k, 0, 0) + dot(ds_t, k_t, 0, 0)) * factor).astype(BF)
            dk = ((dot(ds, q, 1, 0) + kv_ref[0:main, head]) * factor).astype(BF)
            dk_t = ((dot(ds_t, q, 1, 0) + kv_ref[main:, head]) * factor).astype(BF)
            head_v = slice(hc + h * HD, hc + (h + 1) * HD)
            dv = (dot(p.astype(BF), go, 1, 0) + kv_ref[0:main, head_v]).astype(BF)
            dv_t = (dot(p_t.astype(BF), go, 1, 0) + kv_ref[main:, head_v]).astype(BF)
            d_ref[rows, cols[1]] = dk
            d_ref[rows, cols[2]] = dv
            d_ref[tail, cols[1]] = jnp.where(here, dk_t, d_ref[tail, cols[1]])
            d_ref[tail, cols[2]] = jnp.where(here, dv_t, d_ref[tail, cols[2]])
        return carry

    lax.fori_loop(0, n_i, image, 0)
    gb_ref[...] = jnp.sum(d_ref[...].astype(F32), 0, keepdims=True)
    total = dot(d_ref[...], w_ref[0 : 3 * hc, :], 1, 0)
    for ref in adds:
        total = total + ref[...].astype(F32)
    gn_ref[...] = total.astype(BF)


def attend_bwd(n_i, g, half, adds=()):
    rows, width = g.shape
    hc = half[3].shape[0] // 4
    main = (rows - PAD) // n_i
    shapes = [((rows, 3 * hc), BF), ((1, 3 * hc), F32), ((rows, width), BF)]
    return call(
        functools.partial(attend_bwd_kernel, n_i, main, hc // HD, len(adds)),
        [g, *half, *adds],
        shapes,
        scratch=[pltpu.VMEM((rows, hc), BF), pltpu.VMEM((main + PAD, 2 * hc), F32)],
        flops=2 * rows * width * 4 * hc + 10 * n_i * main * main * hc,
        name="attend_bwd",
    )


epsilon = 1e-06
inv_root_two = 0.7071067811865476
inv_root_tau = 0.3989422804014327
HINT = 30
def step_of(rows):
    return next(s for s in (48, 64, 32, 16) if rows % s == 0)


def call(kernel, ins, outs, scratch=(), flops=0, name=None, in_specs=None, **grid):
    moved = sum(x.size * x.dtype.itemsize for x in ins)
    moved += sum(int(jnp.dtype(d).itemsize) * functools.reduce(lambda a, b: a * b, s) for s, d in outs)
    vmem = pl.BlockSpec(memory_space=pltpu.VMEM)
    return pl.pallas_call(
        kernel,
        in_specs=in_specs or [vmem] * len(ins),
        out_specs=grid.pop("out_specs", [vmem] * len(outs)),
        out_shape=[jax.ShapeDtypeStruct(*s) for s in outs],
        scratch_shapes=list(scratch),
        compiler_params=pltpu.CompilerParams(vmem_limit_bytes=60 * 2**20),
        cost_estimate=pl.CostEstimate(
            flops=int(flops) * HINT, bytes_accessed=int(moved) * HINT, transcendentals=0
        ),
        name=name,
        **grid,
    )(*ins)


def mean_parts(rows):
    centred = rows - jnp.mean(rows, axis=1, keepdims=True)
    spread = jnp.mean(centred * centred, axis=1, keepdims=True)
    inverse = lax.rsqrt(spread + epsilon)
    return centred * inverse, inverse


def fold(x):
    total = x[0:8]
    for at in range(8, x.shape[0], 8):
        total = total + x[at : at + 8]
    return total


def pack_kernel(n_i, main, norm, img_ref, gain_ref, shift_ref, x_ref, other_ref):
    width = x_ref.shape[1]

    def emit(at, x, count):
        x_ref[pl.ds(at, count), :] = x
        if norm:
            unit, _ = mean_parts(x.astype(F32))
            other_ref[pl.ds(at, count), :] = (unit * gain_ref[...] + shift_ref[...]).astype(BF)

    size = step_of(main)
    if not norm:
        other_ref[...] = jnp.zeros(other_ref.shape, F32)
    tail_row = lax.broadcasted_iota(jnp.int32, (PAD, 1), 0)
    tails = jnp.zeros((PAD, width), F32)
    for i in range(n_i):

        def step(r, carry, i=i):
            at = pl.multiple_of(r * size, size)
            x = img_ref[i, pl.ds(at, size), :]
            emit(pl.multiple_of(i * main + r * size, size), x, size)
            if not norm:
                other_ref[...] += fold(x.astype(F32))
            return carry

        lax.fori_loop(0, main // size, step, 0)
        tails = jnp.where(tail_row == i, img_ref[i, main : main + 1, :].astype(F32), tails)
    emit(n_i * main, tails.astype(BF), PAD)
    if not norm:
        other_ref[...] += fold(tails)


def pack(img, gain, shift, norm):
    n_i, seq, width = img.shape
    rows = n_i * (seq - 1) + PAD
    other = ((rows, width), BF) if norm else ((8, width), F32)
    return call(
        functools.partial(pack_kernel, n_i, seq - 1, norm),
        [img, gain, shift],
        [((rows, width), BF), other],
        name="pack",
    )


def loop_rows(rows, step):
    size = step_of(rows)

    def one(r, carry):
        step(pl.ds(pl.multiple_of(r * size, size), size))
        return carry

    lax.fori_loop(0, rows // size, one, 0)


def norm_kernel(x_ref, a_ref, b_ref, c_ref, bias_ref, gain_ref, shift_ref, mid_ref, n_ref):
    def step(at):
        moved = a_ref[at, :].astype(F32) + b_ref[at, :].astype(F32) + c_ref[at, :].astype(F32)
        middle = x_ref[at, :].astype(F32) + (moved + bias_ref[...])
        mid_ref[at, :] = middle
        unit, _ = mean_parts(middle)
        n_ref[at, :] = (unit * gain_ref[...] + shift_ref[...]).astype(BF)

    loop_rows(x_ref.shape[0], step)


def norm_second(x, parts, bias, gain, shift):
    return call(
        norm_kernel,
        [x, *parts, bias, gain, shift],
        [(x.shape, F32), (x.shape, BF)],
        name="norm_second",
    )


def norm_back_kernel(res_f32, x_ref, a_ref, b_ref, c_ref, add_ref, gain_ref, *outs):
    out_ref, low_ref, gain_out, shift_out, bias_out = outs
    for ref in (gain_out, shift_out, bias_out):
        ref[...] = jnp.zeros(ref.shape, F32)

    def step(at):
        grad = a_ref[at, :].astype(F32) + b_ref[at, :].astype(F32) + c_ref[at, :].astype(F32)
        unit, inverse = mean_parts(x_ref[at, :].astype(F32))
        scaled = grad * gain_ref[...]
        first = jnp.mean(scaled, axis=1, keepdims=True)
        second = jnp.mean(scaled * unit, axis=1, keepdims=True)
        total = add_ref[at, :].astype(F32) + inverse * (scaled - first - unit * second)
        low = total.astype(BF)
        low_ref[at, :] = low
        if res_f32:
            out_ref[at, :] = total
            bias_out[...] += fold(low.astype(F32))
        gain_out[...] += fold(grad * unit)
        shift_out[...] += fold(grad)

    loop_rows(x_ref.shape[0], step)


def norm_back(x, parts, add, gain, keep):
    rows, width = x.shape
    full = (x.shape, F32) if keep else ((8, width), F32)
    return call(
        functools.partial(norm_back_kernel, keep),
        [x, *parts, add, gain],
        [full, (x.shape, BF)] + [((8, width), F32)] * 3,
        name="norm_back",
    )


def unpack_kernel(n_i, main, sum_parts, *refs):
    size = step_of(main)
    if sum_parts:
        mid_ref, a_ref, b_ref, c_ref, bias_ref, out_ref = refs
    else:
        mid_ref, out_ref = refs

    def value(at):
        x = mid_ref[at, :]
        if sum_parts:
            moved = a_ref[at, :].astype(F32) + b_ref[at, :].astype(F32) + c_ref[at, :].astype(F32)
            x = (x.astype(F32) + moved + bias_ref[...]).astype(BF)
        return x

    for i in range(n_i):

        def step(r, carry, i=i):
            at = pl.multiple_of(i * main + r * size, size)
            out_ref[i, pl.ds(pl.multiple_of(r * size, size), size), :] = value(pl.ds(at, size))
            return carry

        lax.fori_loop(0, main // size, step, 0)
    tails = value(pl.ds(n_i * main, PAD)).astype(F32)
    for i in range(n_i):
        out_ref[i, main : main + 1, :] = tails[i : i + 1].astype(BF)


def unpack(n_i, seq, first, parts=(), bias=None):
    width = first.shape[1]
    ins = [first, *parts] + ([bias] if parts else [])
    return call(
        functools.partial(unpack_kernel, n_i, seq - 1, bool(parts)),
        ins,
        [((n_i, seq, width), BF)],
        name="unpack",
    )[0]


def mlp_kernel(n_add, n0, n1, c0, c1, up_ref, upb_ref, down_ref, *refs):
    act_ref, gh_ref, g0, g1, gub_ref, acc = refs[2 * n_add :]
    j, last = pl.program_id(0), pl.num_programs(0) - 1
    size = n0.shape[0]
    for i, (n_ref, c_ref) in enumerate(((n0, c0), (n1, c1))):
        rows = slice(i * size, (i + 1) * size)
        h = dot(n_ref[...], up_ref[...], 1, 0) + upb_ref[...]
        da = dot(c_ref[...], down_ref[...], 1, 1)
        cdf = 0.5 * (1.0 + lax.erf(h * inv_root_two))
        act_ref[rows, :] = (h * cdf).astype(BF)
        gh = (da * (cdf + h * (jnp.exp(-0.5 * h * h) * inv_root_tau))).astype(BF)
        gh_ref[rows, :] = gh
        total = jnp.sum(gh.astype(F32), axis=0, keepdims=True)
        gub_ref[...] = total if i == 0 else gub_ref[...] + total
        part = dot(gh, up_ref[...], 1, 1)

        @pl.when(j == 0)
        def _():
            acc[rows, :] = part

        @pl.when(j > 0)
        def _():
            acc[rows, :] += part

    @pl.when(j == last)
    def _():
        for i, out in enumerate((g0, g1)):
            total = acc[i * size : (i + 1) * size, :]
            if n_add:
                total = total + refs[i][...].astype(F32)
            out[...] = total.astype(BF)


def mlp(k, n_hi, n, c, up, upb, down, before):
    rows, width = n[0].shape
    units = up.shape[1]
    tile = min(512, units)
    steps = units // tile
    here = whole_spec((rows, width))
    held = [] if before is None else [before[2], before[3], before[0], before[1]]
    wide = pl.BlockSpec((2 * rows, tile), lambda j: (0, k * steps + j))
    return call(
        functools.partial(mlp_kernel, len(held) // 2),
        [*n, *c, up, upb, down, *held],
        [((2 * rows, n_hi * units), BF)] * 2 + [((rows, width), BF)] * 2 + [((1, units), F32)],
        scratch=[pltpu.VMEM((2 * rows, width), F32)],
        flops=12 * rows * width * units,
        in_specs=[here] * 4
        + [
            pl.BlockSpec((width, tile), lambda j: (0, j)),
            pl.BlockSpec((1, tile), lambda j: (0, j)),
            pl.BlockSpec((tile, width), lambda j: (j, 0)),
        ]
        + ([here] * 2 + [pl.BlockSpec(memory_space=pl.ANY)] * 2 if held else []),
        out_specs=[wide] * 2 + [here] * 2 + [pl.BlockSpec((1, tile), lambda j: (0, j))],
        grid=(steps,),
        input_output_aliases={9: 0, 10: 1} if held else {},
        name="mlp",
    )


def row_product_kernel(n_parts, act_ref, *refs):
    parts, outs = refs[:n_parts], refs[n_parts:]
    size, units = outs[0].shape[0], parts[0].shape[0]
    for i, out in enumerate(outs):
        rows = slice(i * size, (i + 1) * size)
        total = None
        for k, ref in enumerate(parts):
            part = dot(act_ref[rows, k * units : (k + 1) * units], ref[...], 1, 0)
            total = part if total is None else total + part
        out[...] = total.astype(BF)


def row_product(act, parts):
    rows, width = act.shape[0] // 2, parts[0].shape[1]
    return call(
        functools.partial(row_product_kernel, len(parts)),
        [act, *parts],
        [((rows, width), BF)] * 2,
        flops=4 * rows * width * act.shape[1],
        name="row_product",
    )


def wgrad_kernel(n_left, n_right, index_ref, *refs):
    left, right = refs[:n_left], refs[n_left : n_left + n_right]
    out_ref, held, sems = refs[n_left + n_right :]
    size = right[0].shape[0]
    copies = [
        pltpu.make_async_copy(r, held.at[pl.ds(i * size, size)], sems.at[i])
        for i, r in enumerate(right)
    ]

    first = pl.program_id(0) == 0

    @pl.when(first)
    def _():
        for copy in copies:
            copy.start()

    @pl.when(first)
    def _():
        for copy in copies:
            copy.wait()

    rows = jnp.concatenate([ref[...] for ref in left], 0)
    out_ref[...] = dot(rows, held[...], 0, 0).astype(BF)


def wgrad(left, right, index, tile):
    width = right[0].shape[1]
    total = sum(r.shape[0] for r in right)
    blocks = index.shape[0]
    in_specs = [pl.BlockSpec((x.shape[0], tile), lambda j, at: (0, at[j])) for x in left]
    in_specs += [pl.BlockSpec(memory_space=pl.ANY)] * len(right)
    moved = 2 * (total * (width + blocks * tile) + blocks * tile * width)
    return pl.pallas_call(
        functools.partial(wgrad_kernel, len(left), len(right)),
        grid_spec=pltpu.PrefetchScalarGridSpec(
            num_scalar_prefetch=1,
            grid=(blocks,),
            in_specs=in_specs,
            out_specs=pl.BlockSpec((tile, width), lambda j, at: (j, 0)),
            scratch_shapes=[
                pltpu.VMEM((total, width), BF),
                pltpu.SemaphoreType.DMA((len(right),)),
            ],
        ),
        out_shape=jax.ShapeDtypeStruct((blocks * tile, width), BF),
        compiler_params=pltpu.CompilerParams(vmem_limit_bytes=60 * 2**20),
        cost_estimate=pl.CostEstimate(
            flops=2 * total * blocks * tile * width * HINT,
            bytes_accessed=moved * HINT,
            transcendentals=0,
        ),
        name="wgrad",
    )(index, *left, *right)


def place_kernel(count, transposed, at_ref, *refs):
    pieces, out_ref = refs[:count], refs[count]
    total = sum(ref.shape[0] for ref in pieces)
    size = total // at_ref.shape[0]
    target = refs[count + 1] if transposed else out_ref
    i = 0
    for ref in pieces:
        for start in range(0, ref.shape[0], size):
            rows = pl.ds(pl.multiple_of(at_ref[i] * size, size), size)
            target[rows, :] = ref[start : start + size, :].astype(target.dtype)
            i += 1
    if transposed:
        for at in range(0, total, 256):
            out_ref[:, at : at + 256] = target[at : at + 256, :].astype(F32).T


def place(pieces, at, transposed):
    width = pieces[0].shape[1]
    rows = sum(x.shape[0] for x in pieces)
    shape = (width, rows) if transposed else (rows, width)
    vmem = pl.BlockSpec(memory_space=pltpu.VMEM)
    return call(
        functools.partial(place_kernel, len(pieces), transposed),
        [at, *pieces],
        [(shape, F32)],
        scratch=[pltpu.VMEM((rows, width), BF)] if transposed else [],
        in_specs=[pl.BlockSpec(memory_space=pltpu.SMEM)] + [vmem] * len(pieces),
        name="place",
    )[0]


def attend_wgrad_kernel(n, rows_of, *refs):
    d, heads, first, branch = [refs[i * n : (i + 1) * n] for i in range(4)]
    out_ref, held, sems = refs[4 * n :]
    size, hc = d[0].shape[0], heads[0].shape[1]
    sources = list(first) + list(branch)
    copies = [
        pltpu.make_async_copy(r, held.at[pl.ds(i * size, size)], sems.at[i])
        for i, r in enumerate(sources)
    ]
    for copy in copies:
        copy.start()
    for at, left in ((0, d), (n, heads)):
        total = None
        for i, ref in enumerate(left):
            copies[at + i].wait()
            part = dot(ref[...], held[(at + i) * size : (at + i + 1) * size, :], 0, 0)
            total = part if total is None else total + part
        low = total.astype(BF)
        for i in range(low.shape[0] // hc):
            to = rows_of[i if at == 0 else 3] * hc
            out_ref[to : to + hc, :] = low[i * hc : (i + 1) * hc]


def attend_wgrad(d, heads, first, branch, rows_of):
    size, width = first[0].shape
    hc = heads[0].shape[1]
    vmem = pl.BlockSpec(memory_space=pltpu.VMEM)
    n = len(d)
    return call(
        functools.partial(attend_wgrad_kernel, n, tuple(rows_of)),
        [*d, *heads, *first, *branch],
        [((4 * hc, width), BF)],
        scratch=[pltpu.VMEM((2 * n * size, width), BF), pltpu.SemaphoreType.DMA((2 * n,))],
        flops=8 * n * size * hc * width,
        in_specs=[vmem] * (2 * n) + [pl.BlockSpec(memory_space=pl.ANY)] * (2 * n),
        name="attend_wgrad",
    )[0]


def place_heads_kernel(count, at_ref, *refs):
    pieces, qkv_ref, out_ref, buf = refs[:count], *refs[count:]
    hc = out_ref.shape[0] // 2
    size = buf.shape[0] // at_ref.shape[0]
    i = 0
    for ref in pieces:
        for start in range(0, ref.shape[0], size):
            rows = pl.ds(pl.multiple_of(at_ref[i] * size, size), size)
            buf[rows, :] = ref[start : start + size, :]
            i += 1
    for core in (0, 1):
        for mat in range(4):
            x = buf[(core * 4 + mat) * hc : (core * 4 + mat + 1) * hc, :].astype(F32)
            if mat == 3:
                out_ref[core * hc : (core + 1) * hc, :] = x
            else:
                qkv_ref[mat, core * hc : (core + 1) * hc, :] = x


def place_heads(pieces, at):
    rows, width = sum(x.shape[0] for x in pieces), pieces[0].shape[1]
    hc = rows // 8
    size = rows // at.shape[0]
    if size % 16:
        buf, i = jnp.zeros((rows, width), BF), 0
        for x in pieces:
            for start in range(0, x.shape[0], size):
                buf = lax.dynamic_update_slice_in_dim(buf, x[start : start + size], at[i] * size, 0)
                i += 1
        buf = buf.reshape(2, 4, hc, width).astype(F32)
        mats = [buf[:, i].reshape(2 * hc, width) for i in range(4)]
        return jnp.stack(mats[:3]), mats[3]
    vmem = pl.BlockSpec(memory_space=pltpu.VMEM)
    return call(
        functools.partial(place_heads_kernel, len(pieces)),
        [at, *pieces],
        [((3, 2 * hc, width), F32), ((2 * hc, width), F32)],
        scratch=[pltpu.VMEM((rows, width), BF)],
        in_specs=[pl.BlockSpec(memory_space=pltpu.SMEM)] + [vmem] * len(pieces),
        name="place_heads",
    )


class Order:
    def __init__(self):
        self.last, self.also = None, ()

    def gate(self, x):
        if self.last is None:
            return x
        return lax.optimization_barrier((x, self.last, *self.also))[0]

    def __call__(self, kernel, x, *rest):
        out = kernel(self.gate(x), *rest)
        self.last, self.also = jax.tree.leaves(out)[-1], ()
        return out

    def meet(self, *arrays):
        self.also += arrays


class Layout:
    def __init__(self, dp, tensor):
        self.dp, self.tensor = dp, tensor
        self.n_p, self.n_hi = dp // 2, tensor // 2
        self.bits = [1 << b for b in range(self.n_p.bit_length() - 1)]

    def move(self, x, p=0, c=0, hi=0, lo=0):
        dp_mask, tensor_mask = 2 * p + c, 2 * hi + lo
        pairs = [
            (d * self.tensor + t, (d ^ dp_mask) * self.tensor + (t ^ tensor_mask))
            for d in range(self.dp)
            for t in range(self.tensor)
        ]
        return lax.ppermute(x, ("dp", "tensor"), pairs)

    def place_of(self, p, order):
        n = len(order)
        place = 0
        for i, bit in enumerate(order):
            place = place + (p // bit) % 2 * (1 << (n - 1 - i))
        return place

    def spread_masks(self, order):
        masks = [0]
        for bit in order:
            masks += [m ^ bit for m in masks]
        return masks

    def spread_direct(self, block):
        return {m: self.move(block, p=m) if m else block for m in range(self.n_p)}


def on_device(
    lay,
    images,
    first_gain,
    first_shift,
    qkv_weight,
    qv_bias,
    out_weight,
    out_bias,
    second_gain,
    second_shift,
    up_weight,
    up_bias,
    down_weight,
    down_bias,
    cotangent,
):
    n_p, n_hi = lay.n_p, lay.n_hi
    n_i, seq, width = images.shape
    columns = qkv_weight.shape[2]
    units = up_weight.shape[1]
    hc, hu = columns // 2, units // 2
    dp = lax.axis_index("dp")
    p, c = dp // 2, dp % 2
    up_order, down_order = lay.bits, lay.bits[::-1]
    order = Order()
    first_gain, first_shift, out_bias, second_gain, second_shift, down_bias = [
        v.reshape(1, width)
        for v in (first_gain, first_shift, out_bias, second_gain, second_shift, down_bias)
    ]

    def half(x, axis):
        n = x.shape[axis] // 2
        return lax.dynamic_slice_in_dim(x, c * n, n, axis)

    def block(x, axis, at):
        n = x.shape[axis] // n_p
        return lax.dynamic_slice_in_dim(x, at * n, n, axis)

    def put(buf, x, axis, at):
        return lax.dynamic_update_slice_in_dim(buf, x, at, axis)

    x_unit, first_own = order(pack, images, first_gain, first_shift, True)
    first_c, first_z = lay.move(first_own, c=1), lay.move(first_own, lo=1)
    head_rows = jnp.swapaxes(qkv_weight, 1, 2)

    def weights_here(x):
        return jnp.concatenate([half(x[i], 0) for i in range(3)] + [half(out_weight, 0)])

    if n_p == 4:

        def cut_of(x):
            mat = lax.dynamic_index_in_dim(x, jnp.minimum(p, 2), 0, keepdims=False)
            return jnp.where(p == 3, half(out_weight, 0), half(mat, 0))

        work_cut = order(cut_of, head_rows)
    else:
        work_cut = block(weights_here(head_rows), 0, p)
    work_hi = [lay.move(work_cut, hi=k) for k in range(1, n_hi)]
    qv_half, upb_half = half(qv_bias, 1), half(up_bias, 0)
    bias_all = [jnp.concatenate([qv_half.reshape(-1), upb_half])]
    work_mine = order(weights_here, head_rows)
    work = [work_mine]
    forward = [[None] * 4 for _ in range(n_hi)]

    def qkv_bias_of(b):
        return jnp.concatenate([b[:hc], jnp.zeros((hc,), F32), b[hc : 2 * hc]]).reshape(1, -1)

    qkv_bias = [qkv_bias_of(bias_all[0])]

    def attention(k, u, n, adds=()):
        adds = list(adds) + ([forward[k - 1][u][4]] if k else [])
        forward[k][u] = order(lambda x: attend_fwd(n_i, x, work[k], qkv_bias[k], adds), n)
        return forward[k][u][4]

    def stage(held, axis, bit):
        return jnp.concatenate([held, lay.move(held, p=bit)], axis)

    attention(0, 0, first_own)
    bias_hi = [lay.move(order.gate(bias_all[0]), hi=k) for k in range(1, n_hi)]
    attention(0, 1, first_c)
    seed_unit, grad_down_bias = order(pack, cotangent, first_gain, first_shift, False)
    seed_c = lay.move(seed_unit, c=1)
    order.meet(*work_hi)
    work_got = [lay.spread_direct(order.gate(x)) for x in work_hi]
    first_zc = lay.move(order.gate(first_z), c=1)
    attention(0, 2, first_z)
    seed_z = lay.move(seed_unit, lo=1)
    attention(0, 3, first_zc)
    up_cut = order(lambda x: block(half(x, 1), 1, p), up_weight)
    up_hi = [lay.move(up_cut, hi=k) for k in range(1, n_hi)]
    down_cut = order(lambda x: block(half(x, 0), 0, p), down_weight)
    down_hi = [lay.move(down_cut, hi=k) for k in range(1, n_hi)]

    def assemble(got):
        masks = sorted(got)

        def run(x):
            full = jnp.zeros_like(work_mine)
            for mask in masks:
                x = x if mask == 0 else got[mask]
                full = put(full, x, 0, (p ^ mask) * x.shape[0])
            return full

        return order(run, got[0])

    work += [assemble(got) for got in work_got]
    bias_all += [order.gate(x) for x in bias_hi]
    qkv_bias += [qkv_bias_of(b) for b in bias_all[1:]]
    normed = (first_own, first_c, first_z, first_zc)
    for k in range(1, n_hi - 1):
        for u in range(4):
            attention(k, u, normed[u])
    k = n_hi - 1

    def widen(pairs, axis):
        return [order(lambda x, y=y: jnp.concatenate([x, y], axis), x) for x, y in pairs]

    moved_3 = lay.move(attention(k, 3, first_zc), c=1)
    order.meet(seed_c)
    moved_1 = lay.move(attention(k, 1, first_c), c=1)
    moved_2 = lay.move(attention(k, 2, first_z, [moved_3]), lo=1)
    order.meet(moved_1, seed_z, *up_hi)
    seed_zc = lay.move(order.gate(seed_z), c=1)
    up_got = [order.gate(x) for x in up_hi]
    up_got = [(x, lay.move(x, p=up_order[0])) for x in up_got]
    down_got = [order.gate(x) for x in down_hi]
    down_got = [(x, lay.move(x, p=down_order[0])) for x in down_got]
    attention_parts = (attention(k, 0, first_own), moved_1, moved_2)
    normed_first = list(normed)
    up_work = [order(lambda x: half(x, 1), up_weight)]
    down_work = [order(lambda x: half(x, 0), down_weight)]
    for i in range(1, len(lay.bits)):
        up_got = [(x, lay.move(x, p=up_order[i])) for x in widen(up_got, 1)]
        down_got = [(x, lay.move(x, p=down_order[i])) for x in widen(down_got, 0)]
    order.meet(seed_zc)
    seed = [seed_unit, seed_c, seed_z, seed_zc]

    middle, second_own = order(
        lambda x: norm_second(x, attention_parts, out_bias, second_gain, second_shift), x_unit
    )
    second_c, second_z = lay.move(second_own, c=1), lay.move(second_own, lo=1)

    def fill(parts, axis, order_of):
        size = parts[0].shape[axis] * 2 // n_p
        shape = [width, width]
        shape[axis] = hu
        masks = lay.spread_masks(order_of)

        def run(x):
            full, at = jnp.zeros(shape, BF), 0
            for part in (x, *parts[1:]):
                for i in range(part.shape[axis] // size):
                    piece = lax.slice_in_dim(part, i * size, (i + 1) * size, axis=axis)
                    full = put(full, piece, axis, (p ^ masks[at]) * size)
                    at += 1
            return full

        return order(run, parts[0])

    up_half = [upb_half.reshape(1, -1)] + [b[2 * hc :].reshape(1, -1) for b in bias_all[1:]]

    def mlp_half(k, first, second, seeds, before):
        return order(
            lambda x: mlp(k, n_hi, [x, second], seeds, up_work[k], up_half[k], down_work[k], before),
            first,
        )

    near = mlp_half(0, second_own, second_c, seed[:2], None)
    up_work += [fill(parts, 1, up_order) for parts in up_got]
    down_work += [fill(parts, 0, down_order) for parts in down_got]
    near_bias, far_bias = [near[4]], []
    for k in range(1, n_hi):
        near = mlp_half(k, second_own, second_c, seed[:2], near)
        near_bias.append(near[4])
    second_zc = lay.move(order.gate(second_z), c=1)
    other_c = lay.move(near[3], c=1)
    low_near = order(lambda x: row_product(x, down_work), near[0])
    low_near_c = lay.move(low_near[1], c=1)
    far = None
    for k in range(n_hi):
        if k == n_hi - 1:
            order.meet(other_c, low_near_c)
        far = mlp_half(k, second_z, second_zc, seed[2:], far)
        far_bias.append(far[4])
    normed_second = [second_own, second_c, second_z, second_zc]

    def index(order_of, other):
        top = lay.place_of(p, order_of) // (n_p // 2)
        return jnp.stack([2 * k + (top ^ other) for k in range(n_hi)]).astype(jnp.int32)

    def mlp_grad(which, right, order_of, other):
        return order(
            lambda x: wgrad([x, far[which]], right, index(order_of, other), hu // 2), near[which]
        )

    far_c = lay.move(far[3], c=1)
    down_send = mlp_grad(0, seed, down_order, 1)
    down_recv = lay.move(down_send, p=down_order[0])

    def join(*parts):
        total = parts[0].astype(F32)
        for x in parts[1:]:
            total = total + x.astype(F32)
        return total.astype(BF)

    far_sum = order(lambda x: join(x, far_c), far[2])
    grad_second = (near[2], other_c, lay.move(far_sum, lo=1))
    up_send = mlp_grad(1, normed_second, up_order, 1)
    up_recv = lay.move(up_send, p=up_order[0])
    down_keep = mlp_grad(0, seed, down_order, 0)
    grad_middle, grad_branch, grad_second_gain, grad_second_shift, grad_out_bias = order(
        lambda x: norm_back(x, grad_second, seed_unit, second_gain, True), middle
    )
    branch_c, branch_z = lay.move(grad_branch, c=1), lay.move(grad_branch, lo=1)
    low_far = order(lambda x: row_product(x, down_work), far[0])
    low_far_c = lay.move(low_far[1], c=1)
    up_keep = mlp_grad(1, normed_second, up_order, 0)

    def halve(keep, recv, order_of, stage, parts):
        bit = order_of[stage]
        side = (p // bit) % 2
        shape = (parts, 2, keep.shape[0] // (2 * parts), width)

        def pick(x, s):
            x = lax.dynamic_index_in_dim(x.reshape(shape), s, 1, keepdims=False)
            return x.reshape(-1, width)

        send = order(lambda x: join(pick(x, 1 - side), pick(recv, 1 - side)), keep)
        keep = join(pick(keep, side), pick(recv, side))
        return keep, lay.move(send, p=bit)

    def settle_hi(keep, recv):
        size = keep.shape[0] // n_hi
        total = order(lambda x: join(x, recv), keep)
        got = [lay.move(total[k * size : (k + 1) * size], hi=k) for k in range(1, n_hi)]
        return total[:size], got

    class Spread:
        def __init__(self, mine, order_of):
            self.pieces, self.order_of, self.bits = [mine], order_of, order_of[::-1]
            self.got, self.at = lay.move(mine, p=self.bits[0]), 1

        def step(self):
            self.pieces.append(self.got)
            held = order(lambda x: jnp.concatenate([x] + self.pieces[1:]), self.pieces[0])
            if self.at < len(self.bits):
                self.got = lay.move(held, p=self.bits[self.at])
            else:
                self.pieces = [held, lay.move(held, c=1)]
            self.at += 1

        def finish(self):
            while self.at <= len(self.bits):
                self.step()
            masks = lay.spread_masks(self.bits)
            places = [lay.place_of(p ^ mask, self.order_of) for mask in masks]
            at = [c * n_p + x for x in places] + [(1 - c) * n_p + x for x in places]
            return self.pieces, jnp.stack(at).astype(jnp.int32)

    backward = [[None] * 4 for _ in range(n_hi)]
    branch = [grad_branch, branch_c, branch_z, None]

    def attention_back(k, u, adds=()):
        adds = list(adds) + ([backward[k + 1][u][2]] if k < n_hi - 1 else [])
        f = forward[k][u]
        backward[k][u] = order(
            lambda g: attend_bwd(n_i, g, (f[0], f[2], f[3], work[k]), adds),
            branch[u],
        )
        return backward[k][u][2]

    def attention_send(k, order_of):
        owner = [0] * n_p
        for q in range(n_p):
            owner[lay.place_of(q, order_of)] = lay.place_of(q, orders[0])
        grad = order(
            lambda x: attend_wgrad(
                [x] + [b[0] for b in backward[k][1:]],
                [f[1] for f in forward[k]],
                normed_first,
                branch,
                owner if n_p == 4 else range(4),
            ),
            backward[k][0][0],
        )
        if n_p != 4:
            blocks = jnp.split(grad, n_p)
            grad = jnp.concatenate([blocks[i] for i in owner])
        top = lay.place_of(p, order_of) // (n_p // 2)
        size = grad.shape[0] // 2
        send = order(lambda x: lax.dynamic_slice_in_dim(x, (1 - top) * size, size, 0), grad)
        keep = lax.dynamic_slice_in_dim(grad, top * size, size, 0)
        return keep, lay.move(send, p=order_of[0])

    down_pair, up_pair = (down_keep, down_recv), (up_keep, up_recv)
    attn_pairs = [None] * n_hi
    orders = [up_order] + [down_order] * (n_hi - 1)
    n_stage = len(lay.bits)
    k = n_hi - 1
    down_pair = halve(*down_pair, down_order, 1, n_hi)
    attention_back(k, 0)
    branch[3] = lay.move(order.gate(branch_z), c=1)
    attention_back(k, 1)
    up_pair = halve(*up_pair, up_order, 1, n_hi)
    low_far_sum = order(lambda x: join(x, low_far_c), low_far[0])
    low_far_z = lay.move(low_far_sum, lo=1)
    attention_back(k, 2)
    for step in range(2, n_stage):
        down_pair = halve(*down_pair, down_order, step, n_hi)
        up_pair = halve(*up_pair, up_order, step, n_hi)
    down_mine, down_hi_got = settle_hi(*down_pair)
    attention_back(k, 3)
    attn_pairs[k] = attention_send(k, orders[k])
    up_mine, up_hi_got = settle_hi(*up_pair)
    result_parts = (low_near[0], low_near_c, low_far_z)
    result = order(lambda x: unpack(n_i, seq, x, result_parts, down_bias), middle)
    for k in range(n_hi - 2, 0, -1):
        for u in range(4):
            attention_back(k, u)
        attn_pairs[k] = attention_send(k, orders[k])
    moved_3 = lay.move(attention_back(0, 3), c=1)
    down_mine = order(lambda x: join(x, *down_hi_got), down_mine)
    down_all = Spread(down_mine, down_order)
    moved_1 = lay.move(attention_back(0, 1), c=1)
    down_all.step()
    moved_2 = lay.move(attention_back(0, 2, [moved_3]), lo=1)
    for k in range(1, n_hi):
        for step in range(1, n_stage):
            attn_pairs[k] = halve(*attn_pairs[k], orders[k], step, 1)
    order.meet(moved_1)
    grad_first = (attention_back(0, 0), moved_1, moved_2)
    up_mine = order(lambda x: join(x, *up_hi_got), up_mine)
    up_all = Spread(up_mine, up_order)
    attn_hi = []
    for k in range(1, n_hi):
        total = order(lambda x, k=k: join(x, attn_pairs[k][1]), attn_pairs[k][0])
        attn_hi.append(lay.move(total, hi=k))
    down_all = down_all.finish()
    grad = order(
        lambda x: attend_wgrad(
            [x] + [b[0] for b in backward[0][1:]],
            [f[1] for f in forward[0]],
            normed_first,
            branch,
            range(4),
        ),
        backward[0][0][0],
    )
    places = [lay.place_of(p ^ mask, orders[0]) for mask in range(n_p)]
    attn_own = block(grad, 0, places[0])
    attn_got = []
    for mask in range(1, n_p):
        out = order(lambda x, mask=mask: block(x, 0, places[mask]), grad)
        attn_got.append(lay.move(out, p=mask))
    up_all.step()

    def place_all(blocks, at, transposed):
        return order(lambda x: place([x] + blocks[1:], at, transposed), blocks[0])

    grad_down_weight = place_all(*down_all, False)
    _, grad_images, grad_first_gain, grad_first_shift, _ = order(
        lambda x: norm_back(x, grad_first, grad_middle, first_gain, False), x_unit
    )
    attn_mine = order(lambda x: join(x, *attn_got, *attn_hi), attn_own)
    attn_all = lay.spread_direct(attn_mine)

    tensor_at = lax.axis_index("tensor")
    all_units, all_columns = units * lay.tensor, columns * lay.tensor
    grad_up_bias = jnp.concatenate([(a + b)[0] for a, b in zip(near_bias, far_bias)])
    wide_up = jnp.zeros((all_units,), F32)
    wide_qv = jnp.zeros((2, all_columns), F32)
    for k in range(n_hi):
        shard = tensor_at ^ (2 * k)
        wide_up = put(wide_up, grad_up_bias[k * hu : (k + 1) * hu], 0, shard * units + c * hu)
        bias = sum(b[1] for b in backward[k])[0]
        bias = jnp.stack([bias[:hc], bias[2 * hc :]])
        wide_qv = put(wide_qv, bias, 1, shard * columns + c * hc)
    sums = (
        grad_first_gain,
        grad_first_shift,
        grad_out_bias,
        grad_second_gain,
        grad_second_shift,
        grad_down_bias,
    )
    vector = jnp.concatenate(
        [jnp.sum(x, axis=0) for x in sums] + [wide_up, wide_qv.reshape(-1)]
    )
    hops = [dict(c=1)] + [
        dict(lo=(1 << b) & 1, hi=(1 << b) >> 1) for b in range(lay.tensor.bit_length() - 1)
    ]
    hops += [dict(p=bit) for bit in lay.bits]

    def hop(vector):
        got = lay.move(vector, **hops.pop(0))
        return vector, got

    def add(pair):
        return order(lambda x: x + pair[1], pair[0])

    pair = hop(vector)
    grad_images = order(lambda x: unpack(n_i, seq, x), grad_images)
    pair = hop(add(pair))
    for _ in range(lay.tensor.bit_length() - 2):
        pair = hop(add(pair))
    up_all = up_all.finish()
    pair = hop(add(pair))
    masks = sorted(attn_all)
    held = order(
        lambda x: jnp.concatenate([x] + [attn_all[mask] for mask in masks[1:]]), attn_all[0]
    )
    held_c = lay.move(held, c=1)
    grad_up_weight = place_all(*up_all, True)
    at = [lay.place_of(p ^ mask, orders[0]) for mask in masks]
    at = [c * n_p + x for x in at] + [(1 - c) * n_p + x for x in at]
    attn_all = ([held, held_c], jnp.stack(at).astype(jnp.int32))
    while hops:
        pair = hop(add(pair))
    vector = add(pair)
    norms = vector[: 6 * width].reshape(6, width)
    vector = vector[6 * width :]
    grad_up_bias = lax.dynamic_slice_in_dim(vector, tensor_at * units, units, 0)
    grad_qv_bias = lax.dynamic_slice_in_dim(
        vector[all_units:].reshape(2, all_columns), tensor_at * columns, columns, 1
    )

    grad_qkv_weight, grad_out_weight = place_heads(*attn_all)
    grad_qkv_weight = jnp.swapaxes(grad_qkv_weight, 1, 2)
    return (
        result,
        grad_images,
        norms[0],
        norms[1],
        grad_qkv_weight,
        grad_qv_bias,
        grad_out_weight,
        norms[2],
        norms[3],
        norms[4],
        grad_up_weight,
        grad_up_bias,
        grad_down_weight,
        norms[5],
    )


def solution(mesh):
    lay = Layout(mesh.shape["dp"], mesh.shape["tensor"])
    rows = P(("dp", "tensor"), None, None)
    qkv, qv = P(None, None, "tensor"), P(None, "tensor")
    line, up, down, rep = P("tensor"), P(None, "tensor"), P("tensor", None), P()
    return jax.shard_map(
        functools.partial(on_device, lay),
        mesh=mesh,
        in_specs=(rows, rep, rep, qkv, qv, down, rep, rep, rep, up, line, down, rep, rows),
        out_specs=(rows, rows, rep, rep, qkv, qv, down, rep, rep, rep, up, line, down, rep),
        check_vma=False,
    )
```
